32 devices in a mesh: seq: 2 (over x), fsdp: 16 (over z, y, core).
Axes of the slice: x: 2, y: 2, z: 4, core: 2. Of those that a mesh axis runs over, the one named last changes fastest.
Arguments:
- hidden_in: bfloat16 [32768, 768], P(('fsdp', 'seq')), may hold values from -6 to 6
- prev_logits: bfloat16 [12, 32768, 512], P('seq', 'fsdp'), may hold values from -5 to 5
- segment: int32 [32768], P('fsdp'), may hold values from 0 to 1, as said below
- w_query: bfloat16 [768, 768], P(('seq', 'fsdp')), may hold values from -0.21875 to 0.21875
- b_query: bfloat16 [768], P(('seq', 'fsdp')), may hold values from -3 to 3
- w_key: bfloat16 [768, 768], P(('seq', 'fsdp')), may hold values from -0.21875 to 0.21875
- w_value: bfloat16 [768, 768], P(('seq', 'fsdp')), may hold values from -0.21875 to 0.21875
- b_value: bfloat16 [768], P(('seq', 'fsdp')), may hold values from -3 to 3
- w_out: bfloat16 [768, 768], P(('seq', 'fsdp')), may hold values from -1.75 to 1.75
- b_out: bfloat16 [768], P(('seq', 'fsdp')), may hold values from -3 to 3
- gain_attn: bfloat16 [768], P(('seq', 'fsdp')), may hold values from 0.25 to 1.75
- shift_attn: bfloat16 [768], P(('seq', 'fsdp')), may hold values from -3 to 3
- w_inner: bfloat16 [768, 3072], P(('seq', 'fsdp')), may hold values from -0.21875 to 0.21875
- b_inner: bfloat16 [3072], P(('seq', 'fsdp')), may hold values from -3 to 3
- w_outer: bfloat16 [3072, 768], P(('seq', 'fsdp')), may hold values from -0.109375 to 0.109375
- b_outer: bfloat16 [768], P(('seq', 'fsdp')), may hold values from -3 to 3
- gain_ffn: bfloat16 [768], P(('seq', 'fsdp')), may hold values from 0.25 to 1.75
- shift_ffn: bfloat16 [768], P(('seq', 'fsdp')), may hold values from -3 to 3
- out_grad: bfloat16 [32768, 768], P(('fsdp', 'seq')), may hold values from -6 to 6
Outputs:
- hidden_out: bfloat16 [32768, 768], P(('fsdp', 'seq'))
- new_logits: bfloat16 [12, 32768, 512], P('seq', 'fsdp')
- input_grad: bfloat16 [32768, 768], P(('fsdp', 'seq'))
- prev_grad: bfloat16 [12, 32768, 512], P('seq', 'fsdp')
- grad_w_query: float32 [768, 768], P(('seq', 'fsdp'))
- grad_b_query: float32 [768], P(('seq', 'fsdp'))
- grad_w_key: float32 [768, 768], P(('seq', 'fsdp'))
- grad_w_value: float32 [768, 768], P(('seq', 'fsdp'))
- grad_b_value: float32 [768], P(('seq', 'fsdp'))
- grad_w_out: float32 [768, 768], P(('seq', 'fsdp'))
- grad_b_out: float32 [768], P(('seq', 'fsdp'))
- grad_gain_attn: float32 [768], P(('seq', 'fsdp'))
- grad_shift_attn: float32 [768], P(('seq', 'fsdp'))
- grad_w_inner: float32 [768, 3072], P(('seq', 'fsdp'))
- grad_b_inner: float32 [3072], P(('seq', 'fsdp'))
- grad_w_outer: float32 [3072, 768], P(('seq', 'fsdp'))
- grad_b_outer: float32 [768], P(('seq', 'fsdp'))
- grad_gain_ffn: float32 [768], P(('seq', 'fsdp'))
- grad_shift_ffn: float32 [768], P(('seq', 'fsdp'))
The draws below stay inside these ranges and needn't reach their ends.
Inputs may be any that keep to these rules, and one draw needn't show every extreme that they name: Sequences lie one after another in token order and segment alternates 0, 1, 0, ... from one sequence to the next. The first sequence has exactly 4096 tokens and every later one 1024 to 4096, except the last, which the end of the batch cuts off.
All inputs are finite; a program needn't handle non-finite values.
Results may differ from the reference program's by a relative error of at most 0.015.
Values may be sent and summed in bfloat16 or wider, within the bound.
No kernel may reach another device: no remote copies, remote signals or barrier semaphores. Data moves between devices by JAX's collectives and lax.ppermute only.
A program may use at most 256 MiB of HBM per device.

```python
import math
import jax
import jax.numpy as jnp
from jax import lax

D = 768
H = 12
HD = 64
FF = 3072
WIN = 512
LEN_MIN = 1024
LEN_MAX = 4096
TOKENS = 32768


def draw_segment(key, part):
    seq_total = TOKENS // LEN_MIN + 1
    lengths = jax.random.randint(key, (seq_total,), LEN_MIN, LEN_MAX + 1)
    lengths = lengths.at[0].set(LEN_MAX)
    seq_ends = jnp.cumsum(lengths)
    positions = jnp.arange(TOKENS, dtype=jnp.int32)
    seq_index = jnp.searchsorted(seq_ends, positions, side='right')
    return (seq_index % 2).astype(jnp.int32)


def raised(entries, rng, source, target, blocks, factor):
    def block_of(axis_at):
        return (jnp.arange(entries.shape[axis_at]) // (entries.shape[axis_at] // blocks)).reshape((-1,) + (1,) * (entries.ndim - 1 - axis_at))

    first = jax.random.permutation(rng, blocks)[block_of(target)]
    other_side = (block_of(target) + blocks // 2) % blocks
    return jnp.where((block_of(source) == first) | (block_of(source) == other_side), factor * entries, entries)


def shard_levels(rng, dims, pieces, least, top_value):
    gain = 1.0
    for position, blocks in pieces:
        draws = jax.random.uniform(jax.random.fold_in(jax.random.fold_in(rng, 6), position), (blocks,), jnp.float32, least / len(pieces), top_value / len(pieces))
        gain = gain * jnp.repeat(jnp.exp(draws), dims[position] // blocks).reshape((-1,) + (1,) * (len(dims) - 1 - position))
    return gain


def gaussian(key, shape, width, most, split=(), kind=jnp.bfloat16):
    values = jax.random.normal(key, shape, jnp.float32) * width
    if len(split) > 0:
        values = shard_levels(key, shape, split, -0.22, 0.18) * values
    return jnp.clip(values, min=-most, max=most).astype(kind)


def gaussian_with(rng, extent, scale, most, pieces, heavy, held_as=jnp.bfloat16):
    drawn = scale * jax.random.normal(rng, extent, jnp.float32)
    if pieces:
        drawn = drawn * shard_levels(rng, extent, pieces, -0.22, 0.18)
    return jnp.clip(raised(drawn, jax.random.fold_in(rng, 3), *heavy), -most, most).astype(held_as)


def setup_inputs(seed: int = 0) -> dict:
    splits = jax.random.split(jax.random.key(seed), 20)
    hidden_in = gaussian_with(splits[0], (TOKENS, D), 1.0, 6.0, ((0, 32),), (0, 1, 32, 2.75))
    prev_logits = gaussian(splits[1], (H, TOKENS, WIN), 1.0, 5.0, ((0, 2), (1, 16)))
    segment = draw_segment(jax.random.fold_in(splits[19], 71), 0)
    w_query = gaussian(splits[3], (D, D), D ** -0.5, 0.21875, ((0, 32),))
    b_query = gaussian(splits[4], (D,), 0.5, 3.0, ((0, 32),))
    w_key = gaussian(splits[5], (D, D), D ** -0.5, 0.21875, ((0, 32),))
    w_value = gaussian(splits[6], (D, D), D ** -0.5, 0.21875, ((0, 32),))
    b_value = gaussian(splits[7], (D,), 0.5, 3.0, ((0, 32),))
    w_out = gaussian(splits[8], (D, D), (max(1, 8 * D // WIN)) ** -0.5, 1.75, ((0, 32),))
    b_out = gaussian(splits[9], (D,), 0.5, 3.0, ((0, 32),))
    gain_attn = jnp.clip(1.0 + 0.15 * jax.random.normal(splits[10], (D,), jnp.float32), 0.25, 1.75).astype(jnp.bfloat16)
    shift_attn = gaussian(splits[11], (D,), 0.5, 3.0, ((0, 32),))
    w_inner = gaussian(splits[12], (D, FF), D ** -0.5, 0.21875, ((0, 32),))
    b_inner = gaussian(splits[13], (FF,), 0.5, 3.0, ((0, 32),))
    w_outer = gaussian(splits[14], (FF, D), FF ** -0.5, 0.109375, ((0, 32),))
    b_outer = gaussian(splits[15], (D,), 0.5, 3.0, ((0, 32),))
    gain_ffn = jnp.clip(1.0 + 0.15 * jax.random.normal(splits[16], (D,), jnp.float32), 0.25, 1.75).astype(jnp.bfloat16)
    shift_ffn = gaussian(splits[17], (D,), 0.5, 3.0, ((0, 32),))
    out_grad = gaussian_with(splits[18], (TOKENS, D), 1.0, 6.0, ((0, 32),), (0, 1, 32, 2.75))
    return dict(hidden_in=hidden_in, prev_logits=prev_logits, segment=segment, w_query=w_query, b_query=b_query, w_key=w_key, w_value=w_value, b_value=b_value, w_out=w_out, b_out=b_out, gain_attn=gain_attn, shift_attn=shift_attn, w_inner=w_inner, b_inner=b_inner, w_outer=w_outer, b_outer=b_outer, gain_ffn=gain_ffn, shift_ffn=shift_ffn, out_grad=out_grad)


@jax.custom_vjp
def low(v):
    return lax.optimization_barrier(v.astype(jnp.bfloat16)).astype(jnp.float32)

@jax.custom_vjp
def low_back(v):
    return v

def low_keep(v):
    return (low(v), None)

def low_pass(kept, grad):
    return (grad,)

def back_keep(v):
    return (v, None)

def back_low(kept, grad):
    return (low(grad),)
low.defvjp(low_keep, low_pass)
low_back.defvjp(back_keep, back_low)
NORM_EPSILON = 1e-06
MASK_VALUE = -1e+30

def matmul(left_op, right_op):
    return jnp.dot(left_op, right_op, precision=lax.Precision.HIGHEST)

def layer_norm(values, scales, offset):
    row_mean = lax.optimization_barrier(jnp.mean(values, axis=-1, keepdims=True))
    centred = values - row_mean
    row_var = lax.optimization_barrier(jnp.mean(centred * centred, axis=-1, keepdims=True))
    return centred * lax.rsqrt(row_var + NORM_EPSILON) * scales + offset

def gelu_exact(inputs):
    return 0.5 * inputs * (1.0 + lax.erf(inputs * 0.7071067811865476))

def attend(window_block):
    queries, key_rows, values, prior_logits, allowed = window_block
    scores = jnp.einsum('gqhd,gkhd->ghqk', queries, key_rows, precision=lax.Precision.HIGHEST) * (1.0 / math.sqrt(HD)) + prior_logits
    scores = low_back(scores)
    masked = jnp.where(allowed[:, None], scores, MASK_VALUE)
    row_top = lax.optimization_barrier(jnp.max(masked, axis=-1, keepdims=True))
    exp_terms = jnp.exp(masked - row_top)
    probs_full = exp_terms / lax.optimization_barrier(jnp.sum(exp_terms, axis=-1, keepdims=True))
    mixed_rows = jnp.einsum('ghqk,gkhd->gqhd', low(probs_full), values, precision=lax.Precision.HIGHEST)
    return (mixed_rows, scores)

def forward(tokens, prior_logits, allowed, weights):
    query_w, query_b, key_w, value_w, value_b, out_w, out_b, attn_gain, attn_shift, inner_w, inner_b, outer_w, outer_b, ffn_gain, ffn_shift = weights
    windows = tokens.shape[0] // WIN
    per_step = math.gcd(windows, 8)
    steps_count = windows // per_step

    def split_heads(array):
        return array.reshape(steps_count, per_step, WIN, H, HD)
    queries = split_heads(low_back(low(matmul(tokens, query_w) + query_b)))
    key_rows = split_heads(low_back(low(matmul(tokens, key_w))))
    values = split_heads(low_back(low(matmul(tokens, value_w) + value_b)))
    window_blocks = (queries, key_rows, values, prior_logits.reshape(steps_count, per_step, H, WIN, WIN), allowed.reshape(steps_count, per_step, WIN, WIN))
    mixed_rows, scores = lax.map(jax.checkpoint(attend), window_blocks)
    attended = low_back(low(mixed_rows.reshape(tokens.shape[0], H * HD)))
    resid_one = tokens + low_back(matmul(attended, out_w) + out_b)
    hidden = layer_norm(resid_one, attn_gain, attn_shift)
    pre_act = low_back(matmul(low(hidden), inner_w) + inner_b)
    branch = low_back(matmul(low(gelu_exact(pre_act)), outer_w) + outer_b)
    result = layer_norm(hidden + branch, ffn_gain, ffn_shift)
    return (result, scores.reshape(windows, H, WIN, WIN))

def reference(hidden_in, prev_logits, segment, w_query, b_query, w_key, w_value, b_value, w_out, b_out, gain_attn, shift_attn, w_inner, b_inner, w_outer, b_outer, gain_ffn, shift_ffn, out_grad):
    windows = TOKENS // WIN
    prior_logits = prev_logits.astype(jnp.float32).reshape(H, windows, WIN, WIN).transpose(1, 0, 2, 3)
    seg_blocks = segment.reshape(windows, WIN)
    allowed = seg_blocks[:, :, None] == seg_blocks[:, None, :]
    weights = tuple((member.astype(jnp.float32) for member in (w_query, b_query, w_key, w_value, b_value, w_out, b_out, gain_attn, shift_attn, w_inner, b_inner, w_outer, b_outer, gain_ffn, shift_ffn)))

    def layer_fn(tokens, prior_in, weight_set):
        return forward(tokens, prior_in, allowed, weight_set)
    (result, scores), pull_back = jax.vjp(layer_fn, hidden_in.astype(jnp.float32), prior_logits, weights)
    d_tokens, d_prior, d_weights = pull_back((out_grad.astype(jnp.float32), jnp.zeros_like(scores)))
    logits = scores.transpose(1, 0, 2, 3).reshape(H, TOKENS, WIN)
    prior_grad = d_prior.transpose(1, 0, 2, 3).reshape(H, TOKENS, WIN)
    return (result.astype(jnp.bfloat16), logits.astype(jnp.bfloat16), d_tokens.astype(jnp.bfloat16), prior_grad.astype(jnp.bfloat16), d_weights[0], d_weights[1], d_weights[2], d_weights[3], d_weights[4], d_weights[5], d_weights[6], d_weights[7], d_weights[8], d_weights[9], d_weights[10], d_weights[11], d_weights[12], d_weights[13], d_weights[14])
```

```python
import math

import jax
import jax.numpy as jnp
from jax import lax
from jax.experimental import pallas as pl
from jax.experimental.pallas import tpu as pltpu
from jax.sharding import PartitionSpec as P

NORM_EPSILON = 1e-06
MASK_VALUE = -1e30
INV_SQRT_TWO = 0.7071067811865476
INV_SQRT_TWO_PI = 0.3989422804014327
VMEM_LIMIT = 48 * 1024 * 1024
BF16 = jnp.bfloat16
F32 = jnp.float32


def matmul(left_op, right_op):
    return jnp.dot(left_op, right_op, preferred_element_type=F32)


def matmul_tn(left_op, right_op):
    return lax.dot_general(
        left_op, right_op, (((0,), (0,)), ((), ())), preferred_element_type=F32
    )


def matmul_nt(left_op, right_op):
    return lax.dot_general(
        left_op, right_op, (((1,), (1,)), ((), ())), preferred_element_type=F32
    )


def column_sum(values):
    return jnp.sum(values.astype(F32), axis=0)


def swap(value, hop):
    axis, mask = hop
    size = lax.axis_size(axis)
    return lax.ppermute(value, axis, [(i, i ^ mask) for i in range(size)])


def my_bit(hop):
    axis, mask = hop
    return (lax.axis_index(axis) // mask) % 2


def ordered_pair(mine, other, bit, axis):
    return jnp.where(
        bit == 0,
        jnp.concatenate([mine, other], axis=axis),
        jnp.concatenate([other, mine], axis=axis),
    )


def gather_hop(value, hop, place):
    other = swap(value, hop)
    return ordered_pair(
        jnp.expand_dims(value, place), jnp.expand_dims(other, place), my_bit(hop), place
    )


def reduce_hop(value, hop, place):
    bit = my_bit(hop)
    send = lax.dynamic_index_in_dim(value, 1 - bit, place, keepdims=False)
    keep = lax.dynamic_index_in_dim(value, bit, place, keepdims=False)
    return (keep.astype(F32) + swap(send, hop).astype(F32)).astype(BF16)


def plan_hops(count):
    bits = [("fsdp", 1 << n) for n in range(count)]
    return list(reversed(bits[2:])), bits[1], bits[0]


def gather_rows(shard, count, seq_first):
    far, near, core = plan_hops(count)
    value = shard
    for place, hop in enumerate(far):
        value = gather_hop(value, hop, place)
    done = len(far)
    if seq_first:
        value = gather_hop(value, ("seq", 1), 0)
        value = gather_hop(value, near, done + 1)
    else:
        value = gather_hop(value, near, done)
        value = gather_hop(value, ("seq", 1), 0)
    value = gather_hop(value, core, done + 2)
    return value.reshape(-1, shard.shape[-1])


def scatter_rows(grad, rows, count, seq_first):
    far, near, core = plan_hops(count)
    done = len(far)
    value = grad.reshape((2,) * (count + 1) + (rows, grad.shape[-1]))
    value = reduce_hop(value, core, done + 2)
    if seq_first:
        value = reduce_hop(value, ("seq", 1), 0)
        value = reduce_hop(value, near, done)
    else:
        value = reduce_hop(value, near, done + 1)
        value = reduce_hop(value, ("seq", 1), 0)
    for place in reversed(range(done)):
        value = reduce_hop(value, far[place], place)
    return value


def lane_halves():
    lanes = lax.broadcasted_iota(jnp.int32, (1, 128), 1)
    low = jnp.where(lanes < 64, 1.0, 0.0)
    return low.astype(BF16), (1.0 - low).astype(BF16)


def attend_body(start, q_ref, k_ref, v_ref, prior_ref, row_seg, col_seg, *rest):
    logits_ref, probs_ref, out_ref = rest[-3:]
    halves = lane_halves()
    allowed = row_seg[...] == col_seg[0]
    queries = q_ref[...]
    mixed = None
    for head, half in enumerate(halves):
        scores = matmul_nt(queries, k_ref[...] * half) + prior_ref[head].astype(F32)
        logits_ref[head] = scores.astype(BF16)
        masked = jnp.where(allowed, scores, MASK_VALUE)
        top = jnp.max(masked, axis=1, keepdims=True)
        terms = jnp.exp(masked - top)
        total = jnp.sum(terms, axis=1, keepdims=True)
        probs = (terms * (1.0 / total)).astype(BF16)
        probs_ref[head] = probs
        part = matmul(probs, v_ref[...] * half)
        mixed = part if mixed is None else mixed + part
    out_ref[...] = mixed.astype(BF16)


def attend(qkv, prior, seg_rows, seg_cols, start, first, count, earlier):
    heads, group, window = prior.shape
    pairs = heads // 2
    share = heads * 64

    def qkv_spec(part):
        return pl.BlockSpec(
            (window, 128), lambda w, p, s: (first + w, part * pairs + p)
        )

    pair_spec = pl.BlockSpec((2, window, window), lambda w, p, s: (p, s[0] + w, 0))
    in_specs = [
        qkv_spec(0),
        qkv_spec(1),
        qkv_spec(2),
        pair_spec,
        pl.BlockSpec((window, 1), lambda w, p, s: (s[0] + w, 0)),
        pl.BlockSpec((1, 1, window), lambda w, p, s: (s[0] + w, 0, 0)),
    ]
    operands = [qkv, qkv, qkv, prior, seg_rows, seg_cols]
    aliases = {}
    if earlier is not None:
        aliases = {len(operands) + 1: 0, len(operands) + 2: 1}
        operands += list(earlier)
        in_specs += [pl.BlockSpec(memory_space=pl.ANY)] * 2
    big = jax.ShapeDtypeStruct(prior.shape, BF16)
    return pl.pallas_call(
        attend_body,
        grid_spec=pltpu.PrefetchScalarGridSpec(
            num_scalar_prefetch=1,
            grid=(count, pairs),
            in_specs=in_specs,
            out_specs=[
                pair_spec,
                pair_spec,
                pl.BlockSpec((window, 128), lambda w, p, s: (w, p)),
            ],
        ),
        out_shape=[
            big,
            big,
            jax.ShapeDtypeStruct((count * window, share), BF16),
        ],
        input_output_aliases=aliases,
        compiler_params=pltpu.CompilerParams(vmem_limit_bytes=VMEM_LIMIT),
        cost_estimate=pl.CostEstimate(
            flops=count * heads * window * window * 1024,
            transcendentals=count * heads * window * window,
            bytes_accessed=count * heads * window * window * 6,
        ),
        name="attend",
    )(start, *operands)


def attend_back_body(
    start, q_ref, k_ref, v_ref, probs_ref, grad_ref, out_ref, *rest
):
    d_scores_ref, d_qkv_ref = rest[-2:]
    pair = pl.program_id(1)
    pairs = pl.num_programs(1)
    halves = lane_halves()
    grads = grad_ref[...]
    product = grads.astype(F32) * out_ref[...].astype(F32)
    d_queries = d_keys = d_values = None
    for head, half in enumerate(halves):
        probs = probs_ref[head]
        inner = jnp.sum(product * half.astype(F32), axis=1, keepdims=True)
        d_probs = matmul_nt(grads, v_ref[...] * half)
        d_scores = (probs.astype(F32) * (d_probs - inner)).astype(BF16)
        d_scores_ref[head] = d_scores
        parts = (
            matmul(d_scores, k_ref[...] * half),
            matmul_tn(d_scores, q_ref[...] * half),
            matmul_tn(probs, grads * half),
        )
        if head == 0:
            d_queries, d_keys, d_values = parts
        else:
            d_queries += parts[0]
            d_keys += parts[1]
            d_values += parts[2]
    for slot, value in enumerate((d_queries * 0.125, d_keys, d_values)):
        lanes = pl.ds(pl.multiple_of((slot * pairs + pair) * 128, 128), 128)
        d_qkv_ref[:, lanes] = value.astype(BF16)


def attend_back(qkv, probs, grads, outs, start, first, count, earlier):
    heads, group, window = probs.shape
    pairs = heads // 2
    share = heads * 64

    def qkv_spec(part):
        return pl.BlockSpec(
            (window, 128), lambda w, p, s: (first + w, part * pairs + p)
        )

    pair_spec = pl.BlockSpec((2, window, window), lambda w, p, s: (p, s[0] + w, 0))
    row_spec = pl.BlockSpec((window, 128), lambda w, p, s: (w, p))
    in_specs = [qkv_spec(0), qkv_spec(1), qkv_spec(2), pair_spec, row_spec, row_spec]
    operands = [qkv, qkv, qkv, probs, grads, outs]
    aliases = {}
    if earlier is not None:
        aliases = {len(operands) + 1: 0}
        operands.append(earlier)
        in_specs.append(pl.BlockSpec(memory_space=pl.ANY))
    return pl.pallas_call(
        attend_back_body,
        grid_spec=pltpu.PrefetchScalarGridSpec(
            num_scalar_prefetch=1,
            grid=(count, pairs),
            in_specs=in_specs,
            out_specs=[
                pair_spec,
                pl.BlockSpec((window, 3 * share), lambda w, p, s: (w, 0)),
            ],
        ),
        out_shape=[
            jax.ShapeDtypeStruct(probs.shape, BF16),
            jax.ShapeDtypeStruct((count * window, 3 * share), BF16),
        ],
        input_output_aliases=aliases,
        compiler_params=pltpu.CompilerParams(vmem_limit_bytes=VMEM_LIMIT),
        cost_estimate=pl.CostEstimate(
            flops=count * heads * window * window * 2048,
            transcendentals=0,
            bytes_accessed=count * heads * window * window * 4,
        ),
        name="attend_back",
    )(start, *operands)


def normed(values):
    centred = values - jnp.mean(values, axis=-1, keepdims=True)
    inv_dev = lax.rsqrt(
        jnp.mean(centred * centred, axis=-1, keepdims=True) + NORM_EPSILON
    )
    return centred * inv_dev, inv_dev


def normed_back(scaled, unit, inv_dev):
    return inv_dev * (
        scaled
        - jnp.mean(scaled, axis=-1, keepdims=True)
        - unit * jnp.mean(scaled * unit, axis=-1, keepdims=True)
    )


def shards(
    hidden_in,
    prev_logits,
    segment,
    w_query,
    b_query,
    w_key,
    w_value,
    b_value,
    w_out,
    b_out,
    gain_attn,
    shift_attn,
    w_inner,
    b_inner,
    w_outer,
    b_outer,
    gain_ffn,
    shift_ffn,
    out_grad,
):
    seq = lax.axis_index("seq")
    fsdp_count = lax.axis_size("fsdp")
    count = fsdp_count.bit_length() - 1
    devices = 2 * fsdp_count
    heads, group, window = prev_logits.shape
    rows, width = w_query.shape
    inner_rows = b_inner.shape[0]
    hidden_units = inner_rows * devices
    share = width // 2
    tokens = hidden_in.shape[0]
    own_windows = tokens // window
    seq_hop = ("seq", 1)
    far, near, core = plan_hops(count)

    others = [
        swap(hidden_in[w * window : (w + 1) * window], seq_hop)
        for w in range(own_windows)
    ]

    vectors = (b_query, b_value, b_out, gain_attn, shift_attn, b_outer, gain_ffn, shift_ffn)
    bias_row = jnp.concatenate(vectors + (b_inner,))
    bias_count = bias_row.shape[0]

    def columns_of(side):
        return jnp.concatenate(
            [
                lax.dynamic_slice_in_dim(w, side * share, share, axis=1)
                for w in (w_query, w_key, w_value)
            ],
            axis=1,
        )

    padded_row = jnp.pad(bias_row, (0, 3 * share - bias_count))[None]
    mine = jnp.concatenate([columns_of(seq), padded_row], axis=0)
    theirs = swap(jnp.concatenate([columns_of(1 - seq), padded_row], axis=0), seq_hop)
    unit = ordered_pair(mine[None], theirs[None], seq, 0)
    place = 1
    for hop in far + [near, core]:
        unit = gather_hop(unit, hop, place)
        place += 1
    unit = unit.reshape(2, fsdp_count, rows + 1, 3 * share)
    qkv_weight = unit[:, :, :rows].reshape(width, 3 * share)
    bias_all = unit[:, :, rows, :bias_count].astype(F32)
    small = bias_all[:, :, : 8 * rows].reshape(devices, 8, rows)
    small = small.transpose(1, 0, 2).reshape(8, width)
    inner_bias = bias_all[:, :, 8 * rows :].reshape(hidden_units)
    query_bias, value_bias, out_bias, attn_gain, attn_shift, outer_bias, ffn_gain, ffn_shift = small
    qkv_bias = jnp.concatenate(
        [
            lax.dynamic_slice_in_dim(query_bias, seq * share, share),
            jnp.zeros((share,), F32),
            lax.dynamic_slice_in_dim(value_bias, seq * share, share),
        ]
    )
    qkv_scale = jnp.concatenate([jnp.full((share,), 0.125, F32), jnp.ones((2 * share,), F32)])

    half_inner = hidden_units // 2
    first_shard = jnp.concatenate([w_inner[:, :half_inner], w_out[:, :share]], axis=1)
    second_shard = jnp.concatenate([w_inner[:, half_inner:], w_out[:, share:]], axis=1)
    first_full = gather_rows(first_shard, count, False)
    second_full = gather_rows(second_shard, count, True)
    inner_full = jnp.concatenate([first_full[:, :half_inner], second_full[:, :half_inner]], axis=1)
    out_full = jnp.concatenate([first_full[:, half_inner:], second_full[:, half_inner:]], axis=1)
    outer_full = jnp.concatenate(
        [
            gather_rows(w_outer[:, :share], count, False),
            gather_rows(w_outer[:, share:], count, True),
        ],
        axis=1,
    )

    def project(block):
        product = matmul(block, qkv_weight) + qkv_bias
        return (product.astype(BF16).astype(F32) * qkv_scale).astype(BF16)

    seg_rows = segment[:, None]
    seg_cols = segment.reshape(group // window, 1, window)
    own_start = (seq * own_windows).astype(jnp.int32).reshape(1)
    other_start = ((1 - seq) * own_windows).astype(jnp.int32).reshape(1)

    own_qkv = project(hidden_in)
    logits, probs, own_out = attend(
        own_qkv, prev_logits, seg_rows, seg_cols, own_start, 0, own_windows, None
    )
    other_qkv = []
    other_out = []
    received = []
    for w in range(own_windows):
        other_qkv.append(project(others[w]))
        logits, probs, out = attend(
            other_qkv[w], prev_logits, seg_rows, seg_cols, other_start + w, 0, 1, (logits, probs)
        )
        other_out.append(out)
        received.append(swap(out, seq_hop))
    attended = ordered_pair(own_out, jnp.concatenate(received, axis=0), seq, 1)

    resid_one = hidden_in.astype(F32) + matmul(attended, out_full) + out_bias
    unit_one, inv_one = normed(resid_one)
    hidden = unit_one * attn_gain + attn_shift
    hidden_low = hidden.astype(BF16)
    pre_act = matmul(hidden_low, inner_full) + inner_bias
    phi = 0.5 * (1.0 + lax.erf(pre_act * INV_SQRT_TWO))
    slope = phi + pre_act * (INV_SQRT_TWO_PI * jnp.exp(-0.5 * pre_act * pre_act))
    inner_low = (pre_act * phi).astype(BF16)
    resid_two = hidden + matmul(inner_low, outer_full) + outer_bias
    unit_two, inv_two = normed(resid_two)
    hidden_out = (unit_two * ffn_gain + ffn_shift).astype(BF16)
    cotangent = out_grad.astype(F32)
    g_ffn_gain = jnp.sum(cotangent * unit_two, axis=0)
    g_ffn_shift = jnp.sum(cotangent, axis=0)
    d_resid_two = normed_back(cotangent * ffn_gain, unit_two, inv_two)
    d_branch = d_resid_two.astype(BF16)
    g_outer_bias = column_sum(d_branch)
    g_outer = matmul_tn(inner_low, d_branch).astype(BF16)
    d_pre = (matmul_nt(d_branch, outer_full) * slope).astype(BF16)
    g_inner_bias = column_sum(d_pre)
    g_inner = matmul_tn(hidden_low, d_pre).astype(BF16)
    d_hidden = d_resid_two + matmul_nt(d_pre, inner_full)
    d_resid_one = normed_back(d_hidden * attn_gain, unit_one, inv_one)
    g_attn_gain = jnp.sum(d_hidden * unit_one, axis=0)
    g_attn_shift = column_sum(d_hidden)
    d_proj = d_resid_one.astype(BF16)
    g_out_bias = column_sum(d_proj)
    g_out = matmul_tn(attended, d_proj).astype(BF16)

    def d_heads_of(side):
        part = lax.dynamic_slice_in_dim(out_full, side * share, share, axis=0)
        return matmul_nt(d_proj, part).astype(BF16)

    d_theirs = d_heads_of(1 - seq)
    d_others = [
        swap(d_theirs[w * window : (w + 1) * window], seq_hop) for w in range(own_windows)
    ]
    d_own = d_heads_of(seq)

    s_outer_first = scatter_rows(g_outer[:, :share], inner_rows, count, False)
    s_outer_second = scatter_rows(g_outer[:, share:], inner_rows, count, True)
    grad_first = jnp.concatenate([g_inner[:, :half_inner], g_out[:, :share]], axis=1)
    grad_second = jnp.concatenate([g_inner[:, half_inner:], g_out[:, share:]], axis=1)
    s_first = scatter_rows(grad_first, rows, count, False)
    s_second = scatter_rows(grad_second, rows, count, True)
    s_outer = jnp.concatenate([s_outer_first, s_outer_second], axis=1)
    s_inner = jnp.concatenate([s_first[:, :half_inner], s_second[:, :half_inner]], axis=1)
    s_out = jnp.concatenate([s_first[:, half_inner:], s_second[:, half_inner:]], axis=1)

    d_scores = None
    other_d_qkv = []
    input_received = []
    for w in range(own_windows):
        d_scores, d_qkv = attend_back(
            other_qkv[w], probs, d_others[w], other_out[w], other_start + w, 0, 1, d_scores
        )
        other_d_qkv.append(d_qkv)
        input_received.append(swap(matmul_nt(d_qkv, qkv_weight).astype(BF16), seq_hop))
    d_scores, own_d_qkv = attend_back(
        own_qkv, probs, d_own, own_out, own_start, 0, own_windows, d_scores
    )
    input_grad = (
        d_resid_one
        + matmul_nt(own_d_qkv, qkv_weight)
        + jnp.concatenate(input_received, axis=0).astype(F32)
    ).astype(BF16)
    g_qkv = matmul_tn(hidden_in, own_d_qkv)
    qkv_sum = column_sum(own_d_qkv)
    for w in range(own_windows):
        g_qkv += matmul_tn(others[w], other_d_qkv[w])
        qkv_sum += column_sum(other_d_qkv[w])

    def both_sides(part):
        blank = jnp.zeros_like(part)
        return ordered_pair(part, blank, seq, 0)

    bias_grads = jnp.stack(
        [
            both_sides(qkv_sum[:share]),
            both_sides(qkv_sum[2 * share :]),
            g_out_bias,
            g_attn_gain,
            g_attn_shift,
            g_outer_bias,
            g_ffn_gain,
            g_ffn_shift,
        ]
    )
    bias_grads = bias_grads.reshape(8, devices, rows).transpose(1, 0, 2).reshape(devices, 8 * rows)
    bias_grads = jnp.concatenate([bias_grads, g_inner_bias.reshape(devices, inner_rows)], axis=1)
    bias_grads = jnp.pad(bias_grads, ((0, 0), (0, 3 * share - bias_count)))
    tail = jnp.concatenate(
        [
            g_qkv.reshape(2, fsdp_count, rows, 3 * share),
            bias_grads.reshape(2, fsdp_count, 1, 3 * share),
        ],
        axis=2,
    ).astype(BF16)
    tail = tail.reshape((2,) * (count + 1) + (rows + 1, 3 * share))
    places = list(range(1, count + 1))
    order = [core, near] + list(reversed(far))
    for hop in order:
        tail = reduce_hop(tail, hop, len(places))
        places.pop()
    other_tail = swap(lax.dynamic_index_in_dim(tail, 1 - seq, 0, keepdims=False), seq_hop)
    own_tail = lax.dynamic_index_in_dim(tail, seq, 0, keepdims=False)
    bias_sum = own_tail[rows].astype(F32) + other_tail[rows].astype(F32)
    small_grads = bias_sum[: 8 * rows].reshape(8, rows)

    def weight_part(slot):
        lanes = slice(slot * share, (slot + 1) * share)
        return ordered_pair(own_tail[:rows, lanes], other_tail[:rows, lanes], seq, 1).astype(F32)

    return (
        hidden_out,
        logits,
        input_grad,
        d_scores,
        weight_part(0),
        small_grads[0],
        weight_part(1),
        weight_part(2),
        small_grads[1],
        s_out.astype(F32),
        small_grads[2],
        small_grads[3],
        small_grads[4],
        s_inner.astype(F32),
        bias_sum[8 * rows : bias_count],
        s_outer.astype(F32),
        small_grads[5],
        small_grads[6],
        small_grads[7],
    )


def solution(mesh):
    in_specs = (
        P(("fsdp", "seq"), None),
        P("seq", "fsdp", None),
        P("fsdp"),
        P(("seq", "fsdp"), None),
        P(("seq", "fsdp")),
        P(("seq", "fsdp"), None),
        P(("seq", "fsdp"), None),
        P(("seq", "fsdp")),
        P(("seq", "fsdp"), None),
        P(("seq", "fsdp")),
        P(("seq", "fsdp")),
        P(("seq", "fsdp")),
        P(("seq", "fsdp"), None),
        P(("seq", "fsdp")),
        P(("seq", "fsdp"), None),
        P(("seq", "fsdp")),
        P(("seq", "fsdp")),
        P(("seq", "fsdp")),
        P(("fsdp", "seq"), None),
    )
    out_specs = (
        P(("fsdp", "seq"), None),
        P("seq", "fsdp", None),
        P(("fsdp", "seq"), None),
        P("seq", "fsdp", None),
        P(("seq", "fsdp"), None),
        P(("seq", "fsdp")),
        P(("seq", "fsdp"), None),
        P(("seq", "fsdp"), None),
        P(("seq", "fsdp")),
        P(("seq", "fsdp"), None),
        P(("seq", "fsdp")),
        P(("seq", "fsdp")),
        P(("seq", "fsdp")),
        P(("seq", "fsdp"), None),
        P(("seq", "fsdp")),
        P(("seq", "fsdp"), None),
        P(("seq", "fsdp")),
        P(("seq", "fsdp")),
        P(("seq", "fsdp")),
    )
    return jax.shard_map(shards, mesh=mesh, in_specs=in_specs, out_specs=out_specs, check_vma=False)
```

```python
import functools
import math

import jax
import jax.numpy as jnp
from jax import lax
from jax.experimental import pallas as pl
from jax.experimental.pallas import tpu as pltpu
from jax.sharding import PartitionSpec as P

NORM_EPSILON = 1e-06
MASK_VALUE = -1e30
INV_SQRT_TWO = 0.7071067811865476
INV_SQRT_TWO_PI = 0.3989422804014327
VMEM_LIMIT = 56 * 1024 * 1024
BF16 = jnp.bfloat16
F32 = jnp.float32
SMALL_COST = pl.CostEstimate(flops=1024, transcendentals=0, bytes_accessed=1024)


def matmul(left_op, right_op):
    return jnp.dot(left_op, right_op, preferred_element_type=F32)


def matmul_tn(left_op, right_op):
    return lax.dot_general(
        left_op, right_op, (((0,), (0,)), ((), ())), preferred_element_type=F32
    )


def matmul_nt(left_op, right_op):
    return lax.dot_general(
        left_op, right_op, (((1,), (1,)), ((), ())), preferred_element_type=F32
    )


def column_sum(values):
    return jnp.sum(values.astype(F32), axis=0)


BOTH = ("seq", "fsdp")


def trade(value, partner):
    seq_count, fsdp_count = lax.axis_size("seq"), lax.axis_size("fsdp")
    pairs = []
    for seq in range(seq_count):
        for at in range(fsdp_count):
            to_seq, to = partner(seq, at)
            pairs.append((seq * fsdp_count + at, to_seq * fsdp_count + to))
    return lax.ppermute(value, BOTH, pairs)


def across(hop):
    axis, mask = hop
    if axis == "seq":
        return lambda seq, at: (seq ^ mask, at)
    return lambda seq, at: (seq, at ^ mask)


def swap(value, hop):
    return trade(value, across(hop))


def bit_of(hop, seq, at):
    axis, mask = hop
    return (seq if axis == "seq" else at // mask) % 2


def my_bit(hop):
    at = lax.axis_index(hop[0]).astype(jnp.int32)
    return bit_of(hop, at, at)


def after(value, *others):
    return lax.optimization_barrier((value,) + others)[0]


def merge_body(where_ref, *refs, plans):
    seq, at = where_ref[0], where_ref[1]
    outs = refs[sum(len(plan) for plan in plans) :]
    for plan, out_ref in zip(plans, outs):
        for target in plan:
            source, refs = refs[0], refs[1:]
            for n in range(source.shape[0]):
                out_ref[target(n, seq, at)] = source[n]


def merge(where, *items):
    sources = [blocks for item in items for blocks, _ in item]
    plans = [[target for _, target in item] for item in items]
    outs = []
    for item in items:
        total_blocks = sum(blocks.shape[0] for blocks, _ in item)
        outs.append(jax.ShapeDtypeStruct((total_blocks,) + item[0][0].shape[1:], BF16))
    return pl.pallas_call(
        functools.partial(merge_body, plans=plans),
        in_specs=[pl.BlockSpec(memory_space=pltpu.SMEM)]
        + [pl.BlockSpec(memory_space=pltpu.VMEM)] * len(sources),
        out_specs=[pl.BlockSpec(memory_space=pltpu.VMEM)] * len(outs),
        out_shape=outs,
        compiler_params=pltpu.CompilerParams(vmem_limit_bytes=VMEM_LIMIT),
        cost_estimate=SMALL_COST,
        name="merge",
    )(where, *sources)


def spread(hop, inner):
    def target(flip):
        def place(n, seq, at):
            bit = bit_of(hop, seq, at)
            bit = 1 - bit if flip else bit
            return (n // inner) * 2 * inner + n % inner + bit * inner

        return place

    return target(False), target(True)


def joined(mine, other, hop, inner):
    own_place, other_place = spread(hop, inner)
    return [(mine, own_place), (other, other_place)]


def by_core(core, zero, one):
    def place(n, seq, at):
        bit = bit_of(core, seq, at)
        return (1 - bit) * zero(n, seq, at) + bit * one(n, seq, at)

    return place


def joined_by_core(mine, other, core, zero, one):
    zero_places, one_places = spread(*zero), spread(*one)
    return [
        (mine, by_core(core, zero_places[0], one_places[0])),
        (other, by_core(core, zero_places[1], one_places[1])),
    ]


def split(value, hop, place):
    bit = my_bit(hop)
    return (
        lax.dynamic_index_in_dim(value, 1 - bit, place, keepdims=False),
        lax.dynamic_index_in_dim(value, bit, place, keepdims=False),
    )


def total(one, two):
    return (one.astype(F32) + two.astype(F32)).astype(BF16)


def plan_hops(count):
    bits = [("fsdp", 1 << n) for n in range(count)]
    return list(reversed(bits[2:])), bits[1], bits[0]


def place_of(rows, inner_rows):
    count = 8 * rows + inner_rows
    per_row = inner_rows // rows
    entry = lax.broadcasted_iota(jnp.int32, (1, count), 1)
    row, lane = entry * 0, entry * 0
    for slot in range(8):
        inside = (entry >= slot * rows) & (entry < (slot + 1) * rows)
        row = jnp.where(inside, entry - slot * rows, row)
        lane = jnp.where(inside, slot, lane)
    for unit in range(rows):
        low = 8 * rows + unit * per_row
        inside = (entry >= low) & (entry < low + per_row)
        row = jnp.where(inside, unit, row)
        lane = jnp.where(inside, 8 + entry - low, lane)
    return row, lane


def pack_body(where_ref, q_ref, k_ref, v_ref, inner_ref, out_ref, *rest):
    small_refs = rest[:9]
    quarter_refs = (rest[9:11], rest[11:13])
    wide_refs = rest[13:15]
    line_ref, whole_ref = rest[15:]
    rows, width = q_ref.shape
    share = width // 2
    half = inner_ref.shape[1] // 2
    lanes = quarter_refs[0][0].shape[1]
    inner_rows = small_refs[8].shape[1]
    side, core = where_ref[0], where_ref[1] % 2
    for slot, ref in enumerate(small_refs):
        line_ref[0:1, slot * rows : slot * rows + ref.shape[1]] = ref[...].astype(F32)
    row, lane = place_of(rows, inner_rows)
    count = 8 * rows + inner_rows
    spread_line = jnp.where(
        lax.broadcasted_iota(jnp.int32, (rows, count), 0) == row, line_ref[0:1, :count], 0.0
    )
    pick = jnp.where(lax.broadcasted_iota(jnp.int32, (128, count), 0) == lane, 1.0, 0.0)
    extra = matmul_nt(spread_line.astype(BF16), pick.astype(BF16)).astype(BF16)
    for turn in range(2):
        start = pl.multiple_of(((side + turn) % 2) * share, 128)
        for slot, ref in enumerate((q_ref, k_ref, v_ref)):
            whole_ref[:, slot * share : (slot + 1) * share] = ref[:, pl.ds(start, share)]
        whole_ref[:, 3 * share :] = extra
        for other in range(2):
            at = pl.multiple_of(((core + other) % 2) * lanes, 128)
            quarter_refs[turn][other][...] = whole_ref[:, pl.ds(at, lanes)]
    for turn, ref in enumerate(wide_refs):
        part = (core + turn) % 2
        ref[:, :half] = inner_ref[:, pl.ds(pl.multiple_of(part * half, 128), half)]
        ref[:, half:] = out_ref[:, pl.ds(pl.multiple_of(part * share, 128), share)]


def pack(where, w_query, w_key, w_value, w_inner, w_out, vectors):
    rows, width = w_query.shape
    lines = [v.reshape(1, -1) for v in vectors]
    count = sum(line.shape[1] for line in lines)
    lanes = 3 * width // 2 + 128
    quarter = jax.ShapeDtypeStruct((rows, lanes // 2), BF16)
    wide = jax.ShapeDtypeStruct((rows, (w_inner.shape[1] + width) // 2), BF16)
    return pl.pallas_call(
        pack_body,
        in_specs=[pl.BlockSpec(memory_space=pltpu.SMEM)]
        + [pl.BlockSpec(memory_space=pltpu.VMEM)] * (5 + len(lines)),
        out_specs=[pl.BlockSpec(memory_space=pltpu.VMEM)] * 6,
        out_shape=[quarter] * 4 + [wide] * 2,
        scratch_shapes=[
            pltpu.VMEM((8, -(-count // 128) * 128), F32),
            pltpu.VMEM((rows, lanes), BF16),
        ],
        cost_estimate=SMALL_COST,
        name="pack",
    )(where, w_query, w_key, w_value, w_inner, w_out, *lines)


def unpack_body(first_ref, second_ref, *rest):
    out_refs = rest[:9]
    rows = first_ref.shape[0]
    inner_rows = out_refs[8].shape[1]
    count = 8 * rows + inner_rows
    row, lane = place_of(rows, inner_rows)
    pick = jnp.where(lax.broadcasted_iota(jnp.int32, (128, count), 0) == lane, 1.0, 0.0)
    pick = pick.astype(BF16)
    spread = matmul(first_ref[...], pick) + matmul(second_ref[...], pick)
    inside = lax.broadcasted_iota(jnp.int32, (rows, count), 0) == row
    line = jnp.sum(jnp.where(inside, spread, 0.0), axis=0, keepdims=True)
    for slot, ref in enumerate(out_refs):
        ref[...] = line[:, slot * rows : slot * rows + ref.shape[1]]


def unpack(first, second, inner_rows):
    rows = first.shape[0]
    outs = pl.pallas_call(
        unpack_body,
        in_specs=[pl.BlockSpec(memory_space=pltpu.VMEM)] * 2,
        out_specs=[pl.BlockSpec(memory_space=pltpu.VMEM)] * 9,
        out_shape=[jax.ShapeDtypeStruct((1, rows), F32)] * 8
        + [jax.ShapeDtypeStruct((1, inner_rows), F32)],
        name="unpack",
    )(first, second)
    return [out.reshape(-1) for out in outs]


def project_rows(rows_ref, weight, bias, out_ref, at, step):
    share = weight.shape[1] // 3
    for start in range(0, rows_ref.shape[0], step):
        product = (matmul(rows_ref[start : start + step, :], weight) + bias).astype(BF16)
        place = slice(at + start, at + start + step)
        out_ref[place, :share] = product[:, :share] * 0.125
        out_ref[place, share:] = product[:, share:]


def project_first_body(where_ref, token_ref, mine_ref, other_ref, *rest):
    out_ref, weight_ref, small_ref, bias_ref, whole_ref, turned_ref, sems = rest
    half = mine_ref.shape[1]
    core = where_ref[1] % 2
    copies = [
        pltpu.make_async_copy(
            ref, whole_ref.at[:, pl.ds(pl.multiple_of(part * half, 128), half)], sems.at[n]
        )
        for n, (ref, part) in enumerate(((mine_ref, core), (other_ref, 1 - core)))
    ]
    for copy in copies:
        copy.start()
    for copy in copies:
        copy.wait()
    lanes = weight_ref.shape[1]
    share = lanes // 3
    small = whole_ref[:, lanes:]
    small_ref[...] = small
    weight_ref[...] = whole_ref[:, :lanes]
    turned_ref[...] = small.astype(F32).T
    mine = pl.ds(pl.multiple_of(where_ref[0] * share, 128), share)
    bias_ref[:, :share] = turned_ref[0:1, mine]
    bias_ref[:, share : 2 * share] = jnp.zeros((1, share), F32)
    bias_ref[:, 2 * share :] = turned_ref[1:2, mine]
    project_rows(token_ref, whole_ref[:, :lanes], bias_ref[...], out_ref, 0, 256)


def project_first(where, tokens, mine, other):
    width = tokens.shape[1]
    lanes = 2 * mine.shape[1]
    vmem = pl.BlockSpec(memory_space=pltpu.VMEM)
    smem = pl.BlockSpec(memory_space=pltpu.SMEM)
    return pl.pallas_call(
        project_first_body,
        in_specs=[smem, vmem] + [pl.BlockSpec(memory_space=pl.ANY)] * 2,
        out_specs=[vmem] * 4,
        out_shape=[
            jax.ShapeDtypeStruct((tokens.shape[0], lanes - 128), BF16),
            jax.ShapeDtypeStruct((width, lanes - 128), BF16),
            jax.ShapeDtypeStruct((width, 128), BF16),
            jax.ShapeDtypeStruct((1, lanes - 128), F32),
        ],
        scratch_shapes=[
            pltpu.VMEM((width, lanes), BF16),
            pltpu.VMEM((128, width), F32),
            pltpu.SemaphoreType.DMA((2,)),
        ],
        compiler_params=pltpu.CompilerParams(vmem_limit_bytes=VMEM_LIMIT),
        cost_estimate=SMALL_COST,
        name="project_first",
    )(where, tokens, mine, other)


def project_rest_body(weight_ref, bias_ref, *rest):
    *chunk_refs, out_ref = rest
    at = 0
    for ref in chunk_refs:
        project_rows(ref, weight_ref[...], bias_ref[...], out_ref, at, ref.shape[0])
        at += ref.shape[0]


def project_rest(chunks, weight, bias):
    rows = sum(chunk.shape[0] for chunk in chunks)
    vmem = pl.BlockSpec(memory_space=pltpu.VMEM)
    return pl.pallas_call(
        project_rest_body,
        in_specs=[vmem] * (2 + len(chunks)),
        out_specs=vmem,
        out_shape=jax.ShapeDtypeStruct((rows, weight.shape[1]), BF16),
        compiler_params=pltpu.CompilerParams(vmem_limit_bytes=VMEM_LIMIT),
        cost_estimate=SMALL_COST,
        name="project_rest",
    )(weight, bias, *chunks)


def lane_halves():
    lanes = lax.broadcasted_iota(jnp.int32, (1, 128), 1)
    low = jnp.where(lanes < 64, 1.0, 0.0)
    return low.astype(BF16), (1.0 - low).astype(BF16)


def attend_body(start, q_ref, k_ref, v_ref, prior_ref, row_seg, col_seg, *rest):
    logits_ref, probs_ref, out_ref = rest[-3:]
    halves = lane_halves()
    allowed = row_seg[...] == col_seg[0]
    queries = q_ref[...]
    mixed = None
    for head, half in enumerate(halves):
        scores = matmul_nt(queries, k_ref[...] * half) + prior_ref[head].astype(F32)
        logits_ref[head] = scores.astype(BF16)
        masked = jnp.where(allowed, scores, MASK_VALUE)
        top = jnp.max(masked, axis=1, keepdims=True)
        terms = jnp.exp(masked - top)
        total = jnp.sum(terms, axis=1, keepdims=True)
        probs = (terms * (1.0 / total)).astype(BF16)
        probs_ref[head] = probs
        part = matmul(probs, v_ref[...] * half)
        mixed = part if mixed is None else mixed + part
    out_ref[...] = mixed.astype(BF16)


def attend(qkv, prior, seg_rows, seg_cols, start, first, count, earlier):
    heads, group, window = prior.shape
    pairs = heads // 2
    share = heads * 64

    def qkv_spec(part):
        return pl.BlockSpec(
            (window, 128), lambda w, p, s: (first + w, part * pairs + p)
        )

    pair_spec = pl.BlockSpec((2, window, window), lambda w, p, s: (p, s[0] + w, 0))
    in_specs = [
        qkv_spec(0),
        qkv_spec(1),
        qkv_spec(2),
        pair_spec,
        pl.BlockSpec((window, 1), lambda w, p, s: (s[0] + w, 0)),
        pl.BlockSpec((1, 1, window), lambda w, p, s: (s[0] + w, 0, 0)),
    ]
    operands = [qkv, qkv, qkv, prior, seg_rows, seg_cols]
    aliases = {}
    if earlier is not None:
        aliases = {len(operands) + 1: 0, len(operands) + 2: 1}
        operands += list(earlier)
        in_specs += [pl.BlockSpec(memory_space=pl.ANY)] * 2
    big = jax.ShapeDtypeStruct(prior.shape, BF16)
    return pl.pallas_call(
        attend_body,
        grid_spec=pltpu.PrefetchScalarGridSpec(
            num_scalar_prefetch=1,
            grid=(count, pairs),
            in_specs=in_specs,
            out_specs=[
                pair_spec,
                pair_spec,
                pl.BlockSpec((window, 128), lambda w, p, s: (w, p)),
            ],
        ),
        out_shape=[
            big,
            big,
            jax.ShapeDtypeStruct((count * window, share), BF16),
        ],
        input_output_aliases=aliases,
        compiler_params=pltpu.CompilerParams(vmem_limit_bytes=VMEM_LIMIT),
        cost_estimate=SMALL_COST,
        name="attend",
    )(start, *operands)


def attend_back_body(
    start, q_ref, k_ref, v_ref, probs_ref, grad_ref, out_ref, *rest
):
    d_scores_ref, d_qkv_ref, sums_ref = rest[-3:]
    pair = pl.program_id(1)
    pairs = pl.num_programs(1)
    halves = lane_halves()
    grads = grad_ref[...]
    product = grads.astype(F32) * out_ref[...].astype(F32)
    d_queries = d_keys = d_values = None
    for head, half in enumerate(halves):
        probs = probs_ref[head]
        inner = jnp.sum(product * half.astype(F32), axis=1, keepdims=True)
        d_probs = matmul_nt(grads, v_ref[...] * half)
        d_scores = (probs.astype(F32) * (d_probs - inner)).astype(BF16)
        d_scores_ref[head] = d_scores
        parts = (
            matmul(d_scores, k_ref[...] * half),
            matmul_tn(d_scores, q_ref[...] * half),
            matmul_tn(probs, grads * half),
        )
        if head == 0:
            d_queries, d_keys, d_values = parts
        else:
            d_queries += parts[0]
            d_keys += parts[1]
            d_values += parts[2]
    for slot, value in enumerate((d_queries * 0.125, d_keys, d_values)):
        lanes = pl.ds(pl.multiple_of((slot * pairs + pair) * 128, 128), 128)
        d_qkv_ref[:, lanes] = value.astype(BF16)
        sums_ref[:, lanes] = row_sum(value)


def attend_back(qkv, probs, grads, outs, start, first, earlier):
    heads, group, window = probs.shape
    pairs = heads // 2
    share = heads * 64

    def qkv_spec(part):
        return pl.BlockSpec(
            (window, 128), lambda w, p, s: (first + w, part * pairs + p)
        )

    pair_spec = pl.BlockSpec((2, window, window), lambda w, p, s: (p, s[0] + w, 0))
    row_spec = pl.BlockSpec((window, 128), lambda w, p, s: (w, p))
    in_specs = [qkv_spec(0), qkv_spec(1), qkv_spec(2), pair_spec, row_spec, row_spec]
    operands = [qkv, qkv, qkv, probs, grads, outs]
    aliases = {}
    if earlier is not None:
        aliases = {len(operands) + 1: 0}
        operands.append(earlier)
        in_specs.append(pl.BlockSpec(memory_space=pl.ANY))
    return pl.pallas_call(
        attend_back_body,
        grid_spec=pltpu.PrefetchScalarGridSpec(
            num_scalar_prefetch=1,
            grid=(1, pairs),
            in_specs=in_specs,
            out_specs=[
                pair_spec,
                pl.BlockSpec((window, 3 * share), lambda w, p, s: (0, 0)),
                pl.BlockSpec((1, 3 * share), lambda w, p, s: (0, 0)),
            ],
        ),
        out_shape=[
            jax.ShapeDtypeStruct(probs.shape, BF16),
            jax.ShapeDtypeStruct((window, 3 * share), BF16),
            jax.ShapeDtypeStruct((1, 3 * share), F32),
        ],
        input_output_aliases=aliases,
        compiler_params=pltpu.CompilerParams(vmem_limit_bytes=VMEM_LIMIT),
        cost_estimate=SMALL_COST,
        name="attend_back",
    )(start, *operands)


def normed(values):
    centred = values - jnp.mean(values, axis=-1, keepdims=True)
    inv_dev = lax.rsqrt(
        jnp.mean(centred * centred, axis=-1, keepdims=True) + NORM_EPSILON
    )
    return centred * inv_dev, inv_dev


def normed_back(scaled, unit, inv_dev):
    return inv_dev * (
        scaled
        - jnp.mean(scaled, axis=-1, keepdims=True)
        - unit * jnp.mean(scaled * unit, axis=-1, keepdims=True)
    )


def row_sum(values):
    return jnp.sum(values, axis=0, keepdims=True)


def forward_back_body(
    where_ref,
    own_ref,
    received_ref,
    token_ref,
    grad_ref,
    vector_ref,
    bias_ref,
    mine_ref,
    other_ref,
    whole_outer_ref,
    *rest,
    chunk,
):
    rest = rest[-16:]
    (
        result_ref,
        attended_ref,
        hidden_ref,
        inner_ref,
        d_branch_ref,
        d_pre_ref,
        d_proj_ref,
        d_theirs_ref,
        d_own_ref,
        sums_ref,
        inner_sums_ref,
        slope_ref,
        d_heads_ref,
        wide_ref,
        outer_ref,
        sems,
    ) = rest
    core = where_ref[1] % 2
    copies = [
        pltpu.make_async_copy(mine_ref, wide_ref.at[core], sems.at[0]),
        pltpu.make_async_copy(other_ref, wide_ref.at[1 - core], sems.at[1]),
        pltpu.make_async_copy(whole_outer_ref, outer_ref, sems.at[2]),
    ]
    for copy in copies:
        copy.start()
    first_ref, second_ref = wide_ref.at[0], wide_ref.at[1]
    share = own_ref.shape[1]
    half = outer_ref.shape[0] // 2
    side = where_ref[0]
    mine = pl.ds(pl.multiple_of(side * share, 128), share)
    theirs = pl.ds(pl.multiple_of((1 - side) * share, 128), share)
    attended_ref[:, mine] = own_ref[...]
    attended_ref[:, theirs] = received_ref[...]
    attended = attended_ref[...]
    out_bias, attn_gain, attn_shift, outer_bias, ffn_gain, ffn_shift = (
        vector_ref[n : n + 1] for n in range(6)
    )
    copies[0].wait()
    copies[1].wait()
    projected = jnp.concatenate(
        [matmul(attended, first_ref[:, half:]), matmul(attended, second_ref[:, half:])], axis=1
    )
    resid_one = token_ref[...].astype(F32) + projected + out_bias
    unit_one, inv_one = normed(resid_one)
    hidden = unit_one * attn_gain + attn_shift
    hidden_low = hidden.astype(BF16)
    hidden_ref[...] = hidden_low
    spans = [
        (ref, start, part * half + start)
        for part, ref in enumerate((first_ref, second_ref))
        for start in range(0, half, chunk)
    ]
    copies[2].wait()
    resid_two = hidden + outer_bias
    for ref, start, place in spans:
        lanes = slice(place, place + chunk)
        pre_act = matmul(hidden_low, ref[:, start : start + chunk]) + bias_ref[:, lanes]
        phi = 0.5 * (1.0 + lax.erf(pre_act * INV_SQRT_TWO))
        density = INV_SQRT_TWO_PI * jnp.exp(-0.5 * pre_act * pre_act)
        inner_low = (pre_act * phi).astype(BF16)
        inner_ref[:, lanes] = inner_low
        slope_ref[:, lanes] = (phi + pre_act * density).astype(BF16)
        resid_two += matmul(inner_low, outer_ref[lanes, :])
    unit_two, inv_two = normed(resid_two)
    result_ref[...] = (unit_two * ffn_gain + ffn_shift).astype(BF16)
    cotangent = grad_ref[...].astype(F32)
    d_resid_two = normed_back(cotangent * ffn_gain, unit_two, inv_two)
    d_branch = d_resid_two.astype(BF16)
    d_branch_ref[...] = d_branch
    d_hidden = d_resid_two
    inner_sums = []
    for ref, start, place in spans:
        lanes = slice(place, place + chunk)
        d_pre = matmul_nt(d_branch, outer_ref[lanes, :]) * slope_ref[:, lanes].astype(F32)
        inner_sums.append(row_sum(d_pre))
        d_pre_low = d_pre.astype(BF16)
        d_pre_ref[:, lanes] = d_pre_low
        d_hidden += matmul_nt(d_pre_low, ref[:, start : start + chunk])
    d_resid_one = normed_back(d_hidden * attn_gain, unit_one, inv_one)
    d_proj = d_resid_one.astype(BF16)
    d_proj_ref[...] = d_proj
    d_heads_ref[...] = (
        matmul_nt(d_proj[:, :share], first_ref[:, half:])
        + matmul_nt(d_proj[:, share:], second_ref[:, half:])
    ).astype(BF16)
    d_own_ref[...] = d_heads_ref[:, mine]
    d_theirs_ref[...] = d_heads_ref[:, theirs]
    sums_ref[...] = jnp.concatenate(
        [
            row_sum(d_resid_one),
            row_sum(d_hidden * unit_one),
            row_sum(d_hidden),
            row_sum(d_resid_two),
            row_sum(cotangent * unit_two),
            row_sum(cotangent),
            jnp.zeros((2, d_resid_one.shape[1]), F32),
        ],
        axis=0,
    )
    inner_sums_ref[...] = jnp.concatenate(inner_sums, axis=1)


def forward_back(where, own, received, tokens, grads, weights, vectors, bias, at, rows, earlier):
    width = tokens.shape[1]
    share = own.shape[1]
    units = bias.shape[1]
    chunk = units // 6
    tops = [(2, width, units // 2 + share), (units, width)]

    def whole(array):
        return pl.BlockSpec(array.shape, lambda i, s: (0, 0), pipeline_mode=pl.Buffered(1))

    def local(lanes):
        return pl.BlockSpec((rows, lanes), lambda i, s: (0, 0), pipeline_mode=pl.Buffered(1))

    def placed(lanes):
        return pl.BlockSpec((rows, lanes), lambda i, s: (at, 0), pipeline_mode=pl.Buffered(1))

    lanes_out = [width, width, width, units, width, units, width, share, share]
    sources = list(weights)
    kept = len(lanes_out) - 2
    aliases = {}
    if earlier is not None:
        sources += list(earlier)
        aliases = {7 + len(sources) - kept + n: n for n in range(kept)}
    return pl.pallas_call(
        functools.partial(forward_back_body, chunk=chunk),
        grid_spec=pltpu.PrefetchScalarGridSpec(
            num_scalar_prefetch=1,
            grid=(1,),
            in_specs=[
                local(share),
                local(share),
                placed(width),
                placed(width),
                whole(vectors),
                whole(bias),
            ]
            + [pl.BlockSpec(memory_space=pl.ANY)] * len(sources),
            out_specs=[placed(lanes) for lanes in lanes_out[:kept]]
            + [local(lanes) for lanes in lanes_out[kept:]]
            + [
                pl.BlockSpec((8, width), lambda i, s: (0, 0)),
                pl.BlockSpec((1, units), lambda i, s: (0, 0)),
            ],
            scratch_shapes=[pltpu.VMEM((rows, units), BF16), pltpu.VMEM((rows, width), BF16)]
            + [pltpu.VMEM(shape, BF16) for shape in tops]
            + [pltpu.SemaphoreType.DMA((3,))],
        ),
        out_shape=[
            jax.ShapeDtypeStruct((tokens.shape[0] if n < kept else rows, lanes), BF16)
            for n, lanes in enumerate(lanes_out)
        ]
        + [
            jax.ShapeDtypeStruct((8, width), F32),
            jax.ShapeDtypeStruct((1, units), F32),
        ],
        input_output_aliases=aliases,
        compiler_params=pltpu.CompilerParams(vmem_limit_bytes=VMEM_LIMIT),
        cost_estimate=SMALL_COST,
        name="forward_back",
    )(where, own, received, tokens, grads, vectors, bias, *sources)


def shards(
    hidden_in,
    prev_logits,
    segment,
    w_query,
    b_query,
    w_key,
    w_value,
    b_value,
    w_out,
    b_out,
    gain_attn,
    shift_attn,
    w_inner,
    b_inner,
    w_outer,
    b_outer,
    gain_ffn,
    shift_ffn,
    out_grad,
):
    seq = lax.axis_index("seq").astype(jnp.int32)
    fsdp_count = lax.axis_size("fsdp")
    count = fsdp_count.bit_length() - 1
    devices = 2 * fsdp_count
    heads, group, window = prev_logits.shape
    rows, width = w_query.shape
    inner_rows = b_inner.shape[0]
    hidden_units = inner_rows * devices
    share = width // 2
    half = hidden_units // 2
    tokens = hidden_in.shape[0]
    own_windows = tokens // window
    seq_hop = ("seq", 1)
    far, near, core = plan_hops(count)
    done = len(far)

    vectors = (b_query, b_value, b_out, gain_attn, shift_attn, b_outer, gain_ffn, shift_ffn, b_inner)
    where = jnp.stack([seq, lax.axis_index("fsdp").astype(jnp.int32)])
    unit, unit_core, unit_seq, unit_both, wide, wide_core = pack(
        where, w_query, w_key, w_value, w_inner, w_out, vectors
    )
    parts = 4
    part_rows = tokens // parts
    others = []

    def next_part(*earlier):
        part = hidden_in[len(others) * part_rows : (len(others) + 1) * part_rows]
        others.append(swap(after(part, *earlier), seq_hop))

    def quad(flip_seq, flip_core):
        def place(n, at_seq, at):
            one, two = bit_of(seq_hop, at_seq, at), bit_of(core, at_seq, at)
            return 2 * (1 - one if flip_seq else one) + (1 - two if flip_core else two)

        return place

    def both_flipped(at_seq, at):
        return at_seq ^ 1, at ^ 1

    def pairs_of(blocks):
        return blocks.reshape(-1, 2 * blocks.shape[1], blocks.shape[2])

    def hopped(blocks, hop, inner):
        return joined(blocks, swap(blocks, hop), hop, inner)

    unit, wide = merge(
        where,
        [
            (unit[None], quad(False, False)),
            (swap(unit_seq, seq_hop)[None], quad(True, False)),
            (swap(unit_core, core)[None], quad(False, True)),
            (trade(unit_both, both_flipped)[None], quad(True, True)),
        ],
        joined(wide[None], swap(wide_core, core)[None], core, 1),
    )
    unit, wide = pairs_of(unit), pairs_of(wide)
    next_part(unit)
    wide_item = hopped(wide, far[0], 1)
    unit, wide = merge(
        where, hopped(unit, far[0], 1), [(after(wide_item[0][0], others[0]), wide_item[0][1]), wide_item[1]]
    )
    for place, hop in enumerate(far[1:]):
        last = place == len(far) - 2
        if last:
            next_part(unit)
        unit_item = hopped(unit, hop, 1)
        if last:
            unit_item[0] = (after(unit_item[0][0], others[-1]), unit_item[0][1])
        (unit,) = merge(where, unit_item)
        if not last:
            (wide,) = merge(where, hopped(wide, hop, 1))
    outer = lax.all_gather(after(w_outer, unit), ("seq", "fsdp"), axis=0, tiled=True)
    next_part(unit)
    wide_item = hopped(after(wide, unit), far[-1], 1)
    unit, wide = merge(
        where, hopped(unit, near, 1), [(after(wide_item[0][0], others[-1]), wide_item[0][1]), wide_item[1]]
    )
    next_part(unit)
    unit = unit.reshape(width, unit.shape[-1])
    unit_other = swap(unit, core)

    def near_or_seq(at_seq, at):
        return across(near if at % 2 == 0 else seq_hop)(at_seq, at)

    def seq_or_near(at_seq, at):
        return across(seq_hop if at % 2 == 0 else near)(at_seq, at)

    wide_other = trade(wide, near_or_seq)
    own_qkv, qkv_weight, small, qkv_bias = project_first(where, hidden_in, unit, unit_other)

    seg_rows = segment[:, None]
    seg_cols = segment.reshape(group // window, 1, window)
    own_start = (seq * own_windows).reshape(1)
    other_start = ((1 - seq) * own_windows).reshape(1)

    own_out = []
    logits_probs = None
    for w in range(own_windows):
        logits, probs, out = attend(
            own_qkv, prev_logits, seg_rows, seg_cols, own_start + w, w, 1, logits_probs
        )
        logits_probs = (logits, probs)
        own_out.append(out)
        if w == 0:
            blocks = wide.shape[0]
            (wide,) = merge(
                where,
                joined_by_core(
                    after(wide, out, others[-1]), wide_other, core, (near, 1), (seq_hop, blocks)
                ),
            )
            wide_other = trade(wide, seq_or_near)
            own_qkv = after(own_qkv, wide)
    other_qkv = project_rest(after(tuple(others), own_out[-1]), qkv_weight, qkv_bias)
    other_out = []
    received = []
    for w in range(own_windows):
        logits, probs, out = attend(
            other_qkv, prev_logits, seg_rows, seg_cols, other_start + w, w, 1, (logits, probs)
        )
        other_out.append(out)
        if w == 0:
            blocks = wide.shape[0]
            (wide,) = merge(
                where,
                joined_by_core(after(wide, out), wide_other, core, (seq_hop, blocks), (near, 1)),
            )
            out = after(out, wide)
            wide = wide.reshape(width, wide.shape[-1])
            wide_other = swap(wide, core)
            other_qkv = after(other_qkv, wide)
        received.append(swap(out, seq_hop))
    weights = (wide, wide_other, outer)
    small = small.astype(F32)
    layer_vectors = jnp.concatenate([small[:, 2:8].T, jnp.zeros((2, width), F32)], axis=0)
    inner_bias = small[:, 8 : 8 + hidden_units // width].reshape(1, hidden_units)

    full = None
    d_others, d_own = [], []
    sums, inner_sums = 0.0, 0.0
    for w in range(own_windows):
        outs = forward_back(
            where,
            own_out[w],
            received[w],
            hidden_in,
            out_grad,
            weights,
            layer_vectors,
            inner_bias,
            w,
            window,
            full,
        )
        full = outs[:7]
        d_others.append(swap(outs[7], seq_hop))
        d_own.append(outs[8])
        sums += outs[9]
        inner_sums += outs[10]
    hidden_out, attended, hidden, inner, d_branch, d_pre, d_proj = full

    class Reduction:
        def __init__(self, value, hops):
            self.value, self.hops = value, list(hops)
            self.send()

        def send(self):
            if self.hops:
                hop, place = self.hops.pop(0)
                away, self.keep = split(self.value, hop, place)
                self.other = swap(away, hop)

        def add(self, latest):
            self.value = total(after(self.keep, latest), self.other)
            self.send()
            return self.value

    grid = (2,) * (count + 1)
    outer_hops = [(core, done + 2), (near, done + 1)]
    outer_hops += [(far[n], n + 1) for n in reversed(range(done))] + [(seq_hop, 0)]
    inner_hops = [(core, done + 2), (seq_hop, 0), (near, done)]
    inner_hops += [(far[n], n) for n in reversed(range(done))]
    tail_hops = [(core, done + 2), (near, done + 1)]
    tail_hops += [(far[n], n + 1) for n in reversed(range(done))]

    inner, attended = after((inner, attended), d_others[0])
    g_outer = matmul_tn(inner, d_branch).astype(BF16)
    g_out = matmul_tn(attended, d_proj).astype(BF16)
    outer_grad = jnp.concatenate(
        [
            g_outer.reshape(grid + (inner_rows, width)),
            g_out.reshape(grid + (rows, width)),
        ],
        axis=-2,
    )
    outer_sum = Reduction(outer_grad, outer_hops)
    g_inner = matmul_tn(after(hidden, outer_grad), d_pre).astype(BF16)
    inner_sum = Reduction(g_inner.reshape(grid + (rows, hidden_units)), inner_hops)
    latest = outer_sum.add(g_inner)
    latest = inner_sum.add(latest)

    d_scores = None
    input_received = []
    other_qkv = after(other_qkv, latest)
    g_qkv, qkv_sum = 0.0, 0.0
    for w in range(own_windows):
        d_scores, d_qkv, column_sums = attend_back(
            other_qkv, probs, d_others[w], other_out[w], other_start + w, w, d_scores
        )
        input_received.append(swap(matmul_nt(d_qkv, qkv_weight).astype(BF16), seq_hop))
        per_window = parts // own_windows
        rows_of = jnp.concatenate(others[w * per_window : (w + 1) * per_window], axis=0)
        g_qkv += matmul_tn(rows_of, d_qkv)
        qkv_sum += column_sums
    latest = outer_sum.add(d_qkv)
    own_qkv = after(own_qkv, latest)
    own_d_qkv = []
    for w in range(own_windows):
        d_scores, d_qkv, column_sums = attend_back(
            own_qkv, probs, d_own[w], own_out[w], own_start + w, w, d_scores
        )
        if w == 0:
            latest = inner_sum.add(d_qkv)
            own_qkv = after(own_qkv, latest)
        if w == own_windows - 1:
            latest = outer_sum.add(d_qkv)
            d_qkv = after(d_qkv, latest)
        own_d_qkv.append(d_qkv)
        g_qkv += matmul_tn(hidden_in[w * window : (w + 1) * window], d_qkv)
        qkv_sum += column_sums
    qkv_sum = qkv_sum.reshape(-1)

    def both_sides(part):
        blank = jnp.zeros_like(part)
        return jnp.where(
            seq == 0, jnp.concatenate([part, blank]), jnp.concatenate([blank, part])
        )

    small_grads = jnp.concatenate(
        [
            both_sides(qkv_sum[:share])[:, None],
            both_sides(qkv_sum[2 * share :])[:, None],
            sums[:6].T,
            inner_sums.reshape(width, hidden_units // width),
        ],
        axis=1,
    )
    lanes = small_grads.shape[1]
    tail = jnp.concatenate(
        [g_qkv.astype(BF16), jnp.pad(small_grads, ((0, 0), (0, 128 - lanes))).astype(BF16)], axis=1
    ).reshape(grid + (rows, 3 * share + 128))
    tail_sum = Reduction(tail, tail_hops)
    latest = inner_sum.add(tail)
    waiting = [tail_sum, outer_sum, tail_sum, inner_sum]
    for item in waiting + [outer_sum, tail_sum, inner_sum]:
        latest = item.add(latest)
    while outer_sum.hops or inner_sum.hops or len(tail_sum.value.shape) > 3:
        for item in (outer_sum, inner_sum, tail_sum):
            if len(item.value.shape) > (3 if item is tail_sum else 2):
                latest = item.add(latest)
    tail, outer_grad, inner_grad = tail_sum.value, outer_sum.value, inner_sum.value
    send, own_tail = split(tail, seq_hop, 0)
    other_tail = swap(send, seq_hop)
    grads = unpack(own_tail[:, 3 * share :], other_tail[:, 3 * share :], inner_rows)

    def weight_part(slot):
        at = slice(slot * share, (slot + 1) * share)
        return jnp.where(
            seq == 0,
            jnp.concatenate([own_tail[:, at], other_tail[:, at]], axis=1),
            jnp.concatenate([other_tail[:, at], own_tail[:, at]], axis=1),
        ).astype(F32)

    input_grad = jnp.concatenate(
        [
            (
                d_proj[w * window : (w + 1) * window].astype(F32)
                + matmul_nt(own_d_qkv[w], qkv_weight)
                + input_received[w].astype(F32)
            ).astype(BF16)
            for w in range(own_windows)
        ],
        axis=0,
    )
    return (
        hidden_out,
        logits,
        input_grad,
        d_scores,
        weight_part(0),
        grads[0],
        weight_part(1),
        weight_part(2),
        grads[1],
        outer_grad[inner_rows:].astype(F32),
        grads[2],
        grads[3],
        grads[4],
        inner_grad.astype(F32),
        grads[8],
        outer_grad[:inner_rows].astype(F32),
        grads[5],
        grads[6],
        grads[7],
    )


def solution(mesh):
    in_specs = (
        P(("fsdp", "seq"), None),
        P("seq", "fsdp", None),
        P("fsdp"),
        P(("seq", "fsdp"), None),
        P(("seq", "fsdp")),
        P(("seq", "fsdp"), None),
        P(("seq", "fsdp"), None),
        P(("seq", "fsdp")),
        P(("seq", "fsdp"), None),
        P(("seq", "fsdp")),
        P(("seq", "fsdp")),
        P(("seq", "fsdp")),
        P(("seq", "fsdp"), None),
        P(("seq", "fsdp")),
        P(("seq", "fsdp"), None),
        P(("seq", "fsdp")),
        P(("seq", "fsdp")),
        P(("seq", "fsdp")),
        P(("fsdp", "seq"), None),
    )
    out_specs = (
        P(("fsdp", "seq"), None),
        P("seq", "fsdp", None),
        P(("fsdp", "seq"), None),
        P("seq", "fsdp", None),
        P(("seq", "fsdp"), None),
        P(("seq", "fsdp")),
        P(("seq", "fsdp"), None),
        P(("seq", "fsdp"), None),
        P(("seq", "fsdp")),
        P(("seq", "fsdp"), None),
        P(("seq", "fsdp")),
        P(("seq", "fsdp")),
        P(("seq", "fsdp")),
        P(("seq", "fsdp"), None),
        P(("seq", "fsdp")),
        P(("seq", "fsdp"), None),
        P(("seq", "fsdp")),
        P(("seq", "fsdp")),
        P(("seq", "fsdp")),
    )
    return jax.shard_map(shards, mesh=mesh, in_specs=in_specs, out_specs=out_specs, check_vma=False)
```

```python
import functools
import math

import jax
import jax.numpy as jnp
from jax import lax
from jax.experimental import pallas as pl
from jax.experimental.pallas import tpu as pltpu
from jax.sharding import PartitionSpec as P

NORM_EPSILON = 1e-06
MASK_VALUE = -1e30
INV_SQRT_TWO = 0.7071067811865476
INV_SQRT_TWO_PI = 0.3989422804014327
VMEM_LIMIT = 56 * 1024 * 1024
BF16 = jnp.bfloat16
F32 = jnp.float32
SMALL_COST = pl.CostEstimate(flops=1024, transcendentals=0, bytes_accessed=1024)


def matmul(left_op, right_op):
    return jnp.dot(left_op, right_op, preferred_element_type=F32)


def matmul_tn(left_op, right_op):
    return lax.dot_general(
        left_op, right_op, (((0,), (0,)), ((), ())), preferred_element_type=F32
    )


def matmul_nt(left_op, right_op):
    return lax.dot_general(
        left_op, right_op, (((1,), (1,)), ((), ())), preferred_element_type=F32
    )


def column_sum(values):
    return jnp.sum(values.astype(F32), axis=0)


BOTH = ("seq", "fsdp")


def trade(value, partner):
    seq_count, fsdp_count = lax.axis_size("seq"), lax.axis_size("fsdp")
    pairs = []
    for seq in range(seq_count):
        for at in range(fsdp_count):
            to_seq, to = partner(seq, at)
            pairs.append((seq * fsdp_count + at, to_seq * fsdp_count + to))
    return lax.ppermute(value, BOTH, pairs)


def across(hop):
    axis, mask = hop
    if axis == "seq":
        return lambda seq, at: (seq ^ mask, at)
    return lambda seq, at: (seq, at ^ mask)


def swap(value, hop):
    return trade(value, across(hop))


def bit_of(hop, seq, at):
    axis, mask = hop
    return (seq if axis == "seq" else at // mask) % 2


def my_bit(hop):
    at = lax.axis_index(hop[0]).astype(jnp.int32)
    return bit_of(hop, at, at)


def after(value, *others):
    return lax.optimization_barrier((value,) + others)[0]


def merge_body(where_ref, *refs, plans):
    seq, at = where_ref[0], where_ref[1]
    outs = refs[sum(len(plan) for plan in plans) :]
    for plan, out_ref in zip(plans, outs):
        for target in plan:
            source, refs = refs[0], refs[1:]
            for n in range(source.shape[0]):
                out_ref[target(n, seq, at)] = source[n]


def merge(where, *items):
    sources = [blocks for item in items for blocks, _ in item]
    plans = [[target for _, target in item] for item in items]
    outs = []
    for item in items:
        total_blocks = sum(blocks.shape[0] for blocks, _ in item)
        outs.append(jax.ShapeDtypeStruct((total_blocks,) + item[0][0].shape[1:], BF16))
    return pl.pallas_call(
        functools.partial(merge_body, plans=plans),
        in_specs=[pl.BlockSpec(memory_space=pltpu.SMEM)]
        + [pl.BlockSpec(memory_space=pltpu.VMEM)] * len(sources),
        out_specs=[pl.BlockSpec(memory_space=pltpu.VMEM)] * len(outs),
        out_shape=outs,
        compiler_params=pltpu.CompilerParams(vmem_limit_bytes=VMEM_LIMIT),
        cost_estimate=SMALL_COST,
        name="merge",
    )(where, *sources)


def spread(hop, inner):
    def target(flip):
        def place(n, seq, at):
            bit = bit_of(hop, seq, at)
            bit = 1 - bit if flip else bit
            return (n // inner) * 2 * inner + n % inner + bit * inner

        return place

    return target(False), target(True)


def joined(mine, other, hop, inner):
    own_place, other_place = spread(hop, inner)
    return [(mine, own_place), (other, other_place)]


def by_core(core, zero, one):
    def place(n, seq, at):
        bit = bit_of(core, seq, at)
        return (1 - bit) * zero(n, seq, at) + bit * one(n, seq, at)

    return place


def joined_by_core(mine, other, core, zero, one):
    zero_places, one_places = spread(*zero), spread(*one)
    return [
        (mine, by_core(core, zero_places[0], one_places[0])),
        (other, by_core(core, zero_places[1], one_places[1])),
    ]


def split(value, hop, place):
    bit = my_bit(hop)
    return (
        lax.dynamic_index_in_dim(value, 1 - bit, place, keepdims=False),
        lax.dynamic_index_in_dim(value, bit, place, keepdims=False),
    )


def total(one, two):
    return (one.astype(F32) + two.astype(F32)).astype(BF16)


def plan_hops(count):
    bits = [("fsdp", 1 << n) for n in range(count)]
    return list(reversed(bits[2:])), bits[1], bits[0]


def place_of(rows, inner_rows):
    count = 8 * rows + inner_rows
    per_row = inner_rows // rows
    entry = lax.broadcasted_iota(jnp.int32, (1, count), 1)
    row, lane = entry * 0, entry * 0
    for slot in range(8):
        inside = (entry >= slot * rows) & (entry < (slot + 1) * rows)
        row = jnp.where(inside, entry - slot * rows, row)
        lane = jnp.where(inside, slot, lane)
    for unit in range(rows):
        low = 8 * rows + unit * per_row
        inside = (entry >= low) & (entry < low + per_row)
        row = jnp.where(inside, unit, row)
        lane = jnp.where(inside, 8 + entry - low, lane)
    return row, lane


def pack_body(where_ref, q_ref, k_ref, v_ref, *rest):
    small_refs = rest[:9]
    quarter_refs = (rest[9:11], rest[11:13])
    line_ref, whole_ref = rest[13:]
    rows, width = q_ref.shape
    share = width // 2
    lanes = quarter_refs[0][0].shape[1]
    inner_rows = small_refs[8].shape[1]
    side, core = where_ref[0], where_ref[1] % 2
    for slot, ref in enumerate(small_refs):
        line_ref[0:1, slot * rows : slot * rows + ref.shape[1]] = ref[...].astype(F32)
    row, lane = place_of(rows, inner_rows)
    count = 8 * rows + inner_rows
    spread_line = jnp.where(
        lax.broadcasted_iota(jnp.int32, (rows, count), 0) == row, line_ref[0:1, :count], 0.0
    )
    pick = jnp.where(lax.broadcasted_iota(jnp.int32, (128, count), 0) == lane, 1.0, 0.0)
    extra = matmul_nt(spread_line.astype(BF16), pick.astype(BF16)).astype(BF16)
    for turn in range(2):
        start = pl.multiple_of(((side + turn) % 2) * share, 128)
        for slot, ref in enumerate((q_ref, k_ref, v_ref)):
            whole_ref[:, slot * share : (slot + 1) * share] = ref[:, pl.ds(start, share)]
        whole_ref[:, 3 * share :] = extra
        for other in range(2):
            at = pl.multiple_of(((core + other) % 2) * lanes, 128)
            quarter_refs[turn][other][...] = whole_ref[:, pl.ds(at, lanes)]


def pack(where, w_query, w_key, w_value, vectors):
    rows, width = w_query.shape
    lines = [v.reshape(1, -1) for v in vectors]
    count = sum(line.shape[1] for line in lines)
    lanes = 3 * width // 2 + 128
    quarter = jax.ShapeDtypeStruct((rows, lanes // 2), BF16)
    return pl.pallas_call(
        pack_body,
        in_specs=[pl.BlockSpec(memory_space=pltpu.SMEM)]
        + [pl.BlockSpec(memory_space=pltpu.VMEM)] * (3 + len(lines)),
        out_specs=[pl.BlockSpec(memory_space=pltpu.VMEM)] * 4,
        out_shape=[quarter] * 4,
        scratch_shapes=[
            pltpu.VMEM((8, -(-count // 128) * 128), F32),
            pltpu.VMEM((rows, lanes), BF16),
        ],
        cost_estimate=SMALL_COST,
        name="pack",
    )(where, w_query, w_key, w_value, *lines)


def cut_body(where_ref, inner_ref, out_ref, other_inner_ref, other_out_ref, *half_refs, hop):
    half, share = inner_ref.shape[1] // 2, out_ref.shape[1] // 2
    core = where_ref[1] % 2
    bit = bit_of(hop, where_ref[0], where_ref[1])
    for turn, ref in enumerate(half_refs):
        part = (core + turn) % 2
        inner_lanes = pl.ds(pl.multiple_of(part * half, 128), half)
        out_lanes = pl.ds(pl.multiple_of(part * share, 128), share)
        for place, inner, out in (
            (bit, inner_ref, out_ref),
            (1 - bit, other_inner_ref, other_out_ref),
        ):
            ref[place, :, :half] = inner[:, inner_lanes]
            ref[place, :, half:] = out[:, out_lanes]


def cut(where, inner, out, other_inner, other_out, hop):
    rows = inner.shape[0]
    half = jax.ShapeDtypeStruct((2, rows, (inner.shape[1] + out.shape[1]) // 2), BF16)
    return pl.pallas_call(
        functools.partial(cut_body, hop=hop),
        in_specs=[pl.BlockSpec(memory_space=pltpu.SMEM)]
        + [pl.BlockSpec(memory_space=pltpu.VMEM)] * 4,
        out_specs=[pl.BlockSpec(memory_space=pltpu.VMEM)] * 2,
        out_shape=[half, half],
        cost_estimate=SMALL_COST,
        name="cut",
    )(where, inner, out, other_inner, other_out)


def unpack_body(first_ref, second_ref, *rest):
    out_refs = rest[:9]
    rows = first_ref.shape[0]
    inner_rows = out_refs[8].shape[1]
    count = 8 * rows + inner_rows
    row, lane = place_of(rows, inner_rows)
    pick = jnp.where(lax.broadcasted_iota(jnp.int32, (128, count), 0) == lane, 1.0, 0.0)
    pick = pick.astype(BF16)
    spread = matmul(first_ref[...], pick) + matmul(second_ref[...], pick)
    inside = lax.broadcasted_iota(jnp.int32, (rows, count), 0) == row
    line = jnp.sum(jnp.where(inside, spread, 0.0), axis=0, keepdims=True)
    for slot, ref in enumerate(out_refs):
        ref[...] = line[:, slot * rows : slot * rows + ref.shape[1]]


def unpack(first, second, inner_rows):
    rows = first.shape[0]
    outs = pl.pallas_call(
        unpack_body,
        in_specs=[pl.BlockSpec(memory_space=pltpu.VMEM)] * 2,
        out_specs=[pl.BlockSpec(memory_space=pltpu.VMEM)] * 9,
        out_shape=[jax.ShapeDtypeStruct((1, rows), F32)] * 8
        + [jax.ShapeDtypeStruct((1, inner_rows), F32)],
        name="unpack",
    )(first, second)
    return [out.reshape(-1) for out in outs]


def project_block(rows, weight, bias, out_ref):
    scale = jnp.where(pl.program_id(0) == 0, 0.125, 1.0)
    out_ref[...] = ((matmul(rows, weight) + bias).astype(BF16).astype(F32) * scale).astype(BF16)


def project_first_body(where_ref, token_ref, mine_ref, other_ref, *rest):
    out_ref, weight_ref, small_ref, bias_ref, whole_ref, turned_ref, sems = rest
    half = mine_ref.shape[1]
    share = weight_ref.shape[1]
    step = pl.program_id(0)

    @pl.when(step == 0)
    def _():
        core = where_ref[1] % 2
        copies = [
            pltpu.make_async_copy(
                ref, whole_ref.at[:, pl.ds(pl.multiple_of(part * half, 128), half)], sems.at[n]
            )
            for n, (ref, part) in enumerate(((mine_ref, core), (other_ref, 1 - core)))
        ]
        for copy in copies:
            copy.start()
        for copy in copies:
            copy.wait()
        small = whole_ref[:, 3 * share :]
        small_ref[...] = small
        turned_ref[...] = small.astype(F32).T
        mine = pl.ds(pl.multiple_of(where_ref[0] * share, 128), share)
        bias_ref[:, :share] = turned_ref[0:1, mine]
        bias_ref[:, share : 2 * share] = jnp.zeros((1, share), F32)
        bias_ref[:, 2 * share :] = turned_ref[1:2, mine]

    lanes = pl.ds(pl.multiple_of(step * share, 128), share)
    weight = whole_ref[:, lanes]
    weight_ref[...] = weight
    project_block(token_ref[...], weight, bias_ref[:, lanes], out_ref)


def project_first(where, tokens, mine, other):
    rows, width = tokens.shape
    lanes = 2 * mine.shape[1]
    share = (lanes - 128) // 3
    smem = pl.BlockSpec(memory_space=pltpu.SMEM)
    return pl.pallas_call(
        project_first_body,
        grid=(3,),
        in_specs=[
            smem,
            pl.BlockSpec((rows, width), lambda n: (0, 0), pipeline_mode=pl.Buffered(1)),
        ]
        + [pl.BlockSpec(memory_space=pl.ANY)] * 2,
        out_specs=[
            pl.BlockSpec((rows, share), lambda n: (0, n)),
            pl.BlockSpec((width, share), lambda n: (0, n)),
            pl.BlockSpec((width, 128), lambda n: (0, 0)),
            pl.BlockSpec((1, 3 * share), lambda n: (0, 0)),
        ],
        out_shape=[
            jax.ShapeDtypeStruct((rows, 3 * share), BF16),
            jax.ShapeDtypeStruct((width, 3 * share), BF16),
            jax.ShapeDtypeStruct((width, 128), BF16),
            jax.ShapeDtypeStruct((1, 3 * share), F32),
        ],
        scratch_shapes=[
            pltpu.VMEM((width, lanes), BF16),
            pltpu.VMEM((128, width), F32),
            pltpu.SemaphoreType.DMA((2,)),
        ],
        compiler_params=pltpu.CompilerParams(vmem_limit_bytes=VMEM_LIMIT),
        cost_estimate=SMALL_COST,
        name="project_first",
    )(where, tokens, mine, other)


def project_rest_body(weight_ref, bias_ref, *rest):
    *chunk_refs, out_ref = rest
    rows = jnp.concatenate([ref[...] for ref in chunk_refs], axis=0)
    project_block(rows, weight_ref[...], bias_ref[...], out_ref)


def project_rest(chunks, weight, bias):
    rows = sum(chunk.shape[0] for chunk in chunks)
    width, lanes = weight.shape
    share = lanes // 3
    return pl.pallas_call(
        project_rest_body,
        grid=(3,),
        in_specs=[
            pl.BlockSpec((width, share), lambda n: (0, n)),
            pl.BlockSpec((1, share), lambda n: (0, n)),
        ]
        + [
            pl.BlockSpec(chunk.shape, lambda n: (0, 0), pipeline_mode=pl.Buffered(1))
            for chunk in chunks
        ],
        out_specs=pl.BlockSpec((rows, share), lambda n: (0, n)),
        out_shape=jax.ShapeDtypeStruct((rows, lanes), BF16),
        compiler_params=pltpu.CompilerParams(vmem_limit_bytes=VMEM_LIMIT),
        cost_estimate=SMALL_COST,
        name="project_rest",
    )(weight, bias, *chunks)


def lane_halves():
    lanes = lax.broadcasted_iota(jnp.int32, (1, 128), 1)
    low = jnp.where(lanes < 64, 1.0, 0.0)
    return low.astype(BF16), (1.0 - low).astype(BF16)


def attend_body(start, q_ref, k_ref, v_ref, prior_ref, row_seg, col_seg, *rest):
    logits_ref, probs_ref, out_ref = rest[-3:]
    halves = lane_halves()
    allowed = row_seg[...] == col_seg[0]
    queries = q_ref[...]
    mixed = None
    for head, half in enumerate(halves):
        scores = matmul_nt(queries, k_ref[...] * half) + prior_ref[head].astype(F32)
        logits_ref[head] = scores.astype(BF16)
        masked = jnp.where(allowed, scores, MASK_VALUE)
        top = jnp.max(masked, axis=1, keepdims=True)
        terms = jnp.exp(masked - top)
        total = jnp.sum(terms, axis=1, keepdims=True)
        probs = (terms * (1.0 / total)).astype(BF16)
        probs_ref[head] = probs
        part = matmul(probs, v_ref[...] * half)
        mixed = part if mixed is None else mixed + part
    out_ref[...] = mixed.astype(BF16)


def attend(qkv, prior, seg_rows, seg_cols, start, first, count, earlier):
    heads, group, window = prior.shape
    pairs = heads // 2
    share = heads * 64

    def qkv_spec(part):
        return pl.BlockSpec(
            (window, 128), lambda w, p, s: (first + w, part * pairs + p)
        )

    pair_spec = pl.BlockSpec((2, window, window), lambda w, p, s: (p, s[0] + w, 0))
    in_specs = [
        qkv_spec(0),
        qkv_spec(1),
        qkv_spec(2),
        pair_spec,
        pl.BlockSpec((window, 1), lambda w, p, s: (s[0] + w, 0)),
        pl.BlockSpec((1, 1, window), lambda w, p, s: (s[0] + w, 0, 0)),
    ]
    operands = [qkv, qkv, qkv, prior, seg_rows, seg_cols]
    aliases = {}
    if earlier is not None:
        aliases = {len(operands) + 1: 0, len(operands) + 2: 1}
        operands += list(earlier)
        in_specs += [pl.BlockSpec(memory_space=pl.ANY)] * 2
    big = jax.ShapeDtypeStruct(prior.shape, BF16)
    return pl.pallas_call(
        attend_body,
        grid_spec=pltpu.PrefetchScalarGridSpec(
            num_scalar_prefetch=1,
            grid=(count, pairs),
            in_specs=in_specs,
            out_specs=[
                pair_spec,
                pair_spec,
                pl.BlockSpec((window, 128), lambda w, p, s: (w, p)),
            ],
        ),
        out_shape=[
            big,
            big,
            jax.ShapeDtypeStruct((count * window, share), BF16),
        ],
        input_output_aliases=aliases,
        compiler_params=pltpu.CompilerParams(vmem_limit_bytes=VMEM_LIMIT),
        cost_estimate=SMALL_COST,
        name="attend",
    )(start, *operands)


def attend_back_body(
    start, q_ref, k_ref, v_ref, probs_ref, grad_ref, out_ref, *rest
):
    d_scores_ref, d_qkv_ref, sums_ref = rest[-3:]
    pair = pl.program_id(1)
    pairs = pl.num_programs(1)
    halves = lane_halves()
    grads = grad_ref[...]
    product = grads.astype(F32) * out_ref[...].astype(F32)
    d_queries = d_keys = d_values = None
    for head, half in enumerate(halves):
        probs = probs_ref[head]
        inner = jnp.sum(product * half.astype(F32), axis=1, keepdims=True)
        d_probs = matmul_nt(grads, v_ref[...] * half)
        d_scores = (probs.astype(F32) * (d_probs - inner)).astype(BF16)
        d_scores_ref[head] = d_scores
        parts = (
            matmul(d_scores, k_ref[...] * half),
            matmul_tn(d_scores, q_ref[...] * half),
            matmul_tn(probs, grads * half),
        )
        if head == 0:
            d_queries, d_keys, d_values = parts
        else:
            d_queries += parts[0]
            d_keys += parts[1]
            d_values += parts[2]
    for slot, value in enumerate((d_queries * 0.125, d_keys, d_values)):
        lanes = pl.ds(pl.multiple_of((slot * pairs + pair) * 128, 128), 128)
        d_qkv_ref[:, lanes] = value.astype(BF16)
        sums_ref[:, lanes] = row_sum(value)


def attend_back(qkv, probs, grads, outs, start, first, count, earlier):
    heads, group, window = probs.shape
    pairs = heads // 2
    share = heads * 64

    def qkv_spec(part):
        return pl.BlockSpec(
            (window, 128), lambda w, p, s: (first + w, part * pairs + p)
        )

    pair_spec = pl.BlockSpec((2, window, window), lambda w, p, s: (p, s[0] + w, 0))
    row_spec = pl.BlockSpec((window, 128), lambda w, p, s: (w, p))
    in_specs = [qkv_spec(0), qkv_spec(1), qkv_spec(2), pair_spec, row_spec, row_spec]
    operands = [qkv, qkv, qkv, probs, grads, outs]
    aliases = {}
    if earlier is not None:
        aliases = {len(operands) + 1: 0}
        operands.append(earlier)
        in_specs.append(pl.BlockSpec(memory_space=pl.ANY))
    return pl.pallas_call(
        attend_back_body,
        grid_spec=pltpu.PrefetchScalarGridSpec(
            num_scalar_prefetch=1,
            grid=(count, pairs),
            in_specs=in_specs,
            out_specs=[
                pair_spec,
                pl.BlockSpec((window, 3 * share), lambda w, p, s: (w, 0)),
                pl.BlockSpec((None, 1, 3 * share), lambda w, p, s: (w, 0, 0)),
            ],
        ),
        out_shape=[
            jax.ShapeDtypeStruct(probs.shape, BF16),
            jax.ShapeDtypeStruct((count * window, 3 * share), BF16),
            jax.ShapeDtypeStruct((count, 1, 3 * share), F32),
        ],
        input_output_aliases=aliases,
        compiler_params=pltpu.CompilerParams(vmem_limit_bytes=VMEM_LIMIT),
        cost_estimate=SMALL_COST,
        name="attend_back",
    )(start, *operands)


def normed(values):
    centred = values - jnp.mean(values, axis=-1, keepdims=True)
    inv_dev = lax.rsqrt(
        jnp.mean(centred * centred, axis=-1, keepdims=True) + NORM_EPSILON
    )
    return centred * inv_dev, inv_dev


def normed_back(scaled, unit, inv_dev):
    return inv_dev * (
        scaled
        - jnp.mean(scaled, axis=-1, keepdims=True)
        - unit * jnp.mean(scaled * unit, axis=-1, keepdims=True)
    )


def row_sum(values):
    return jnp.sum(values, axis=0, keepdims=True)


def forward_back_body(
    where_ref,
    own_ref,
    received_ref,
    token_ref,
    grad_ref,
    vector_ref,
    bias_ref,
    mine_ref,
    other_ref,
    whole_outer_ref,
    *rest,
    chunk,
):
    rest = rest[-16:]
    (
        result_ref,
        attended_ref,
        hidden_ref,
        inner_ref,
        d_branch_ref,
        d_pre_ref,
        d_proj_ref,
        d_own_ref,
        d_theirs_ref,
        sums_ref,
        inner_sums_ref,
        slope_ref,
        d_heads_ref,
        wide_ref,
        outer_ref,
        sems,
    ) = rest
    core = where_ref[1] % 2
    copies = [
        pltpu.make_async_copy(mine_ref, wide_ref.at[core], sems.at[0]),
        pltpu.make_async_copy(other_ref, wide_ref.at[1 - core], sems.at[1]),
    ]
    if len(whole_outer_ref.shape) == 2:
        copies.append(pltpu.make_async_copy(whole_outer_ref, outer_ref, sems.at[2]))
    else:
        devices, sides, block = whole_outer_ref.shape[:3]
        for n in range(devices):
            for slot in range(sides):
                at_side = where_ref[0] if slot == 0 else 1 - where_ref[0]
                start = pl.multiple_of((at_side * devices + n) * block, 16)
                copies.append(
                    pltpu.make_async_copy(
                        whole_outer_ref.at[n, slot],
                        outer_ref.at[pl.ds(start, block)],
                        sems.at[2 + n * sides + slot],
                    )
                )
    for copy in copies:
        copy.start()
    first_ref, second_ref = wide_ref.at[0], wide_ref.at[1]
    share = own_ref.shape[1]
    half = outer_ref.shape[0] // 2
    side = where_ref[0]
    mine = pl.ds(pl.multiple_of(side * share, 128), share)
    theirs = pl.ds(pl.multiple_of((1 - side) * share, 128), share)
    attended_ref[:, mine] = own_ref[...]
    attended_ref[:, theirs] = received_ref[...]
    attended = attended_ref[...]
    out_bias, attn_gain, attn_shift, outer_bias, ffn_gain, ffn_shift = (
        vector_ref[n : n + 1] for n in range(6)
    )
    copies[0].wait()
    copies[1].wait()
    projected = jnp.concatenate(
        [matmul(attended, first_ref[:, half:]), matmul(attended, second_ref[:, half:])], axis=1
    )
    resid_one = token_ref[...].astype(F32) + projected + out_bias
    unit_one, inv_one = normed(resid_one)
    hidden = unit_one * attn_gain + attn_shift
    hidden_low = hidden.astype(BF16)
    hidden_ref[...] = hidden_low
    spans = [
        (ref, start, part * half + start)
        for part, ref in enumerate((first_ref, second_ref))
        for start in range(0, half, chunk)
    ]
    for copy in copies[2:]:
        copy.wait()
    resid_two = hidden + outer_bias
    for ref, start, place in spans:
        lanes = slice(place, place + chunk)
        pre_act = matmul(hidden_low, ref[:, start : start + chunk]) + bias_ref[:, lanes]
        phi = 0.5 * (1.0 + lax.erf(pre_act * INV_SQRT_TWO))
        density = INV_SQRT_TWO_PI * jnp.exp(-0.5 * pre_act * pre_act)
        inner_low = (pre_act * phi).astype(BF16)
        inner_ref[:, lanes] = inner_low
        slope_ref[:, lanes] = (phi + pre_act * density).astype(BF16)
        resid_two += matmul(inner_low, outer_ref[lanes, :])
    unit_two, inv_two = normed(resid_two)
    result_ref[...] = (unit_two * ffn_gain + ffn_shift).astype(BF16)
    cotangent = grad_ref[...].astype(F32)
    d_resid_two = normed_back(cotangent * ffn_gain, unit_two, inv_two)
    d_branch = d_resid_two.astype(BF16)
    d_branch_ref[...] = d_branch
    d_hidden = d_resid_two
    inner_sums = []
    for ref, start, place in spans:
        lanes = slice(place, place + chunk)
        d_pre = matmul_nt(d_branch, outer_ref[lanes, :]) * slope_ref[:, lanes].astype(F32)
        inner_sums.append(row_sum(d_pre))
        d_pre_low = d_pre.astype(BF16)
        d_pre_ref[:, lanes] = d_pre_low
        d_hidden += matmul_nt(d_pre_low, ref[:, start : start + chunk])
    d_resid_one = normed_back(d_hidden * attn_gain, unit_one, inv_one)
    d_proj = d_resid_one.astype(BF16)
    d_proj_ref[...] = d_proj
    d_heads_ref[...] = (
        matmul_nt(d_proj[:, :share], first_ref[:, half:])
        + matmul_nt(d_proj[:, share:], second_ref[:, half:])
    ).astype(BF16)
    d_own_ref[...] = d_heads_ref[:, mine]
    d_theirs_ref[...] = d_heads_ref[:, theirs]
    sums_ref[...] = jnp.concatenate(
        [
            row_sum(d_resid_one),
            row_sum(d_hidden * unit_one),
            row_sum(d_hidden),
            row_sum(d_resid_two),
            row_sum(cotangent * unit_two),
            row_sum(cotangent),
            jnp.zeros((2, d_resid_one.shape[1]), F32),
        ],
        axis=0,
    )
    inner_sums_ref[...] = jnp.concatenate(inner_sums, axis=1)


def forward_back(where, own, received, tokens, grads, weights, vectors, bias, at, rows, earlier):
    width = tokens.shape[1]
    share = own.shape[1]
    units = bias.shape[1]
    chunk = units // 6
    tops = [(2, width, units // 2 + share), (units, width)]
    outer_blocks = 1 if weights[2].ndim == 2 else weights[2].shape[0] * weights[2].shape[1]

    def whole(array):
        return pl.BlockSpec(array.shape, lambda i, s: (0, 0), pipeline_mode=pl.Buffered(1))

    def local(lanes):
        return pl.BlockSpec((rows, lanes), lambda i, s: (0, 0), pipeline_mode=pl.Buffered(1))

    def placed(lanes):
        return pl.BlockSpec((rows, lanes), lambda i, s: (at, 0), pipeline_mode=pl.Buffered(1))

    lanes_out = [width, width, width, units, width, units, width, share, share]
    sources = list(weights)
    kept = len(lanes_out) - 1
    aliases = {}
    if earlier is not None:
        sources += list(earlier)
        aliases = {7 + len(sources) - kept + n: n for n in range(kept)}
    return pl.pallas_call(
        functools.partial(forward_back_body, chunk=chunk),
        grid_spec=pltpu.PrefetchScalarGridSpec(
            num_scalar_prefetch=1,
            grid=(1,),
            in_specs=[
                placed(share),
                local(share),
                placed(width),
                placed(width),
                whole(vectors),
                whole(bias),
            ]
            + [pl.BlockSpec(memory_space=pl.ANY)] * len(sources),
            out_specs=[placed(lanes) for lanes in lanes_out[:kept]]
            + [local(lanes) for lanes in lanes_out[kept:]]
            + [
                pl.BlockSpec((8, width), lambda i, s: (0, 0)),
                pl.BlockSpec((1, units), lambda i, s: (0, 0)),
            ],
            scratch_shapes=[pltpu.VMEM((rows, units), BF16), pltpu.VMEM((rows, width), BF16)]
            + [pltpu.VMEM(shape, BF16) for shape in tops]
            + [pltpu.SemaphoreType.DMA((2 + outer_blocks,))],
        ),
        out_shape=[
            jax.ShapeDtypeStruct((tokens.shape[0] if n < kept else rows, lanes), BF16)
            for n, lanes in enumerate(lanes_out)
        ]
        + [
            jax.ShapeDtypeStruct((8, width), F32),
            jax.ShapeDtypeStruct((1, units), F32),
        ],
        input_output_aliases=aliases,
        compiler_params=pltpu.CompilerParams(vmem_limit_bytes=VMEM_LIMIT),
        cost_estimate=SMALL_COST,
        name="forward_back",
    )(where, own, received, tokens, grads, vectors, bias, *sources)


def shards(
    hidden_in,
    prev_logits,
    segment,
    w_query,
    b_query,
    w_key,
    w_value,
    b_value,
    w_out,
    b_out,
    gain_attn,
    shift_attn,
    w_inner,
    b_inner,
    w_outer,
    b_outer,
    gain_ffn,
    shift_ffn,
    out_grad,
):
    seq = lax.axis_index("seq").astype(jnp.int32)
    fsdp_count = lax.axis_size("fsdp")
    count = fsdp_count.bit_length() - 1
    devices = 2 * fsdp_count
    heads, group, window = prev_logits.shape
    rows, width = w_query.shape
    inner_rows = b_inner.shape[0]
    hidden_units = inner_rows * devices
    share = width // 2
    half = hidden_units // 2
    tokens = hidden_in.shape[0]
    own_windows = tokens // window
    seq_hop = ("seq", 1)
    far, near, core = plan_hops(count)
    done = len(far)

    vectors = (b_query, b_value, b_out, gain_attn, shift_attn, b_outer, gain_ffn, shift_ffn, b_inner)
    where = jnp.stack([seq, lax.axis_index("fsdp").astype(jnp.int32)])
    other_inner, other_out = swap(w_inner, far[0]), swap(w_out, far[0])
    unit, unit_core, unit_seq, unit_both = pack(where, w_query, w_key, w_value, vectors)
    parts = 4
    part_rows = tokens // parts
    others = []

    def next_part(*earlier):
        part = hidden_in[len(others) * part_rows : (len(others) + 1) * part_rows]
        others.append(swap(after(part, *earlier), seq_hop))

    def quad(flip_seq, flip_core):
        def place(n, at_seq, at):
            one, two = bit_of(seq_hop, at_seq, at), bit_of(core, at_seq, at)
            return 2 * (1 - one if flip_seq else one) + (1 - two if flip_core else two)

        return place

    def both_flipped(at_seq, at):
        return at_seq ^ 1, at ^ 1

    def pairs_of(blocks):
        return blocks.reshape(-1, 2 * blocks.shape[1], blocks.shape[2])

    def hopped(blocks, hop, inner):
        return joined(blocks, swap(blocks, hop), hop, inner)

    (unit,) = merge(
        where,
        [
            (after(unit, other_inner, other_out)[None], quad(False, False)),
            (swap(unit_seq, seq_hop)[None], quad(True, False)),
            (swap(unit_core, core)[None], quad(False, True)),
            (trade(unit_both, both_flipped)[None], quad(True, True)),
        ],
    )
    unit = pairs_of(unit)
    wide, wide_core = cut(where, after(w_inner, unit), w_out, other_inner, other_out, far[0])
    outer_other = swap(after(w_outer, unit), seq_hop)
    next_part(unit)
    wide_item = joined(after(wide, others[0]), swap(wide_core, core), core, 1)
    if done == 2:
        def flipped(one, two):
            def place(n, at_seq, at):
                bits = bit_of(far[0], at_seq, at), bit_of(far[1], at_seq, at)
                return 4 * n + 2 * (1 - bits[0] if one else bits[0]) + (1 - bits[1] if two else bits[1])

            return place

        unit_item = [(unit, flipped(False, False))]
        for one, two in ((True, False), (False, True), (True, True)):
            mask = one * far[0][1] + two * far[1][1]
            unit_item.append((swap(unit, ("fsdp", mask)), flipped(one, two)))
        unit, wide = merge(where, unit_item, wide_item)
    else:
        unit, wide = merge(where, hopped(unit, far[0], 1), wide_item)
        for hop in far[1:]:
            (unit,) = merge(where, hopped(unit, hop, 1))
    outer = jnp.stack([after(w_outer, unit), outer_other])
    outer = lax.all_gather(outer, "fsdp", axis=0, tiled=False)
    if inner_rows % 16 != 0:
        outer = jnp.where(seq == 0, outer, outer[:, ::-1])
        outer = outer.transpose(1, 0, 2, 3).reshape(hidden_units, width)
    wide = pairs_of(wide)
    for hop in far[1:-1]:
        (wide,) = merge(where, hopped(wide, hop, 1))
    next_part(unit)
    wide_item = hopped(after(wide, unit), far[-1], 1)
    wide_item[0] = (after(wide, others[1]), wide_item[0][1])
    unit, wide = merge(where, hopped(unit, near, 1), wide_item)
    next_part(unit)
    next_part(unit)
    unit = unit.reshape(width, unit.shape[-1])
    unit_other = swap(unit, core)

    def near_or_seq(at_seq, at):
        return across(near if at % 2 == 0 else seq_hop)(at_seq, at)

    def seq_or_near(at_seq, at):
        return across(seq_hop if at % 2 == 0 else near)(at_seq, at)

    wide_other = trade(wide, near_or_seq)
    own_qkv, qkv_weight, small, qkv_bias = project_first(where, hidden_in, unit, unit_other)

    seg_rows = segment[:, None]
    seg_cols = segment.reshape(group // window, 1, window)
    own_start = (seq * own_windows).reshape(1)
    other_start = ((1 - seq) * own_windows).reshape(1)

    logits, probs, own_out = attend(
        own_qkv, prev_logits, seg_rows, seg_cols, own_start, 0, own_windows, None
    )
    blocks = wide.shape[0]
    (wide,) = merge(
        where,
        joined_by_core(
            after(wide, own_out, others[-2], others[-1]), wide_other, core, (near, 1), (seq_hop, blocks)
        ),
    )
    wide_other = trade(wide, seq_or_near)
    other_qkv = project_rest(after(tuple(others), wide), qkv_weight, qkv_bias)
    other_out = []
    received = []
    for w in range(own_windows):
        logits, probs, out = attend(
            other_qkv, prev_logits, seg_rows, seg_cols, other_start + w, w, 1, (logits, probs)
        )
        other_out.append(out)
        if w == 0:
            blocks = wide.shape[0]
            (wide,) = merge(
                where,
                joined_by_core(after(wide, out), wide_other, core, (seq_hop, blocks), (near, 1)),
            )
            out = after(out, wide)
            wide = wide.reshape(width, wide.shape[-1])
            wide_other = swap(wide, core)
            other_qkv = after(other_qkv, wide)
        received.append(swap(out, seq_hop))
    weights = (wide, wide_other, outer)
    small = small.astype(F32)
    layer_vectors = jnp.concatenate([small[:, 2:8].T, jnp.zeros((2, width), F32)], axis=0)
    inner_bias = small[:, 8 : 8 + hidden_units // width].reshape(1, hidden_units)

    full = None
    d_others = []
    sums, inner_sums = 0.0, 0.0
    for w in range(own_windows):
        outs = forward_back(
            where,
            own_out,
            received[w],
            hidden_in,
            out_grad,
            weights,
            layer_vectors,
            inner_bias,
            w,
            window,
            full,
        )
        full = outs[:8]
        d_others.append(swap(outs[8], seq_hop))
        sums += outs[9]
        inner_sums += outs[10]
    hidden_out, attended, hidden, inner, d_branch, d_pre, d_proj, d_own = full

    class Reduction:
        def __init__(self, value, hops):
            self.value, self.hops = value, list(hops)
            self.send()

        def send(self):
            if self.hops:
                hop, place = self.hops.pop(0)
                away, self.keep = split(self.value, hop, place)
                self.other = swap(away, hop)

        def add(self, latest):
            self.value = total(after(self.keep, latest), self.other)
            self.send()
            return self.value

    grid = (2,) * (count + 1)
    outer_hops = [(core, done + 2), (near, done + 1)]
    outer_hops += [(far[n], n + 1) for n in reversed(range(done))] + [(seq_hop, 0)]
    inner_hops = [(core, done + 2), (seq_hop, 0), (near, done)]
    inner_hops += [(far[n], n) for n in reversed(range(done))]
    tail_hops = [(core, done + 2), (near, done + 1)]
    tail_hops += [(far[n], n + 1) for n in reversed(range(done))]

    inner, attended = after((inner, attended), d_others[0])
    g_outer = matmul_tn(inner, d_branch).astype(BF16)
    g_out = matmul_tn(attended, d_proj).astype(BF16)
    outer_grad = jnp.concatenate(
        [
            g_outer.reshape(grid + (inner_rows, width)),
            g_out.reshape(grid + (rows, width)),
        ],
        axis=-2,
    )
    outer_sum = Reduction(outer_grad, outer_hops)
    g_inner = matmul_tn(after(hidden, outer_grad), d_pre).astype(BF16)
    inner_sum = Reduction(g_inner.reshape(grid + (rows, hidden_units)), inner_hops)
    latest = outer_sum.add(g_inner)
    latest = inner_sum.add(latest)

    d_scores = None
    input_received = []
    other_qkv = after(other_qkv, latest)
    g_qkv, qkv_sum = 0.0, 0.0
    for w in range(own_windows):
        d_scores, d_qkv, column_sums = attend_back(
            other_qkv, probs, d_others[w], other_out[w], other_start + w, w, 1, d_scores
        )
        input_received.append(swap(matmul_nt(d_qkv, qkv_weight).astype(BF16), seq_hop))
        per_window = parts // own_windows
        rows_of = jnp.concatenate(others[w * per_window : (w + 1) * per_window], axis=0)
        g_qkv += matmul_tn(rows_of, d_qkv)
        qkv_sum += column_sums[0]
    latest = outer_sum.add(d_qkv)
    latest = inner_sum.add(latest)
    own_qkv = after(own_qkv, latest)
    d_scores, own_d_qkv, column_sums = attend_back(
        own_qkv, probs, d_own, own_out, own_start, 0, own_windows, d_scores
    )
    own_d_qkv = after(own_d_qkv, outer_sum.other, inner_sum.other)
    g_qkv += matmul_tn(hidden_in, own_d_qkv)
    qkv_sum = (qkv_sum + jnp.sum(column_sums, axis=0)).reshape(-1)

    def both_sides(part):
        blank = jnp.zeros_like(part)
        return jnp.where(
            seq == 0, jnp.concatenate([part, blank]), jnp.concatenate([blank, part])
        )

    small_grads = jnp.concatenate(
        [
            both_sides(qkv_sum[:share])[:, None],
            both_sides(qkv_sum[2 * share :])[:, None],
            sums[:6].T,
            inner_sums.reshape(width, hidden_units // width),
        ],
        axis=1,
    )
    lanes = small_grads.shape[1]
    tail = jnp.concatenate(
        [g_qkv.astype(BF16), jnp.pad(small_grads, ((0, 0), (0, 128 - lanes))).astype(BF16)], axis=1
    ).reshape(grid + (rows, 3 * share + 128))
    direct = done == 2
    tail_sum = Reduction(tail, tail_hops[:2] if direct else tail_hops)
    latest = outer_sum.add(tail)
    latest = tail_sum.add(latest)
    latest = inner_sum.add(latest)
    latest = outer_sum.add(latest)
    latest = tail_sum.add(latest)
    if direct:
        bits = my_bit(far[0]), my_bit(far[1])

        def block(one, two):
            at = (1 - bits[0] if one else bits[0], 1 - bits[1] if two else bits[1])
            blocks = tail_sum.value.reshape((2, 4) + tail_sum.value.shape[-2:])
            return lax.dynamic_index_in_dim(blocks, 2 * at[0] + at[1], 1, keepdims=False)

        arrivals = [
            swap(block(one, two), ("fsdp", one * far[0][1] + two * far[1][1]))
            for one, two in ((True, False), (False, True), (True, True))
        ]
        keep = block(False, False)
    latest = inner_sum.add(latest)
    latest = outer_sum.add(latest)
    if direct:
        terms = [after(keep, latest)] + arrivals
        tail = functools.reduce(jnp.add, [term.astype(F32) for term in terms]).astype(BF16)
        latest = tail
    while not direct and len(tail_sum.value.shape) > 3:
        latest = tail_sum.add(latest)
        tail = latest
    while len(outer_sum.value.shape) > 2:
        latest = outer_sum.add(latest)
    while len(inner_sum.value.shape) > 2:
        latest = inner_sum.add(latest)
    outer_grad, inner_grad = outer_sum.value, inner_sum.value
    send, own_tail = split(tail, seq_hop, 0)
    other_tail = swap(send, seq_hop)
    grads = unpack(own_tail[:, 3 * share :], other_tail[:, 3 * share :], inner_rows)

    def weight_part(slot):
        at = slice(slot * share, (slot + 1) * share)
        return jnp.where(
            seq == 0,
            jnp.concatenate([own_tail[:, at], other_tail[:, at]], axis=1),
            jnp.concatenate([other_tail[:, at], own_tail[:, at]], axis=1),
        ).astype(F32)

    input_grad = (
        d_proj.astype(F32)
        + matmul_nt(own_d_qkv, qkv_weight)
        + jnp.concatenate(input_received, axis=0).astype(F32)
    ).astype(BF16)
    return (
        hidden_out,
        logits,
        input_grad,
        d_scores,
        weight_part(0),
        grads[0],
        weight_part(1),
        weight_part(2),
        grads[1],
        outer_grad[inner_rows:].astype(F32),
        grads[2],
        grads[3],
        grads[4],
        inner_grad.astype(F32),
        grads[8],
        outer_grad[:inner_rows].astype(F32),
        grads[5],
        grads[6],
        grads[7],
    )


def solution(mesh):
    in_specs = (
        P(("fsdp", "seq"), None),
        P("seq", "fsdp", None),
        P("fsdp"),
        P(("seq", "fsdp"), None),
        P(("seq", "fsdp")),
        P(("seq", "fsdp"), None),
        P(("seq", "fsdp"), None),
        P(("seq", "fsdp")),
        P(("seq", "fsdp"), None),
        P(("seq", "fsdp")),
        P(("seq", "fsdp")),
        P(("seq", "fsdp")),
        P(("seq", "fsdp"), None),
        P(("seq", "fsdp")),
        P(("seq", "fsdp"), None),
        P(("seq", "fsdp")),
        P(("seq", "fsdp")),
        P(("seq", "fsdp")),
        P(("fsdp", "seq"), None),
    )
    out_specs = (
        P(("fsdp", "seq"), None),
        P("seq", "fsdp", None),
        P(("fsdp", "seq"), None),
        P("seq", "fsdp", None),
        P(("seq", "fsdp"), None),
        P(("seq", "fsdp")),
        P(("seq", "fsdp"), None),
        P(("seq", "fsdp"), None),
        P(("seq", "fsdp")),
        P(("seq", "fsdp"), None),
        P(("seq", "fsdp")),
        P(("seq", "fsdp")),
        P(("seq", "fsdp")),
        P(("seq", "fsdp"), None),
        P(("seq", "fsdp")),
        P(("seq", "fsdp"), None),
        P(("seq", "fsdp")),
        P(("seq", "fsdp")),
        P(("seq", "fsdp")),
    )
    return jax.shard_map(shards, mesh=mesh, in_specs=in_specs, out_specs=out_specs, check_vma=False)
```

```python
import functools
import math

import jax
import jax.numpy as jnp
from jax import lax
from jax.experimental import pallas as pl
from jax.experimental.pallas import tpu as pltpu
from jax.sharding import PartitionSpec as P

NORM_EPSILON = 1e-06
MASK_VALUE = -1e30
INV_SQRT_TWO = 0.7071067811865476
INV_SQRT_TWO_PI = 0.3989422804014327
VMEM_LIMIT = 56 * 1024 * 1024
BF16 = jnp.bfloat16
F32 = jnp.float32
SMALL_COST = pl.CostEstimate(flops=1024, transcendentals=0, bytes_accessed=1024)


def matmul(left_op, right_op):
    return jnp.dot(left_op, right_op, preferred_element_type=F32)


def matmul_tn(left_op, right_op):
    return lax.dot_general(
        left_op, right_op, (((0,), (0,)), ((), ())), preferred_element_type=F32
    )


def matmul_nt(left_op, right_op):
    return lax.dot_general(
        left_op, right_op, (((1,), (1,)), ((), ())), preferred_element_type=F32
    )


def column_sum(values):
    return jnp.sum(values.astype(F32), axis=0)


BOTH = ("seq", "fsdp")


def trade(value, partner):
    seq_count, fsdp_count = lax.axis_size("seq"), lax.axis_size("fsdp")
    pairs = []
    for seq in range(seq_count):
        for at in range(fsdp_count):
            to_seq, to = partner(seq, at)
            pairs.append((seq * fsdp_count + at, to_seq * fsdp_count + to))
    return lax.ppermute(value, BOTH, pairs)


def across(hop):
    axis, mask = hop
    if axis == "seq":
        return lambda seq, at: (seq ^ mask, at)
    return lambda seq, at: (seq, at ^ mask)


def swap(value, hop):
    return trade(value, across(hop))


def bit_of(hop, seq, at):
    axis, mask = hop
    return (seq if axis == "seq" else at // mask) % 2


def my_bit(hop):
    at = lax.axis_index(hop[0]).astype(jnp.int32)
    return bit_of(hop, at, at)


def after(value, *others):
    return lax.optimization_barrier((value,) + others)[0]


def merge_body(where_ref, *refs, plans):
    seq, at = where_ref[0], where_ref[1]
    outs = refs[sum(len(plan) for plan in plans) :]
    for plan, out_ref in zip(plans, outs):
        for target in plan:
            source, refs = refs[0], refs[1:]
            for n in range(source.shape[0]):
                out_ref[target(n, seq, at)] = source[n]


def merge(where, *items):
    sources = [blocks for item in items for blocks, _ in item]
    plans = [[target for _, target in item] for item in items]
    outs = []
    for item in items:
        total_blocks = sum(blocks.shape[0] for blocks, _ in item)
        outs.append(jax.ShapeDtypeStruct((total_blocks,) + item[0][0].shape[1:], BF16))
    return pl.pallas_call(
        functools.partial(merge_body, plans=plans),
        in_specs=[pl.BlockSpec(memory_space=pltpu.SMEM)]
        + [pl.BlockSpec(memory_space=pltpu.VMEM)] * len(sources),
        out_specs=[pl.BlockSpec(memory_space=pltpu.VMEM)] * len(outs),
        out_shape=outs,
        compiler_params=pltpu.CompilerParams(vmem_limit_bytes=VMEM_LIMIT),
        cost_estimate=SMALL_COST,
        name="merge",
    )(where, *sources)


def spread(hop, inner):
    def target(flip):
        def place(n, seq, at):
            bit = bit_of(hop, seq, at)
            bit = 1 - bit if flip else bit
            return (n // inner) * 2 * inner + n % inner + bit * inner

        return place

    return target(False), target(True)


def joined(mine, other, hop, inner):
    own_place, other_place = spread(hop, inner)
    return [(mine, own_place), (other, other_place)]


def by_core(core, zero, one):
    def place(n, seq, at):
        bit = bit_of(core, seq, at)
        return (1 - bit) * zero(n, seq, at) + bit * one(n, seq, at)

    return place


def joined_by_core(mine, other, core, zero, one):
    zero_places, one_places = spread(*zero), spread(*one)
    return [
        (mine, by_core(core, zero_places[0], one_places[0])),
        (other, by_core(core, zero_places[1], one_places[1])),
    ]


def split(value, hop, place):
    bit = my_bit(hop)
    return (
        lax.dynamic_index_in_dim(value, 1 - bit, place, keepdims=False),
        lax.dynamic_index_in_dim(value, bit, place, keepdims=False),
    )


def total(one, two):
    return (one.astype(F32) + two.astype(F32)).astype(BF16)


def plan_hops(count):
    bits = [("fsdp", 1 << n) for n in range(count)]
    return list(reversed(bits[2:])), bits[1], bits[0]


def place_of(rows, inner_rows):
    count = 8 * rows + inner_rows
    per_row = inner_rows // rows
    entry = lax.broadcasted_iota(jnp.int32, (1, count), 1)
    row, lane = entry * 0, entry * 0
    for slot in range(8):
        inside = (entry >= slot * rows) & (entry < (slot + 1) * rows)
        row = jnp.where(inside, entry - slot * rows, row)
        lane = jnp.where(inside, slot, lane)
    for unit in range(rows):
        low = 8 * rows + unit * per_row
        inside = (entry >= low) & (entry < low + per_row)
        row = jnp.where(inside, unit, row)
        lane = jnp.where(inside, 8 + entry - low, lane)
    return row, lane


def pack_body(where_ref, q_ref, k_ref, v_ref, *rest):
    small_refs = rest[:9]
    quarter_refs = (rest[9:11], rest[11:13])
    line_ref, whole_ref = rest[13:]
    rows, width = q_ref.shape
    share = width // 2
    lanes = quarter_refs[0][0].shape[1]
    inner_rows = small_refs[8].shape[1]
    side, core = where_ref[0], where_ref[1] % 2
    for slot, ref in enumerate(small_refs):
        line_ref[0:1, slot * rows : slot * rows + ref.shape[1]] = ref[...].astype(F32)
    row, lane = place_of(rows, inner_rows)
    count = 8 * rows + inner_rows
    spread_line = jnp.where(
        lax.broadcasted_iota(jnp.int32, (rows, count), 0) == row, line_ref[0:1, :count], 0.0
    )
    pick = jnp.where(lax.broadcasted_iota(jnp.int32, (128, count), 0) == lane, 1.0, 0.0)
    extra = matmul_nt(spread_line.astype(BF16), pick.astype(BF16)).astype(BF16)
    for turn in range(2):
        start = pl.multiple_of(((side + turn) % 2) * share, 128)
        for slot, ref in enumerate((q_ref, k_ref, v_ref)):
            whole_ref[:, slot * share : (slot + 1) * share] = ref[:, pl.ds(start, share)]
        whole_ref[:, 3 * share :] = extra
        for other in range(2):
            at = pl.multiple_of(((core + other) % 2) * lanes, 128)
            quarter_refs[turn][other][...] = whole_ref[:, pl.ds(at, lanes)]


def pack(where, w_query, w_key, w_value, vectors):
    rows, width = w_query.shape
    lines = [v.reshape(1, -1) for v in vectors]
    count = sum(line.shape[1] for line in lines)
    lanes = 3 * width // 2 + 128
    quarter = jax.ShapeDtypeStruct((rows, lanes // 2), BF16)
    return pl.pallas_call(
        pack_body,
        in_specs=[pl.BlockSpec(memory_space=pltpu.SMEM)]
        + [pl.BlockSpec(memory_space=pltpu.VMEM)] * (3 + len(lines)),
        out_specs=[pl.BlockSpec(memory_space=pltpu.VMEM)] * 4,
        out_shape=[quarter] * 4,
        scratch_shapes=[
            pltpu.VMEM((8, -(-count // 128) * 128), F32),
            pltpu.VMEM((rows, lanes), BF16),
        ],
        cost_estimate=SMALL_COST,
        name="pack",
    )(where, w_query, w_key, w_value, *lines)


def cut_body(where_ref, inner_ref, out_ref, other_inner_ref, other_out_ref, *half_refs, hop):
    half, share = inner_ref.shape[1] // 2, out_ref.shape[1] // 2
    core = where_ref[1] % 2
    bit = bit_of(hop, where_ref[0], where_ref[1])
    for turn, ref in enumerate(half_refs):
        part = (core + turn) % 2
        inner_lanes = pl.ds(pl.multiple_of(part * half, 128), half)
        out_lanes = pl.ds(pl.multiple_of(part * share, 128), share)
        for place, inner, out in (
            (bit, inner_ref, out_ref),
            (1 - bit, other_inner_ref, other_out_ref),
        ):
            ref[place, :, :half] = inner[:, inner_lanes]
            ref[place, :, half:] = out[:, out_lanes]


def cut(where, inner, out, other_inner, other_out, hop):
    rows = inner.shape[0]
    half = jax.ShapeDtypeStruct((2, rows, (inner.shape[1] + out.shape[1]) // 2), BF16)
    return pl.pallas_call(
        functools.partial(cut_body, hop=hop),
        in_specs=[pl.BlockSpec(memory_space=pltpu.SMEM)]
        + [pl.BlockSpec(memory_space=pltpu.VMEM)] * 4,
        out_specs=[pl.BlockSpec(memory_space=pltpu.VMEM)] * 2,
        out_shape=[half, half],
        cost_estimate=SMALL_COST,
        name="cut",
    )(where, inner, out, other_inner, other_out)


def unpack_body(first_ref, second_ref, *rest):
    out_refs = rest[:9]
    rows = first_ref.shape[0]
    inner_rows = out_refs[8].shape[1]
    count = 8 * rows + inner_rows
    row, lane = place_of(rows, inner_rows)
    pick = jnp.where(lax.broadcasted_iota(jnp.int32, (128, count), 0) == lane, 1.0, 0.0)
    pick = pick.astype(BF16)
    spread = matmul(first_ref[...], pick) + matmul(second_ref[...], pick)
    inside = lax.broadcasted_iota(jnp.int32, (rows, count), 0) == row
    line = jnp.sum(jnp.where(inside, spread, 0.0), axis=0, keepdims=True)
    for slot, ref in enumerate(out_refs):
        ref[...] = line[:, slot * rows : slot * rows + ref.shape[1]]


def unpack(first, second, inner_rows):
    rows = first.shape[0]
    outs = pl.pallas_call(
        unpack_body,
        in_specs=[pl.BlockSpec(memory_space=pltpu.VMEM)] * 2,
        out_specs=[pl.BlockSpec(memory_space=pltpu.VMEM)] * 9,
        out_shape=[jax.ShapeDtypeStruct((1, rows), F32)] * 8
        + [jax.ShapeDtypeStruct((1, inner_rows), F32)],
        name="unpack",
    )(first, second)
    return [out.reshape(-1) for out in outs]


def project_block(rows, weight, bias, out_ref):
    scale = jnp.where(pl.program_id(0) == 0, 0.125, 1.0)
    out_ref[...] = ((matmul(rows, weight) + bias).astype(BF16).astype(F32) * scale).astype(BF16)


def copies_of(pieces, target_of, where_ref, sems):
    seq, at = where_ref[0], where_ref[1]
    copies = []
    for source, place, flip in pieces:
        half = (at + flip) % 2
        if place is None:
            copies.append((source, target_of(half, None)))
            continue
        for n in range(source.shape[0]):
            block = source.shape[1]
            start = pl.multiple_of(place(n, seq, at ^ flip) * block, 16)
            copies.append((source.at[n], target_of(half, pl.ds(start, block))))
    copies = [
        pltpu.make_async_copy(source, target, sems.at[n])
        for n, (source, target) in enumerate(copies)
    ]
    for copy in copies:
        copy.start()
    return copies


def copy_count(pieces):
    return sum(1 if place is None else source.shape[0] for source, place, _ in pieces)


def places_of(pieces):
    return [(place, flip) for _, place, flip in pieces]


def project_first_body(where_ref, token_ref, *rest, places):
    sources, rest = rest[: len(places)], rest[len(places) :]
    out_ref, weight_ref, small_ref, bias_ref, whole_ref, turned_ref, sems = rest
    half = whole_ref.shape[1] // 2
    share = weight_ref.shape[1]
    step = pl.program_id(0)

    @pl.when(step == 0)
    def _():
        def target_of(part, rows):
            lanes = pl.ds(pl.multiple_of(part * half, 128), half)
            return whole_ref.at[:, lanes] if rows is None else whole_ref.at[rows, lanes]

        pieces = [(source,) + place for source, place in zip(sources, places)]
        for copy in copies_of(pieces, target_of, where_ref, sems):
            copy.wait()
        small = whole_ref[:, 3 * share :]
        small_ref[...] = small
        turned_ref[...] = small.astype(F32).T
        mine = pl.ds(pl.multiple_of(where_ref[0] * share, 128), share)
        bias_ref[:, :share] = turned_ref[0:1, mine]
        bias_ref[:, share : 2 * share] = jnp.zeros((1, share), F32)
        bias_ref[:, 2 * share :] = turned_ref[1:2, mine]

    lanes = pl.ds(pl.multiple_of(step * share, 128), share)
    weight = whole_ref[:, lanes]
    weight_ref[...] = weight
    project_block(token_ref[...], weight, bias_ref[:, lanes], out_ref)


def project_first(where, tokens, pieces):
    rows, width = tokens.shape
    lanes = 2 * pieces[0][0].shape[-1]
    share = (lanes - 128) // 3
    smem = pl.BlockSpec(memory_space=pltpu.SMEM)
    return pl.pallas_call(
        functools.partial(project_first_body, places=places_of(pieces)),
        grid=(3,),
        in_specs=[
            smem,
            pl.BlockSpec((rows, width), lambda n: (0, 0), pipeline_mode=pl.Buffered(1)),
        ]
        + [pl.BlockSpec(memory_space=pl.ANY)] * len(pieces),
        out_specs=[
            pl.BlockSpec((rows, share), lambda n: (0, n)),
            pl.BlockSpec((width, share), lambda n: (0, n)),
            pl.BlockSpec((width, 128), lambda n: (0, 0)),
            pl.BlockSpec((1, 3 * share), lambda n: (0, 0)),
        ],
        out_shape=[
            jax.ShapeDtypeStruct((rows, 3 * share), BF16),
            jax.ShapeDtypeStruct((width, 3 * share), BF16),
            jax.ShapeDtypeStruct((width, 128), BF16),
            jax.ShapeDtypeStruct((1, 3 * share), F32),
        ],
        scratch_shapes=[
            pltpu.VMEM((width, lanes), BF16),
            pltpu.VMEM((128, width), F32),
            pltpu.SemaphoreType.DMA((copy_count(pieces),)),
        ],
        compiler_params=pltpu.CompilerParams(vmem_limit_bytes=VMEM_LIMIT),
        cost_estimate=SMALL_COST,
        name="project_first",
    )(where, tokens, *(source for source, _, _ in pieces))


def project_rest_body(weight_ref, bias_ref, *rest):
    *chunk_refs, out_ref, rows_ref = rest

    @pl.when(pl.program_id(0) == 0)
    def _():
        at = 0
        for ref in chunk_refs:
            rows_ref[at : at + ref.shape[0], :] = ref[...]
            at += ref.shape[0]

    project_block(rows_ref[...], weight_ref[...], bias_ref[...], out_ref)


def project_rest(chunks, weight, bias):
    rows = sum(chunk.shape[0] for chunk in chunks)
    width, lanes = weight.shape
    share = lanes // 3
    return pl.pallas_call(
        project_rest_body,
        grid=(3,),
        in_specs=[
            pl.BlockSpec((width, share), lambda n: (0, n)),
            pl.BlockSpec((1, share), lambda n: (0, n)),
        ]
        + [
            pl.BlockSpec(chunk.shape, lambda n: (0, 0), pipeline_mode=pl.Buffered(1))
            for chunk in chunks
        ],
        out_specs=[
            pl.BlockSpec((rows, share), lambda n: (0, n)),
            pl.BlockSpec((rows, width), lambda n: (0, 0)),
        ],
        out_shape=[
            jax.ShapeDtypeStruct((rows, lanes), BF16),
            jax.ShapeDtypeStruct((rows, width), BF16),
        ],
        compiler_params=pltpu.CompilerParams(vmem_limit_bytes=VMEM_LIMIT),
        cost_estimate=SMALL_COST,
        name="project_rest",
    )(weight, bias, *chunks)


def lane_halves():
    lanes = lax.broadcasted_iota(jnp.int32, (1, 128), 1)
    low = jnp.where(lanes < 64, 1.0, 0.0)
    return low.astype(BF16), (1.0 - low).astype(BF16)


def attend_body(start, q_ref, k_ref, v_ref, prior_ref, row_seg, col_seg, *rest):
    logits_ref, probs_ref, out_ref = rest[-3:]
    halves = lane_halves()
    allowed = row_seg[...] == col_seg[0]
    queries = q_ref[...]
    mixed = None
    for head, half in enumerate(halves):
        scores = matmul_nt(queries, k_ref[...] * half) + prior_ref[head].astype(F32)
        logits_ref[head] = scores.astype(BF16)
        masked = jnp.where(allowed, scores, MASK_VALUE)
        top = jnp.max(masked, axis=1, keepdims=True)
        terms = jnp.exp(masked - top)
        total = jnp.sum(terms, axis=1, keepdims=True)
        probs = (terms * (1.0 / total)).astype(BF16)
        probs_ref[head] = probs
        part = matmul(probs, v_ref[...] * half)
        mixed = part if mixed is None else mixed + part
    out_ref[...] = mixed.astype(BF16)


def attend(qkv, prior, seg_rows, seg_cols, start, first, count, earlier):
    heads, group, window = prior.shape
    pairs = heads // 2
    share = heads * 64

    def qkv_spec(part):
        return pl.BlockSpec(
            (window, 128), lambda w, p, s: (first + w, part * pairs + p)
        )

    pair_spec = pl.BlockSpec((2, window, window), lambda w, p, s: (p, s[0] + w, 0))
    in_specs = [
        qkv_spec(0),
        qkv_spec(1),
        qkv_spec(2),
        pair_spec,
        pl.BlockSpec((window, 1), lambda w, p, s: (s[0] + w, 0)),
        pl.BlockSpec((1, 1, window), lambda w, p, s: (s[0] + w, 0, 0)),
    ]
    operands = [qkv, qkv, qkv, prior, seg_rows, seg_cols]
    aliases = {}
    if earlier is not None:
        aliases = {len(operands) + 1: 0, len(operands) + 2: 1}
        operands += list(earlier)
        in_specs += [pl.BlockSpec(memory_space=pl.ANY)] * 2
    big = jax.ShapeDtypeStruct(prior.shape, BF16)
    return pl.pallas_call(
        attend_body,
        grid_spec=pltpu.PrefetchScalarGridSpec(
            num_scalar_prefetch=1,
            grid=(count, pairs),
            in_specs=in_specs,
            out_specs=[
                pair_spec,
                pair_spec,
                pl.BlockSpec((window, 128), lambda w, p, s: (w, p)),
            ],
        ),
        out_shape=[
            big,
            big,
            jax.ShapeDtypeStruct((count * window, share), BF16),
        ],
        input_output_aliases=aliases,
        compiler_params=pltpu.CompilerParams(vmem_limit_bytes=VMEM_LIMIT),
        cost_estimate=SMALL_COST,
        name="attend",
    )(start, *operands)


def attend_back_body(
    start, q_ref, k_ref, v_ref, probs_ref, grad_ref, out_ref, *rest
):
    d_scores_ref, d_qkv_ref, sums_ref = rest[-3:]
    pair = pl.program_id(1)
    pairs = pl.num_programs(1)
    halves = lane_halves()
    grads = grad_ref[...]
    product = grads.astype(F32) * out_ref[...].astype(F32)
    d_queries = d_keys = d_values = None
    for head, half in enumerate(halves):
        probs = probs_ref[head]
        inner = jnp.sum(product * half.astype(F32), axis=1, keepdims=True)
        d_probs = matmul_nt(grads, v_ref[...] * half)
        d_scores = (probs.astype(F32) * (d_probs - inner)).astype(BF16)
        d_scores_ref[head] = d_scores
        parts = (
            matmul(d_scores, k_ref[...] * half),
            matmul_tn(d_scores, q_ref[...] * half),
            matmul_tn(probs, grads * half),
        )
        if head == 0:
            d_queries, d_keys, d_values = parts
        else:
            d_queries += parts[0]
            d_keys += parts[1]
            d_values += parts[2]
    for slot, value in enumerate((d_queries * 0.125, d_keys, d_values)):
        lanes = pl.ds(pl.multiple_of((slot * pairs + pair) * 128, 128), 128)
        d_qkv_ref[:, lanes] = value.astype(BF16)
        sums_ref[:, lanes] = row_sum(value)


def attend_back(qkv, probs, grads, outs, start, first, count, earlier):
    heads, group, window = probs.shape
    pairs = heads // 2
    share = heads * 64

    def qkv_spec(part):
        return pl.BlockSpec(
            (window, 128), lambda w, p, s: (first + w, part * pairs + p)
        )

    pair_spec = pl.BlockSpec((2, window, window), lambda w, p, s: (p, s[0] + w, 0))
    row_spec = pl.BlockSpec((window, 128), lambda w, p, s: (w, p))
    in_specs = [qkv_spec(0), qkv_spec(1), qkv_spec(2), pair_spec, row_spec, row_spec]
    operands = [qkv, qkv, qkv, probs, grads, outs]
    aliases = {}
    if earlier is not None:
        aliases = {len(operands) + 1: 0}
        operands.append(earlier)
        in_specs.append(pl.BlockSpec(memory_space=pl.ANY))
    return pl.pallas_call(
        attend_back_body,
        grid_spec=pltpu.PrefetchScalarGridSpec(
            num_scalar_prefetch=1,
            grid=(count, pairs),
            in_specs=in_specs,
            out_specs=[
                pair_spec,
                pl.BlockSpec((window, 3 * share), lambda w, p, s: (w, 0)),
                pl.BlockSpec((None, 1, 3 * share), lambda w, p, s: (w, 0, 0)),
            ],
        ),
        out_shape=[
            jax.ShapeDtypeStruct(probs.shape, BF16),
            jax.ShapeDtypeStruct((count * window, 3 * share), BF16),
            jax.ShapeDtypeStruct((count, 1, 3 * share), F32),
        ],
        input_output_aliases=aliases,
        compiler_params=pltpu.CompilerParams(vmem_limit_bytes=VMEM_LIMIT),
        cost_estimate=SMALL_COST,
        name="attend_back",
    )(start, *operands)


def normed(values):
    centred = values - jnp.mean(values, axis=-1, keepdims=True)
    inv_dev = lax.rsqrt(
        jnp.mean(centred * centred, axis=-1, keepdims=True) + NORM_EPSILON
    )
    return centred * inv_dev, inv_dev


def normed_back(scaled, unit, inv_dev):
    return inv_dev * (
        scaled
        - jnp.mean(scaled, axis=-1, keepdims=True)
        - unit * jnp.mean(scaled * unit, axis=-1, keepdims=True)
    )


def row_sum(values):
    return jnp.sum(values, axis=0, keepdims=True)


def forward_back_body(
    where_ref,
    own_ref,
    received_ref,
    token_ref,
    grad_ref,
    vector_ref,
    bias_ref,
    *rest,
    chunk,
    places,
):
    sources, whole_outer_ref = rest[: len(places)], rest[len(places)]
    rest = rest[-17:]
    (
        result_ref,
        attended_ref,
        hidden_ref,
        inner_ref,
        d_branch_ref,
        d_pre_ref,
        d_proj_ref,
        d_own_ref,
        d_theirs_ref,
        sums_ref,
        inner_sums_ref,
        slope_ref,
        d_heads_ref,
        wide_ref,
        outer_ref,
        wide_sems,
        outer_sems,
    ) = rest

    def target_of(part, rows):
        return wide_ref.at[part] if rows is None else wide_ref.at[part, rows]

    pieces = [(source,) + place for source, place in zip(sources, places)]
    if places[0][0] is None:
        wide_copies = copies_of(pieces, target_of, where_ref, wide_sems)
        turns = []
    else:
        wide_copies = []
        blocks, block, lanes = sources[0].shape
        halves_ref = wide_ref.reshape(2, 2, blocks, block, lanes)
        turns_ref = wide_ref.reshape(2, blocks, 2, block, lanes)
        seq, at = where_ref[0], where_ref[1]
        turns = []
        for n, (source, place, flip) in enumerate(pieces):
            first = place(0, seq, at ^ flip)
            row_copy = pltpu.make_async_copy(
                source, halves_ref.at[0, jnp.minimum(first // blocks, 1)], wide_sems.at[n]
            )
            turn_copy = pltpu.make_async_copy(
                source, turns_ref.at[1, :, jnp.minimum(first, 1)], wide_sems.at[n]
            )
            turns.append(((at + flip) % 2 == 0, row_copy, turn_copy))

    def each_turn(act):
        for is_first, row_copy, turn_copy in turns:
            pl.when(is_first)(functools.partial(act, row_copy))
            pl.when(jnp.logical_not(is_first))(functools.partial(act, turn_copy))

    each_turn(lambda copy: copy.start())
    if len(whole_outer_ref.shape) == 2:
        outer_copies = [pltpu.make_async_copy(whole_outer_ref, outer_ref, outer_sems.at[0])]
    else:
        devices, sides, block, lanes = whole_outer_ref.shape
        blocks_ref = outer_ref.reshape(sides, devices, block, lanes)
        outer_copies = [
            pltpu.make_async_copy(
                whole_outer_ref.at[:, slot],
                blocks_ref.at[where_ref[0] if slot == 0 else 1 - where_ref[0]],
                outer_sems.at[slot],
            )
            for slot in range(sides)
        ]
    for copy in outer_copies:
        copy.start()
    first_ref, second_ref = wide_ref.at[0], wide_ref.at[1]
    share = own_ref.shape[1]
    half = outer_ref.shape[0] // 2
    side = where_ref[0]
    mine = pl.ds(pl.multiple_of(side * share, 128), share)
    theirs = pl.ds(pl.multiple_of((1 - side) * share, 128), share)
    attended_ref[:, mine] = own_ref[...]
    attended_ref[:, theirs] = received_ref[...]
    attended = attended_ref[...]
    out_bias, attn_gain, attn_shift, outer_bias, ffn_gain, ffn_shift = (
        vector_ref[n : n + 1] for n in range(6)
    )
    for copy in wide_copies:
        copy.wait()
    each_turn(lambda copy: copy.wait())
    projected = jnp.concatenate(
        [matmul(attended, first_ref[:, half:]), matmul(attended, second_ref[:, half:])], axis=1
    )
    resid_one = token_ref[...].astype(F32) + projected + out_bias
    unit_one, inv_one = normed(resid_one)
    hidden = unit_one * attn_gain + attn_shift
    hidden_low = hidden.astype(BF16)
    hidden_ref[...] = hidden_low
    spans = [
        (ref, start, part * half + start)
        for part, ref in enumerate((first_ref, second_ref))
        for start in range(0, half, chunk)
    ]
    for copy in outer_copies:
        copy.wait()
    resid_two = hidden + outer_bias
    for ref, start, place in spans:
        lanes = slice(place, place + chunk)
        pre_act = matmul(hidden_low, ref[:, start : start + chunk]) + bias_ref[:, lanes]
        phi = 0.5 * (1.0 + lax.erf(pre_act * INV_SQRT_TWO))
        density = INV_SQRT_TWO_PI * jnp.exp(-0.5 * pre_act * pre_act)
        inner_low = (pre_act * phi).astype(BF16)
        inner_ref[:, lanes] = inner_low
        slope_ref[:, lanes] = (phi + pre_act * density).astype(BF16)
        resid_two += matmul(inner_low, outer_ref[lanes, :])
    unit_two, inv_two = normed(resid_two)
    result_ref[...] = (unit_two * ffn_gain + ffn_shift).astype(BF16)
    cotangent = grad_ref[...].astype(F32)
    d_resid_two = normed_back(cotangent * ffn_gain, unit_two, inv_two)
    d_branch = d_resid_two.astype(BF16)
    d_branch_ref[...] = d_branch
    d_hidden = d_resid_two
    inner_sums = []
    for ref, start, place in spans:
        lanes = slice(place, place + chunk)
        d_pre = matmul_nt(d_branch, outer_ref[lanes, :]) * slope_ref[:, lanes].astype(F32)
        inner_sums.append(row_sum(d_pre))
        d_pre_low = d_pre.astype(BF16)
        d_pre_ref[:, lanes] = d_pre_low
        d_hidden += matmul_nt(d_pre_low, ref[:, start : start + chunk])
    d_resid_one = normed_back(d_hidden * attn_gain, unit_one, inv_one)
    d_proj = d_resid_one.astype(BF16)
    d_proj_ref[...] = d_proj
    d_heads_ref[...] = (
        matmul_nt(d_proj[:, :share], first_ref[:, half:])
        + matmul_nt(d_proj[:, share:], second_ref[:, half:])
    ).astype(BF16)
    d_own_ref[...] = d_heads_ref[:, mine]
    d_theirs_ref[...] = d_heads_ref[:, theirs]
    sums_ref[...] = jnp.concatenate(
        [
            row_sum(d_resid_one),
            row_sum(d_hidden * unit_one),
            row_sum(d_hidden),
            row_sum(d_resid_two),
            row_sum(cotangent * unit_two),
            row_sum(cotangent),
            jnp.zeros((2, d_resid_one.shape[1]), F32),
        ],
        axis=0,
    )
    inner_sums_ref[...] = jnp.concatenate(inner_sums, axis=1)


def forward_back(
    where, own, received, tokens, grads, pieces, outer, vectors, bias, at, rows, earlier
):
    width = tokens.shape[1]
    share = own.shape[1]
    units = bias.shape[1]
    chunk = units // 6
    tops = [(2, width, units // 2 + share), (units, width)]
    outer_blocks = 1 if outer.ndim == 2 else outer.shape[1]

    def whole(array):
        return pl.BlockSpec(array.shape, lambda i, s: (0, 0), pipeline_mode=pl.Buffered(1))

    def local(lanes):
        return pl.BlockSpec((rows, lanes), lambda i, s: (0, 0), pipeline_mode=pl.Buffered(1))

    def placed(lanes):
        return pl.BlockSpec((rows, lanes), lambda i, s: (at, 0), pipeline_mode=pl.Buffered(1))

    lanes_out = [width, width, width, units, width, units, width, share, share]
    sources = [source for source, _, _ in pieces] + [outer]
    kept = len(lanes_out) - 1
    aliases = {}
    if earlier is not None:
        sources += list(earlier)
        aliases = {7 + len(sources) - kept + n: n for n in range(kept)}
    return pl.pallas_call(
        functools.partial(forward_back_body, chunk=chunk, places=places_of(pieces)),
        grid_spec=pltpu.PrefetchScalarGridSpec(
            num_scalar_prefetch=1,
            grid=(1,),
            in_specs=[
                placed(share),
                local(share),
                placed(width),
                placed(width),
                whole(vectors),
                whole(bias),
            ]
            + [pl.BlockSpec(memory_space=pl.ANY)] * len(sources),
            out_specs=[placed(lanes) for lanes in lanes_out[:kept]]
            + [local(lanes) for lanes in lanes_out[kept:]]
            + [
                pl.BlockSpec((8, width), lambda i, s: (0, 0)),
                pl.BlockSpec((1, units), lambda i, s: (0, 0)),
            ],
            scratch_shapes=[pltpu.VMEM((rows, units), BF16), pltpu.VMEM((rows, width), BF16)]
            + [pltpu.VMEM(shape, BF16) for shape in tops]
            + [pltpu.SemaphoreType.DMA((copy_count(pieces),)), pltpu.SemaphoreType.DMA((outer_blocks,))],
        ),
        out_shape=[
            jax.ShapeDtypeStruct((tokens.shape[0] if n < kept else rows, lanes), BF16)
            for n, lanes in enumerate(lanes_out)
        ]
        + [
            jax.ShapeDtypeStruct((8, width), F32),
            jax.ShapeDtypeStruct((1, units), F32),
        ],
        input_output_aliases=aliases,
        compiler_params=pltpu.CompilerParams(vmem_limit_bytes=VMEM_LIMIT),
        cost_estimate=SMALL_COST,
        name="forward_back",
    )(where, own, received, tokens, grads, vectors, bias, *sources)


def shards(
    hidden_in,
    prev_logits,
    segment,
    w_query,
    b_query,
    w_key,
    w_value,
    b_value,
    w_out,
    b_out,
    gain_attn,
    shift_attn,
    w_inner,
    b_inner,
    w_outer,
    b_outer,
    gain_ffn,
    shift_ffn,
    out_grad,
):
    seq = lax.axis_index("seq").astype(jnp.int32)
    fsdp_count = lax.axis_size("fsdp")
    count = fsdp_count.bit_length() - 1
    devices = 2 * fsdp_count
    heads, group, window = prev_logits.shape
    rows, width = w_query.shape
    inner_rows = b_inner.shape[0]
    hidden_units = inner_rows * devices
    share = width // 2
    half = hidden_units // 2
    tokens = hidden_in.shape[0]
    own_windows = tokens // window
    seq_hop = ("seq", 1)
    far, near, core = plan_hops(count)
    done = len(far)

    vectors = (b_query, b_value, b_out, gain_attn, shift_attn, b_outer, gain_ffn, shift_ffn, b_inner)
    where = jnp.stack([seq, lax.axis_index("fsdp").astype(jnp.int32)])
    other_inner, other_out = swap(w_inner, far[0]), swap(w_out, far[0])
    unit, unit_core, unit_seq, unit_both = pack(where, w_query, w_key, w_value, vectors)
    parts = 4
    part_rows = tokens // parts
    others = []

    def next_part(*earlier):
        part = hidden_in[len(others) * part_rows : (len(others) + 1) * part_rows]
        others.append(swap(after(part, *earlier), seq_hop))

    def quad(flip_seq, flip_core):
        def place(n, at_seq, at):
            one, two = bit_of(seq_hop, at_seq, at), bit_of(core, at_seq, at)
            return 2 * (1 - one if flip_seq else one) + (1 - two if flip_core else two)

        return place

    def both_flipped(at_seq, at):
        return at_seq ^ 1, at ^ 1

    def pairs_of(blocks):
        return blocks.reshape(-1, 2 * blocks.shape[1], blocks.shape[2])

    def hopped(blocks, hop, inner):
        return joined(blocks, swap(blocks, hop), hop, inner)

    (unit,) = merge(
        where,
        [
            (after(unit, other_inner, other_out)[None], quad(False, False)),
            (swap(unit_seq, seq_hop)[None], quad(True, False)),
            (swap(unit_core, core)[None], quad(False, True)),
            (trade(unit_both, both_flipped)[None], quad(True, True)),
        ],
    )
    unit = pairs_of(unit)
    wide, wide_core = cut(where, after(w_inner, unit), w_out, other_inner, other_out, far[0])
    outer_other = swap(after(w_outer, unit), seq_hop)
    next_part(unit)
    wide_item = joined(after(wide, others[0]), swap(wide_core, core), core, 1)
    if done == 2:
        def flipped(one, two):
            def place(n, at_seq, at):
                bits = bit_of(far[0], at_seq, at), bit_of(far[1], at_seq, at)
                return 4 * n + 2 * (1 - bits[0] if one else bits[0]) + (1 - bits[1] if two else bits[1])

            return place

        unit_item = [(unit, flipped(False, False))]
        for one, two in ((True, False), (False, True), (True, True)):
            mask = one * far[0][1] + two * far[1][1]
            unit_item.append((swap(unit, ("fsdp", mask)), flipped(one, two)))
        unit, wide = merge(where, unit_item, wide_item)
    else:
        unit, wide = merge(where, hopped(unit, far[0], 1), wide_item)
        for hop in far[1:]:
            (unit,) = merge(where, hopped(unit, hop, 1))
    outer = jnp.stack([after(w_outer, unit), outer_other])
    outer = lax.all_gather(outer, "fsdp", axis=0, tiled=False)
    if inner_rows % 16 != 0:
        outer = jnp.where(seq == 0, outer, outer[:, ::-1])
        outer = outer.transpose(1, 0, 2, 3).reshape(hidden_units, width)
    wide = pairs_of(wide)
    for hop in far[1:-1]:
        (wide,) = merge(where, hopped(wide, hop, 1))
    next_part(unit)
    wide_item = hopped(after(wide, unit), far[-1], 1)
    in_blocks = 2 * rows % 16 == 0
    unit_other = swap(unit, near)
    if in_blocks:
        near_places = spread(near, 1)
        unit_core, unit_other_core = swap(unit, core), swap(unit_other, core)
        unit_pieces = [
            (unit, near_places[0], 0),
            (unit_other, near_places[1], 0),
            (unit_core, near_places[0], 1),
            (unit_other_core, near_places[1], 1),
        ]
        wide_item[0] = (after(wide, others[1], unit_other), wide_item[0][1])
        (wide,) = merge(where, wide_item)
    else:
        wide_item[0] = (after(wide, others[1]), wide_item[0][1])
        unit, wide = merge(where, joined(unit, unit_other, near, 1), wide_item)
        unit = unit.reshape(width, unit.shape[-1])
        unit_pieces = [(unit, None, 0), (swap(unit, core), None, 1)]
    next_part(unit_pieces[1][0])
    next_part(unit_pieces[1][0])

    def near_or_seq(at_seq, at):
        return across(near if at % 2 == 0 else seq_hop)(at_seq, at)

    def seq_or_near(at_seq, at):
        return across(seq_hop if at % 2 == 0 else near)(at_seq, at)

    wide_other = trade(wide, near_or_seq)
    own_qkv, qkv_weight, small, qkv_bias = project_first(where, hidden_in, unit_pieces)

    seg_rows = segment[:, None]
    seg_cols = segment.reshape(group // window, 1, window)
    own_start = (seq * own_windows).reshape(1)
    other_start = ((1 - seq) * own_windows).reshape(1)

    logits, probs, own_out = attend(
        own_qkv, prev_logits, seg_rows, seg_cols, own_start, 0, own_windows, None
    )
    blocks = wide.shape[0]
    (wide,) = merge(
        where,
        joined_by_core(
            after(wide, own_out, others[-2], others[-1]), wide_other, core, (near, 1), (seq_hop, blocks)
        ),
    )
    wide_other = trade(wide, seq_or_near)
    blocks = wide.shape[0]
    zero_places, one_places = spread(seq_hop, blocks), spread(near, 1)
    wide_places = [by_core(core, zero_places[n], one_places[n]) for n in range(2)]
    other_qkv, other_rows = project_rest(after(tuple(others), wide), qkv_weight, qkv_bias)
    other_out = []
    received = []
    for w in range(own_windows):
        logits, probs, out = attend(
            other_qkv, prev_logits, seg_rows, seg_cols, other_start + w, w, 1, (logits, probs)
        )
        other_out.append(out)
        if w == 0:
            wide_other = after(wide_other, out)
            if in_blocks:
                wide_core, wide_other_core = swap(wide, core), swap(wide_other, core)
                wide_pieces = [
                    (wide, wide_places[0], 0),
                    (wide_other, wide_places[1], 0),
                    (wide_core, wide_places[0], 1),
                    (wide_other_core, wide_places[1], 1),
                ]
            else:
                (wide,) = merge(where, [(wide, wide_places[0]), (wide_other, wide_places[1])])
                wide = wide.reshape(width, wide.shape[-1])
                wide_pieces = [(wide, None, 0), (swap(wide, core), None, 1)]
            other_qkv = after(other_qkv, wide_other)
        received.append(swap(out, seq_hop))
    small = small.astype(F32)
    layer_vectors = jnp.concatenate([small[:, 2:8].T, jnp.zeros((2, width), F32)], axis=0)
    inner_bias = small[:, 8 : 8 + hidden_units // width].reshape(1, hidden_units)

    full = None
    d_others = []
    sums, inner_sums = 0.0, 0.0
    for w in range(own_windows):
        outs = forward_back(
            where,
            own_out,
            received[w],
            hidden_in,
            out_grad,
            wide_pieces,
            outer,
            layer_vectors,
            inner_bias,
            w,
            window,
            full,
        )
        full = outs[:8]
        d_others.append(swap(outs[8], seq_hop))
        sums += outs[9]
        inner_sums += outs[10]
    hidden_out, attended, hidden, inner, d_branch, d_pre, d_proj, d_own = full

    class Reduction:
        def __init__(self, value, hops):
            self.value, self.hops = value, list(hops)
            self.send()

        def send(self):
            if self.hops:
                hop, place = self.hops.pop(0)
                away, self.keep = split(self.value, hop, place)
                self.other = swap(away, hop)

        def add(self, latest):
            self.value = total(after(self.keep, latest), self.other)
            self.send()
            return self.value

    grid = (2,) * (count + 1)
    outer_hops = [(core, done + 2), (near, done + 1)]
    outer_hops += [(far[n], n + 1) for n in reversed(range(done))] + [(seq_hop, 0)]
    inner_hops = [(core, done + 2), (seq_hop, 0), (near, done)]
    inner_hops += [(far[n], n) for n in reversed(range(done))]
    tail_hops = [(core, done + 2), (near, done + 1)]
    tail_hops += [(far[n], n + 1) for n in reversed(range(done))]

    inner, attended = after((inner, attended), d_others[0])
    g_outer = matmul_tn(inner, d_branch).astype(BF16)
    g_out = matmul_tn(attended, d_proj).astype(BF16)
    outer_grad = jnp.concatenate(
        [
            g_outer.reshape(grid + (inner_rows, width)),
            g_out.reshape(grid + (rows, width)),
        ],
        axis=-2,
    )
    outer_sum = Reduction(outer_grad, outer_hops)
    g_inner = matmul_tn(after(hidden, outer_grad), d_pre).astype(BF16)
    inner_sum = Reduction(g_inner.reshape(grid + (rows, hidden_units)), inner_hops)
    latest = outer_sum.add(g_inner)
    latest = inner_sum.add(latest)

    d_scores = None
    input_received = []
    other_qkv = after(other_qkv, latest)
    g_qkv, qkv_sum = 0.0, 0.0
    for w in range(own_windows):
        d_scores, d_qkv, column_sums = attend_back(
            other_qkv, probs, d_others[w], other_out[w], other_start + w, w, 1, d_scores
        )
        input_received.append(swap(matmul_nt(d_qkv, qkv_weight).astype(BF16), seq_hop))
        g_qkv += matmul_tn(other_rows[w * window : (w + 1) * window], d_qkv)
        qkv_sum += column_sums[0]
    latest = outer_sum.add(d_qkv)
    latest = inner_sum.add(latest)
    own_qkv = after(own_qkv, latest)
    d_scores, own_d_qkv, column_sums = attend_back(
        own_qkv, probs, d_own, own_out, own_start, 0, own_windows, d_scores
    )
    own_d_qkv = after(own_d_qkv, outer_sum.other, inner_sum.other)
    g_qkv += matmul_tn(hidden_in, own_d_qkv)
    qkv_sum = (qkv_sum + jnp.sum(column_sums, axis=0)).reshape(-1)

    def both_sides(part):
        blank = jnp.zeros_like(part)
        return jnp.where(
            seq == 0, jnp.concatenate([part, blank]), jnp.concatenate([blank, part])
        )

    small_grads = jnp.concatenate(
        [
            both_sides(qkv_sum[:share])[:, None],
            both_sides(qkv_sum[2 * share :])[:, None],
            sums[:6].T,
            inner_sums.reshape(width, hidden_units // width),
        ],
        axis=1,
    )
    lanes = small_grads.shape[1]
    tail = jnp.concatenate(
        [g_qkv.astype(BF16), jnp.pad(small_grads, ((0, 0), (0, 128 - lanes))).astype(BF16)], axis=1
    ).reshape(grid + (rows, 3 * share + 128))
    direct = done == 2
    tail_sum = Reduction(tail, tail_hops[:2] if direct else tail_hops)
    latest = outer_sum.add(tail)
    latest = tail_sum.add(latest)
    latest = inner_sum.add(latest)
    latest = outer_sum.add(latest)
    latest = tail_sum.add(latest)
    if direct:
        bits = my_bit(far[0]), my_bit(far[1])

        def block(one, two):
            at = (1 - bits[0] if one else bits[0], 1 - bits[1] if two else bits[1])
            blocks = tail_sum.value.reshape((2, 4) + tail_sum.value.shape[-2:])
            return lax.dynamic_index_in_dim(blocks, 2 * at[0] + at[1], 1, keepdims=False)

        arrivals = [
            swap(block(one, two), ("fsdp", one * far[0][1] + two * far[1][1]))
            for one, two in ((True, False), (False, True), (True, True))
        ]
        keep = block(False, False)
    latest = inner_sum.add(latest)
    latest = outer_sum.add(latest)
    if direct:
        terms = [after(keep, latest)] + arrivals
        tail = functools.reduce(jnp.add, [term.astype(F32) for term in terms]).astype(BF16)
        latest = tail
    while not direct and len(tail_sum.value.shape) > 3:
        latest = tail_sum.add(latest)
        tail = latest
    while len(outer_sum.value.shape) > 2:
        latest = outer_sum.add(latest)
    while len(inner_sum.value.shape) > 2:
        latest = inner_sum.add(latest)
    outer_grad, inner_grad = outer_sum.value, inner_sum.value
    send, own_tail = split(tail, seq_hop, 0)
    other_tail = swap(send, seq_hop)
    grads = unpack(own_tail[:, 3 * share :], other_tail[:, 3 * share :], inner_rows)

    def weight_part(slot):
        at = slice(slot * share, (slot + 1) * share)
        return jnp.where(
            seq == 0,
            jnp.concatenate([own_tail[:, at], other_tail[:, at]], axis=1),
            jnp.concatenate([other_tail[:, at], own_tail[:, at]], axis=1),
        ).astype(F32)

    input_grad = (
        d_proj.astype(F32)
        + matmul_nt(own_d_qkv, qkv_weight)
        + jnp.concatenate(input_received, axis=0).astype(F32)
    ).astype(BF16)
    return (
        hidden_out,
        logits,
        input_grad,
        d_scores,
        weight_part(0),
        grads[0],
        weight_part(1),
        weight_part(2),
        grads[1],
        outer_grad[inner_rows:].astype(F32),
        grads[2],
        grads[3],
        grads[4],
        inner_grad.astype(F32),
        grads[8],
        outer_grad[:inner_rows].astype(F32),
        grads[5],
        grads[6],
        grads[7],
    )


def solution(mesh):
    in_specs = (
        P(("fsdp", "seq"), None),
        P("seq", "fsdp", None),
        P("fsdp"),
        P(("seq", "fsdp"), None),
        P(("seq", "fsdp")),
        P(("seq", "fsdp"), None),
        P(("seq", "fsdp"), None),
        P(("seq", "fsdp")),
        P(("seq", "fsdp"), None),
        P(("seq", "fsdp")),
        P(("seq", "fsdp")),
        P(("seq", "fsdp")),
        P(("seq", "fsdp"), None),
        P(("seq", "fsdp")),
        P(("seq", "fsdp"), None),
        P(("seq", "fsdp")),
        P(("seq", "fsdp")),
        P(("seq", "fsdp")),
        P(("fsdp", "seq"), None),
    )
    out_specs = (
        P(("fsdp", "seq"), None),
        P("seq", "fsdp", None),
        P(("fsdp", "seq"), None),
        P("seq", "fsdp", None),
        P(("seq", "fsdp"), None),
        P(("seq", "fsdp")),
        P(("seq", "fsdp"), None),
        P(("seq", "fsdp"), None),
        P(("seq", "fsdp")),
        P(("seq", "fsdp"), None),
        P(("seq", "fsdp")),
        P(("seq", "fsdp")),
        P(("seq", "fsdp")),
        P(("seq", "fsdp"), None),
        P(("seq", "fsdp")),
        P(("seq", "fsdp"), None),
        P(("seq", "fsdp")),
        P(("seq", "fsdp")),
        P(("seq", "fsdp")),
    )
    return jax.shard_map(shards, mesh=mesh, in_specs=in_specs, out_specs=out_specs, check_vma=False)
```

```python
import functools
import math

import jax
import jax.numpy as jnp
from jax import lax
from jax.experimental import pallas as pl
from jax.experimental.pallas import tpu as pltpu
from jax.sharding import PartitionSpec as P

NORM_EPSILON = 1e-06
MASK_VALUE = -1e30
INV_SQRT_TWO = 0.7071067811865476
INV_SQRT_TWO_PI = 0.3989422804014327
VMEM_LIMIT = 56 * 1024 * 1024
BF16 = jnp.bfloat16
F32 = jnp.float32
SMALL_COST = pl.CostEstimate(flops=1024, transcendentals=0, bytes_accessed=1024)


def matmul(left_op, right_op):
    return jnp.dot(left_op, right_op, preferred_element_type=F32)


def matmul_tn(left_op, right_op):
    return lax.dot_general(
        left_op, right_op, (((0,), (0,)), ((), ())), preferred_element_type=F32
    )


def matmul_nt(left_op, right_op):
    return lax.dot_general(
        left_op, right_op, (((1,), (1,)), ((), ())), preferred_element_type=F32
    )


def column_sum(values):
    return jnp.sum(values.astype(F32), axis=0)


BOTH = ("seq", "fsdp")


def trade(value, partner):
    seq_count, fsdp_count = lax.axis_size("seq"), lax.axis_size("fsdp")
    pairs = []
    for seq in range(seq_count):
        for at in range(fsdp_count):
            to_seq, to = partner(seq, at)
            pairs.append((seq * fsdp_count + at, to_seq * fsdp_count + to))
    return lax.ppermute(value, BOTH, pairs)


def across(hop):
    axis, mask = hop
    if axis == "seq":
        return lambda seq, at: (seq ^ mask, at)
    return lambda seq, at: (seq, at ^ mask)


def swap(value, hop):
    return trade(value, across(hop))


def bit_of(hop, seq, at):
    axis, mask = hop
    return (seq if axis == "seq" else at // mask) % 2


def my_bit(hop):
    at = lax.axis_index(hop[0]).astype(jnp.int32)
    return bit_of(hop, at, at)


def after(value, *others):
    return lax.optimization_barrier((value,) + others)[0]


def merge_body(where_ref, *refs, plans):
    seq, at = where_ref[0], where_ref[1]
    outs = refs[sum(len(plan) for plan in plans) :]
    for plan, out_ref in zip(plans, outs):
        for target in plan:
            source, refs = refs[0], refs[1:]
            for n in range(source.shape[0]):
                out_ref[target(n, seq, at)] = source[n]


def merge(where, *items):
    sources = [blocks for item in items for blocks, _ in item]
    plans = [[target for _, target in item] for item in items]
    outs = []
    for item in items:
        total_blocks = sum(blocks.shape[0] for blocks, _ in item)
        outs.append(jax.ShapeDtypeStruct((total_blocks,) + item[0][0].shape[1:], BF16))
    return pl.pallas_call(
        functools.partial(merge_body, plans=plans),
        in_specs=[pl.BlockSpec(memory_space=pltpu.SMEM)]
        + [pl.BlockSpec(memory_space=pltpu.VMEM)] * len(sources),
        out_specs=[pl.BlockSpec(memory_space=pltpu.VMEM)] * len(outs),
        out_shape=outs,
        compiler_params=pltpu.CompilerParams(vmem_limit_bytes=VMEM_LIMIT),
        cost_estimate=SMALL_COST,
        name="merge",
    )(where, *sources)


def spread(hop, inner):
    def target(flip):
        def place(n, seq, at):
            bit = bit_of(hop, seq, at)
            bit = 1 - bit if flip else bit
            return (n // inner) * 2 * inner + n % inner + bit * inner

        return place

    return target(False), target(True)


def joined(mine, other, hop, inner):
    own_place, other_place = spread(hop, inner)
    return [(mine, own_place), (other, other_place)]


def by_core(core, zero, one):
    def place(n, seq, at):
        bit = bit_of(core, seq, at)
        return (1 - bit) * zero(n, seq, at) + bit * one(n, seq, at)

    return place


def joined_by_core(mine, other, core, zero, one):
    zero_places, one_places = spread(*zero), spread(*one)
    return [
        (mine, by_core(core, zero_places[0], one_places[0])),
        (other, by_core(core, zero_places[1], one_places[1])),
    ]


def split(value, hop, place):
    bit = my_bit(hop)
    return (
        lax.dynamic_index_in_dim(value, 1 - bit, place, keepdims=False),
        lax.dynamic_index_in_dim(value, bit, place, keepdims=False),
    )


def total(one, two):
    return (one.astype(F32) + two.astype(F32)).astype(BF16)


def plan_hops(count):
    bits = [("fsdp", 1 << n) for n in range(count)]
    return list(reversed(bits[2:])), bits[1], bits[0]


def place_of(rows, inner_rows):
    count = 8 * rows + inner_rows
    per_row = inner_rows // rows
    entry = lax.broadcasted_iota(jnp.int32, (1, count), 1)
    row, lane = entry * 0, entry * 0
    for slot in range(8):
        inside = (entry >= slot * rows) & (entry < (slot + 1) * rows)
        row = jnp.where(inside, entry - slot * rows, row)
        lane = jnp.where(inside, slot, lane)
    for unit in range(rows):
        low = 8 * rows + unit * per_row
        inside = (entry >= low) & (entry < low + per_row)
        row = jnp.where(inside, unit, row)
        lane = jnp.where(inside, 8 + entry - low, lane)
    return row, lane


def pack_body(where_ref, q_ref, k_ref, v_ref, *rest):
    small_refs = rest[:9]
    quarter_refs = (rest[9:11], rest[11:13])
    line_ref, whole_ref = rest[13:]
    rows, width = q_ref.shape
    share = width // 2
    lanes = quarter_refs[0][0].shape[1]
    inner_rows = small_refs[8].shape[1]
    side, core = where_ref[0], where_ref[1] % 2
    for slot, ref in enumerate(small_refs):
        line_ref[0:1, slot * rows : slot * rows + ref.shape[1]] = ref[...].astype(F32)
    row, lane = place_of(rows, inner_rows)
    count = 8 * rows + inner_rows
    spread_line = jnp.where(
        lax.broadcasted_iota(jnp.int32, (rows, count), 0) == row, line_ref[0:1, :count], 0.0
    )
    pick = jnp.where(lax.broadcasted_iota(jnp.int32, (128, count), 0) == lane, 1.0, 0.0)
    extra = matmul_nt(spread_line.astype(BF16), pick.astype(BF16)).astype(BF16)
    for turn in range(2):
        start = pl.multiple_of(((side + turn) % 2) * share, 128)
        for slot, ref in enumerate((q_ref, k_ref, v_ref)):
            whole_ref[:, slot * share : (slot + 1) * share] = ref[:, pl.ds(start, share)]
        whole_ref[:, 3 * share :] = extra
        for other in range(2):
            at = pl.multiple_of(((core + other) % 2) * lanes, 128)
            quarter_refs[turn][other][...] = whole_ref[:, pl.ds(at, lanes)]


def pack(where, w_query, w_key, w_value, vectors):
    rows, width = w_query.shape
    lines = [v.reshape(1, -1) for v in vectors]
    count = sum(line.shape[1] for line in lines)
    lanes = 3 * width // 2 + 128
    quarter = jax.ShapeDtypeStruct((rows, lanes // 2), BF16)
    return pl.pallas_call(
        pack_body,
        in_specs=[pl.BlockSpec(memory_space=pltpu.SMEM)]
        + [pl.BlockSpec(memory_space=pltpu.VMEM)] * (3 + len(lines)),
        out_specs=[pl.BlockSpec(memory_space=pltpu.VMEM)] * 4,
        out_shape=[quarter] * 4,
        scratch_shapes=[
            pltpu.VMEM((8, -(-count // 128) * 128), F32),
            pltpu.VMEM((rows, lanes), BF16),
        ],
        cost_estimate=SMALL_COST,
        name="pack",
    )(where, w_query, w_key, w_value, *lines)


def cut_body(where_ref, inner_ref, out_ref, other_inner_ref, other_out_ref, *half_refs, hop):
    half, share = inner_ref.shape[1] // 2, out_ref.shape[1] // 2
    core = where_ref[1] % 2
    bit = bit_of(hop, where_ref[0], where_ref[1])
    for turn, ref in enumerate(half_refs):
        part = (core + turn) % 2
        inner_lanes = pl.ds(pl.multiple_of(part * half, 128), half)
        out_lanes = pl.ds(pl.multiple_of(part * share, 128), share)
        for place, inner, out in (
            (bit, inner_ref, out_ref),
            (1 - bit, other_inner_ref, other_out_ref),
        ):
            ref[place, :, :half] = inner[:, inner_lanes]
            ref[place, :, half:] = out[:, out_lanes]


def cut(where, inner, out, other_inner, other_out, hop):
    rows = inner.shape[0]
    half = jax.ShapeDtypeStruct((2, rows, (inner.shape[1] + out.shape[1]) // 2), BF16)
    return pl.pallas_call(
        functools.partial(cut_body, hop=hop),
        in_specs=[pl.BlockSpec(memory_space=pltpu.SMEM)]
        + [pl.BlockSpec(memory_space=pltpu.VMEM)] * 4,
        out_specs=[pl.BlockSpec(memory_space=pltpu.VMEM)] * 2,
        out_shape=[half, half],
        cost_estimate=SMALL_COST,
        name="cut",
    )(where, inner, out, other_inner, other_out)


def unpack_body(first_ref, second_ref, *rest):
    out_refs = rest[:9]
    rows = first_ref.shape[0]
    inner_rows = out_refs[8].shape[1]
    count = 8 * rows + inner_rows
    row, lane = place_of(rows, inner_rows)
    pick = jnp.where(lax.broadcasted_iota(jnp.int32, (128, count), 0) == lane, 1.0, 0.0)
    pick = pick.astype(BF16)
    spread = matmul(first_ref[...], pick) + matmul(second_ref[...], pick)
    inside = lax.broadcasted_iota(jnp.int32, (rows, count), 0) == row
    line = jnp.sum(jnp.where(inside, spread, 0.0), axis=0, keepdims=True)
    for slot, ref in enumerate(out_refs):
        ref[...] = line[:, slot * rows : slot * rows + ref.shape[1]]


def unpack(first, second, inner_rows):
    rows = first.shape[0]
    outs = pl.pallas_call(
        unpack_body,
        in_specs=[pl.BlockSpec(memory_space=pltpu.VMEM)] * 2,
        out_specs=[pl.BlockSpec(memory_space=pltpu.VMEM)] * 9,
        out_shape=[jax.ShapeDtypeStruct((1, rows), F32)] * 8
        + [jax.ShapeDtypeStruct((1, inner_rows), F32)],
        name="unpack",
    )(first, second)
    return [out.reshape(-1) for out in outs]


def project_block(rows, weight, bias, out_ref):
    scale = jnp.where(pl.program_id(0) == 0, 0.125, 1.0)
    out_ref[...] = ((matmul(rows, weight) + bias).astype(BF16).astype(F32) * scale).astype(BF16)


def copies_of(pieces, target_of, where_ref, sems):
    seq, at = where_ref[0], where_ref[1]
    copies = []
    for source, place, flip in pieces:
        half = (at + flip) % 2
        if place is None:
            copies.append((source, target_of(half, None)))
            continue
        for n in range(source.shape[0]):
            block = source.shape[1]
            start = pl.multiple_of(place(n, seq, at ^ flip) * block, 16)
            copies.append((source.at[n], target_of(half, pl.ds(start, block))))
    copies = [
        pltpu.make_async_copy(source, target, sems.at[n])
        for n, (source, target) in enumerate(copies)
    ]
    for copy in copies:
        copy.start()
    return copies


def copy_count(pieces):
    return sum(1 if place is None else source.shape[0] for source, place, _ in pieces)


def places_of(pieces):
    return [(place, flip) for _, place, flip in pieces]


def project_first_body(where_ref, token_ref, *rest, places):
    sources, rest = rest[: len(places)], rest[len(places) :]
    out_ref, weight_ref, small_ref, bias_ref, whole_ref, turned_ref, sems = rest
    half = whole_ref.shape[1] // 2
    share = weight_ref.shape[1]
    step = pl.program_id(0)

    @pl.when(step == 0)
    def _():
        def target_of(part, rows):
            lanes = pl.ds(pl.multiple_of(part * half, 128), half)
            return whole_ref.at[:, lanes] if rows is None else whole_ref.at[rows, lanes]

        pieces = [(source,) + place for source, place in zip(sources, places)]
        if places[0][0] is None:
            copies = copies_of(pieces, target_of, where_ref, sems)
        else:
            blocks, block, _ = sources[0].shape
            turns_ref = whole_ref.reshape(blocks, 2, block, 2 * half)
            seq, at = where_ref[0], where_ref[1]
            copies = []
            for n, (source, place, flip) in enumerate(pieces):
                lanes = pl.ds(pl.multiple_of((at + flip) % 2 * half, 128), half)
                target = turns_ref.at[:, place(0, seq, at ^ flip), :, lanes]
                copies.append(pltpu.make_async_copy(source, target, sems.at[n]))
            for copy in copies:
                copy.start()
        for copy in copies:
            copy.wait()
        small = whole_ref[:, 3 * share :]
        small_ref[...] = small
        turned_ref[...] = small.astype(F32).T
        mine = pl.ds(pl.multiple_of(where_ref[0] * share, 128), share)
        bias_ref[:, :share] = turned_ref[0:1, mine]
        bias_ref[:, share : 2 * share] = jnp.zeros((1, share), F32)
        bias_ref[:, 2 * share :] = turned_ref[1:2, mine]

    lanes = pl.ds(pl.multiple_of(step * share, 128), share)
    weight = whole_ref[:, lanes]
    weight_ref[...] = weight
    project_block(token_ref[...], weight, bias_ref[:, lanes], out_ref)


def project_first(where, tokens, pieces):
    rows, width = tokens.shape
    lanes = 2 * pieces[0][0].shape[-1]
    share = (lanes - 128) // 3
    smem = pl.BlockSpec(memory_space=pltpu.SMEM)
    return pl.pallas_call(
        functools.partial(project_first_body, places=places_of(pieces)),
        grid=(3,),
        in_specs=[
            smem,
            pl.BlockSpec((rows, width), lambda n: (0, 0), pipeline_mode=pl.Buffered(1)),
        ]
        + [pl.BlockSpec(memory_space=pl.ANY)] * len(pieces),
        out_specs=[
            pl.BlockSpec((rows, share), lambda n: (0, n)),
            pl.BlockSpec((width, share), lambda n: (0, n)),
            pl.BlockSpec((width, 128), lambda n: (0, 0)),
            pl.BlockSpec((1, 3 * share), lambda n: (0, 0)),
        ],
        out_shape=[
            jax.ShapeDtypeStruct((rows, 3 * share), BF16),
            jax.ShapeDtypeStruct((width, 3 * share), BF16),
            jax.ShapeDtypeStruct((width, 128), BF16),
            jax.ShapeDtypeStruct((1, 3 * share), F32),
        ],
        scratch_shapes=[
            pltpu.VMEM((width, lanes), BF16),
            pltpu.VMEM((128, width), F32),
            pltpu.SemaphoreType.DMA((copy_count(pieces),)),
        ],
        compiler_params=pltpu.CompilerParams(vmem_limit_bytes=VMEM_LIMIT),
        cost_estimate=SMALL_COST,
        name="project_first",
    )(where, tokens, *(source for source, _, _ in pieces))


def project_rest_body(weight_ref, bias_ref, *rest):
    *chunk_refs, out_ref, rows_ref = rest

    @pl.when(pl.program_id(0) == 0)
    def _():
        at = 0
        for ref in chunk_refs:
            rows_ref[at : at + ref.shape[0], :] = ref[...]
            at += ref.shape[0]

    project_block(rows_ref[...], weight_ref[...], bias_ref[...], out_ref)


def project_rest(chunks, weight, bias):
    rows = sum(chunk.shape[0] for chunk in chunks)
    width, lanes = weight.shape
    share = lanes // 3
    return pl.pallas_call(
        project_rest_body,
        grid=(3,),
        in_specs=[
            pl.BlockSpec((width, share), lambda n: (0, n)),
            pl.BlockSpec((1, share), lambda n: (0, n)),
        ]
        + [
            pl.BlockSpec(chunk.shape, lambda n: (0, 0), pipeline_mode=pl.Buffered(1))
            for chunk in chunks
        ],
        out_specs=[
            pl.BlockSpec((rows, share), lambda n: (0, n)),
            pl.BlockSpec((rows, width), lambda n: (0, 0)),
        ],
        out_shape=[
            jax.ShapeDtypeStruct((rows, lanes), BF16),
            jax.ShapeDtypeStruct((rows, width), BF16),
        ],
        compiler_params=pltpu.CompilerParams(vmem_limit_bytes=VMEM_LIMIT),
        cost_estimate=SMALL_COST,
        name="project_rest",
    )(weight, bias, *chunks)


def lane_halves():
    lanes = lax.broadcasted_iota(jnp.int32, (1, 128), 1)
    low = jnp.where(lanes < 64, 1.0, 0.0)
    return low.astype(BF16), (1.0 - low).astype(BF16)


def attend_body(start, q_ref, k_ref, v_ref, prior_ref, row_seg, col_seg, *rest):
    logits_ref, probs_ref, out_ref = rest[-3:]
    halves = lane_halves()
    allowed = row_seg[...] == col_seg[0]
    queries = q_ref[...]
    mixed = None
    for head, half in enumerate(halves):
        scores = matmul_nt(queries, k_ref[...] * half) + prior_ref[head].astype(F32)
        logits_ref[head] = scores.astype(BF16)
        masked = jnp.where(allowed, scores, MASK_VALUE)
        top = jnp.max(masked, axis=1, keepdims=True)
        terms = jnp.exp(masked - top)
        total = jnp.sum(terms, axis=1, keepdims=True)
        probs = (terms * (1.0 / total)).astype(BF16)
        probs_ref[head] = probs
        part = matmul(probs, v_ref[...] * half)
        mixed = part if mixed is None else mixed + part
    out_ref[...] = mixed.astype(BF16)


def attend(qkv, prior, seg_rows, seg_cols, start, first, count, earlier):
    heads, group, window = prior.shape
    pairs = heads // 2
    share = heads * 64

    def qkv_spec(part):
        return pl.BlockSpec(
            (window, 128), lambda w, p, s: (first + w, part * pairs + p)
        )

    pair_spec = pl.BlockSpec((2, window, window), lambda w, p, s: (p, s[0] + w, 0))
    in_specs = [
        qkv_spec(0),
        qkv_spec(1),
        qkv_spec(2),
        pair_spec,
        pl.BlockSpec((window, 1), lambda w, p, s: (s[0] + w, 0)),
        pl.BlockSpec((1, 1, window), lambda w, p, s: (s[0] + w, 0, 0)),
    ]
    operands = [qkv, qkv, qkv, prior, seg_rows, seg_cols]
    aliases = {}
    if earlier is not None:
        aliases = {len(operands) + 1: 0, len(operands) + 2: 1}
        operands += list(earlier)
        in_specs += [pl.BlockSpec(memory_space=pl.ANY)] * 2
    big = jax.ShapeDtypeStruct(prior.shape, BF16)
    return pl.pallas_call(
        attend_body,
        grid_spec=pltpu.PrefetchScalarGridSpec(
            num_scalar_prefetch=1,
            grid=(count, pairs),
            in_specs=in_specs,
            out_specs=[
                pair_spec,
                pair_spec,
                pl.BlockSpec((window, 128), lambda w, p, s: (w, p)),
            ],
        ),
        out_shape=[
            big,
            big,
            jax.ShapeDtypeStruct((count * window, share), BF16),
        ],
        input_output_aliases=aliases,
        compiler_params=pltpu.CompilerParams(vmem_limit_bytes=VMEM_LIMIT),
        cost_estimate=SMALL_COST,
        name="attend",
    )(start, *operands)


def attend_back_body(
    start, q_ref, k_ref, v_ref, probs_ref, grad_ref, out_ref, *rest
):
    d_scores_ref, d_qkv_ref, sums_ref = rest[-3:]
    pair = pl.program_id(1)
    pairs = pl.num_programs(1)
    halves = lane_halves()
    grads = grad_ref[...]
    product = grads.astype(F32) * out_ref[...].astype(F32)
    d_queries = d_keys = d_values = None
    for head, half in enumerate(halves):
        probs = probs_ref[head]
        inner = jnp.sum(product * half.astype(F32), axis=1, keepdims=True)
        d_probs = matmul_nt(grads, v_ref[...] * half)
        d_scores = (probs.astype(F32) * (d_probs - inner)).astype(BF16)
        d_scores_ref[head] = d_scores
        parts = (
            matmul(d_scores, k_ref[...] * half),
            matmul_tn(d_scores, q_ref[...] * half),
            matmul_tn(probs, grads * half),
        )
        if head == 0:
            d_queries, d_keys, d_values = parts
        else:
            d_queries += parts[0]
            d_keys += parts[1]
            d_values += parts[2]
    for slot, value in enumerate((d_queries * 0.125, d_keys, d_values)):
        lanes = pl.ds(pl.multiple_of((slot * pairs + pair) * 128, 128), 128)
        d_qkv_ref[:, lanes] = value.astype(BF16)
        sums_ref[:, lanes] = row_sum(value)


def attend_back(qkv, probs, grads, outs, start, first, count, earlier):
    heads, group, window = probs.shape
    pairs = heads // 2
    share = heads * 64

    def qkv_spec(part):
        return pl.BlockSpec(
            (window, 128), lambda w, p, s: (first + w, part * pairs + p)
        )

    pair_spec = pl.BlockSpec((2, window, window), lambda w, p, s: (p, s[0] + w, 0))
    row_spec = pl.BlockSpec((window, 128), lambda w, p, s: (w, p))
    in_specs = [qkv_spec(0), qkv_spec(1), qkv_spec(2), pair_spec, row_spec, row_spec]
    operands = [qkv, qkv, qkv, probs, grads, outs]
    aliases = {}
    if earlier is not None:
        aliases = {len(operands) + 1: 0}
        operands.append(earlier)
        in_specs.append(pl.BlockSpec(memory_space=pl.ANY))
    return pl.pallas_call(
        attend_back_body,
        grid_spec=pltpu.PrefetchScalarGridSpec(
            num_scalar_prefetch=1,
            grid=(count, pairs),
            in_specs=in_specs,
            out_specs=[
                pair_spec,
                pl.BlockSpec((window, 3 * share), lambda w, p, s: (w, 0)),
                pl.BlockSpec((None, 1, 3 * share), lambda w, p, s: (w, 0, 0)),
            ],
        ),
        out_shape=[
            jax.ShapeDtypeStruct(probs.shape, BF16),
            jax.ShapeDtypeStruct((count * window, 3 * share), BF16),
            jax.ShapeDtypeStruct((count, 1, 3 * share), F32),
        ],
        input_output_aliases=aliases,
        compiler_params=pltpu.CompilerParams(vmem_limit_bytes=VMEM_LIMIT),
        cost_estimate=SMALL_COST,
        name="attend_back",
    )(start, *operands)


def normed(values):
    centred = values - jnp.mean(values, axis=-1, keepdims=True)
    inv_dev = lax.rsqrt(
        jnp.mean(centred * centred, axis=-1, keepdims=True) + NORM_EPSILON
    )
    return centred * inv_dev, inv_dev


def normed_back(scaled, unit, inv_dev):
    return inv_dev * (
        scaled
        - jnp.mean(scaled, axis=-1, keepdims=True)
        - unit * jnp.mean(scaled * unit, axis=-1, keepdims=True)
    )


def row_sum(values):
    return jnp.sum(values, axis=0, keepdims=True)


def forward_back_body(
    where_ref,
    own_ref,
    received_ref,
    token_ref,
    grad_ref,
    vector_ref,
    bias_ref,
    *rest,
    chunk,
    places,
):
    sources, whole_outer_ref = rest[: len(places)], rest[len(places)]
    rest = rest[-17:]
    (
        result_ref,
        attended_ref,
        hidden_ref,
        inner_ref,
        d_branch_ref,
        d_pre_ref,
        d_proj_ref,
        d_own_ref,
        d_theirs_ref,
        sums_ref,
        inner_sums_ref,
        slope_ref,
        d_heads_ref,
        wide_ref,
        outer_ref,
        wide_sems,
        outer_sems,
    ) = rest

    def target_of(part, rows):
        return wide_ref.at[part] if rows is None else wide_ref.at[part, rows]

    pieces = [(source,) + place for source, place in zip(sources, places)]
    if places[0][0] is None:
        wide_copies = copies_of(pieces, target_of, where_ref, wide_sems)
        turns = []
    else:
        wide_copies = []
        blocks, block, lanes = sources[0].shape
        halves_ref = wide_ref.reshape(2, 2, blocks, block, lanes)
        turns_ref = wide_ref.reshape(2, blocks, 2, block, lanes)
        seq, at = where_ref[0], where_ref[1]
        turns = []
        for n, (source, place, flip) in enumerate(pieces):
            first = place(0, seq, at ^ flip)
            row_copy = pltpu.make_async_copy(
                source, halves_ref.at[0, jnp.minimum(first // blocks, 1)], wide_sems.at[n]
            )
            turn_copy = pltpu.make_async_copy(
                source, turns_ref.at[1, :, jnp.minimum(first, 1)], wide_sems.at[n]
            )
            turns.append(((at + flip) % 2 == 0, row_copy, turn_copy))

    def each_turn(act):
        for is_first, row_copy, turn_copy in turns:
            pl.when(is_first)(functools.partial(act, row_copy))
            pl.when(jnp.logical_not(is_first))(functools.partial(act, turn_copy))

    each_turn(lambda copy: copy.start())
    if len(whole_outer_ref.shape) == 2:
        outer_copies = [pltpu.make_async_copy(whole_outer_ref, outer_ref, outer_sems.at[0])]
    else:
        devices, sides, block, lanes = whole_outer_ref.shape
        blocks_ref = outer_ref.reshape(sides, devices, block, lanes)
        outer_copies = [
            pltpu.make_async_copy(
                whole_outer_ref.at[:, slot],
                blocks_ref.at[where_ref[0] if slot == 0 else 1 - where_ref[0]],
                outer_sems.at[slot],
            )
            for slot in range(sides)
        ]
    for copy in outer_copies:
        copy.start()
    first_ref, second_ref = wide_ref.at[0], wide_ref.at[1]
    share = own_ref.shape[1]
    half = outer_ref.shape[0] // 2
    side = where_ref[0]
    mine = pl.ds(pl.multiple_of(side * share, 128), share)
    theirs = pl.ds(pl.multiple_of((1 - side) * share, 128), share)
    attended_ref[:, mine] = own_ref[...]
    attended_ref[:, theirs] = received_ref[...]
    attended = attended_ref[...]
    out_bias, attn_gain, attn_shift, outer_bias, ffn_gain, ffn_shift = (
        vector_ref[n : n + 1] for n in range(6)
    )
    for copy in wide_copies:
        copy.wait()
    each_turn(lambda copy: copy.wait())
    projected = jnp.concatenate(
        [matmul(attended, first_ref[:, half:]), matmul(attended, second_ref[:, half:])], axis=1
    )
    resid_one = token_ref[...].astype(F32) + projected + out_bias
    unit_one, inv_one = normed(resid_one)
    hidden = unit_one * attn_gain + attn_shift
    hidden_low = hidden.astype(BF16)
    hidden_ref[...] = hidden_low
    spans = [
        (ref, start, part * half + start)
        for part, ref in enumerate((first_ref, second_ref))
        for start in range(0, half, chunk)
    ]
    for copy in outer_copies:
        copy.wait()
    resid_two = hidden + outer_bias
    for ref, start, place in spans:
        lanes = slice(place, place + chunk)
        pre_act = matmul(hidden_low, ref[:, start : start + chunk]) + bias_ref[:, lanes]
        phi = 0.5 * (1.0 + lax.erf(pre_act * INV_SQRT_TWO))
        density = INV_SQRT_TWO_PI * jnp.exp(-0.5 * pre_act * pre_act)
        inner_low = (pre_act * phi).astype(BF16)
        inner_ref[:, lanes] = inner_low
        slope_ref[:, lanes] = (phi + pre_act * density).astype(BF16)
        resid_two += matmul(inner_low, outer_ref[lanes, :])
    unit_two, inv_two = normed(resid_two)
    result_ref[...] = (unit_two * ffn_gain + ffn_shift).astype(BF16)
    cotangent = grad_ref[...].astype(F32)
    d_resid_two = normed_back(cotangent * ffn_gain, unit_two, inv_two)
    d_branch = d_resid_two.astype(BF16)
    d_branch_ref[...] = d_branch
    d_hidden = d_resid_two
    inner_sums = []
    for ref, start, place in spans:
        lanes = slice(place, place + chunk)
        d_pre = matmul_nt(d_branch, outer_ref[lanes, :]) * slope_ref[:, lanes].astype(F32)
        inner_sums.append(row_sum(d_pre))
        d_pre_low = d_pre.astype(BF16)
        d_pre_ref[:, lanes] = d_pre_low
        d_hidden += matmul_nt(d_pre_low, ref[:, start : start + chunk])
    d_resid_one = normed_back(d_hidden * attn_gain, unit_one, inv_one)
    d_proj = d_resid_one.astype(BF16)
    d_proj_ref[...] = d_proj
    d_heads_ref[...] = (
        matmul_nt(d_proj[:, :share], first_ref[:, half:])
        + matmul_nt(d_proj[:, share:], second_ref[:, half:])
    ).astype(BF16)
    d_own_ref[...] = d_heads_ref[:, mine]
    d_theirs_ref[...] = d_heads_ref[:, theirs]
    sums_ref[...] = jnp.concatenate(
        [
            row_sum(d_resid_one),
            row_sum(d_hidden * unit_one),
            row_sum(d_hidden),
            row_sum(d_resid_two),
            row_sum(cotangent * unit_two),
            row_sum(cotangent),
            jnp.zeros((2, d_resid_one.shape[1]), F32),
        ],
        axis=0,
    )
    inner_sums_ref[...] = jnp.concatenate(inner_sums, axis=1)


def forward_back(
    where, own, received, tokens, grads, pieces, outer, vectors, bias, at, rows, earlier
):
    width = tokens.shape[1]
    share = own.shape[1]
    units = bias.shape[1]
    chunk = units // 6
    tops = [(2, width, units // 2 + share), (units, width)]
    outer_blocks = 1 if outer.ndim == 2 else outer.shape[1]

    def whole(array):
        return pl.BlockSpec(array.shape, lambda i, s: (0, 0), pipeline_mode=pl.Buffered(1))

    def local(lanes):
        return pl.BlockSpec((rows, lanes), lambda i, s: (0, 0), pipeline_mode=pl.Buffered(1))

    def placed(lanes):
        return pl.BlockSpec((rows, lanes), lambda i, s: (at, 0), pipeline_mode=pl.Buffered(1))

    lanes_out = [width, width, width, units, width, units, width, share, share]
    sources = [source for source, _, _ in pieces] + [outer]
    kept = len(lanes_out) - 1
    aliases = {}
    if earlier is not None:
        sources += list(earlier)
        aliases = {7 + len(sources) - kept + n: n for n in range(kept)}
    return pl.pallas_call(
        functools.partial(forward_back_body, chunk=chunk, places=places_of(pieces)),
        grid_spec=pltpu.PrefetchScalarGridSpec(
            num_scalar_prefetch=1,
            grid=(1,),
            in_specs=[
                placed(share),
                local(share),
                placed(width),
                placed(width),
                whole(vectors),
                whole(bias),
            ]
            + [pl.BlockSpec(memory_space=pl.ANY)] * len(sources),
            out_specs=[placed(lanes) for lanes in lanes_out[:kept]]
            + [local(lanes) for lanes in lanes_out[kept:]]
            + [
                pl.BlockSpec((8, width), lambda i, s: (0, 0)),
                pl.BlockSpec((1, units), lambda i, s: (0, 0)),
            ],
            scratch_shapes=[pltpu.VMEM((rows, units), BF16), pltpu.VMEM((rows, width), BF16)]
            + [pltpu.VMEM(shape, BF16) for shape in tops]
            + [pltpu.SemaphoreType.DMA((copy_count(pieces),)), pltpu.SemaphoreType.DMA((outer_blocks,))],
        ),
        out_shape=[
            jax.ShapeDtypeStruct((tokens.shape[0] if n < kept else rows, lanes), BF16)
            for n, lanes in enumerate(lanes_out)
        ]
        + [
            jax.ShapeDtypeStruct((8, width), F32),
            jax.ShapeDtypeStruct((1, units), F32),
        ],
        input_output_aliases=aliases,
        compiler_params=pltpu.CompilerParams(vmem_limit_bytes=VMEM_LIMIT),
        cost_estimate=SMALL_COST,
        name="forward_back",
    )(where, own, received, tokens, grads, vectors, bias, *sources)


def shards(
    hidden_in,
    prev_logits,
    segment,
    w_query,
    b_query,
    w_key,
    w_value,
    b_value,
    w_out,
    b_out,
    gain_attn,
    shift_attn,
    w_inner,
    b_inner,
    w_outer,
    b_outer,
    gain_ffn,
    shift_ffn,
    out_grad,
):
    seq = lax.axis_index("seq").astype(jnp.int32)
    fsdp_count = lax.axis_size("fsdp")
    count = fsdp_count.bit_length() - 1
    devices = 2 * fsdp_count
    heads, group, window = prev_logits.shape
    rows, width = w_query.shape
    inner_rows = b_inner.shape[0]
    hidden_units = inner_rows * devices
    share = width // 2
    half = hidden_units // 2
    tokens = hidden_in.shape[0]
    own_windows = tokens // window
    seq_hop = ("seq", 1)
    far, near, core = plan_hops(count)
    done = len(far)

    vectors = (b_query, b_value, b_out, gain_attn, shift_attn, b_outer, gain_ffn, shift_ffn, b_inner)
    where = jnp.stack([seq, lax.axis_index("fsdp").astype(jnp.int32)])
    other_inner, other_out = swap(w_inner, far[0]), swap(w_out, far[0])
    unit, unit_core, unit_seq, unit_both = pack(where, w_query, w_key, w_value, vectors)
    parts = 4
    part_rows = tokens // parts
    others = []

    def next_part(*earlier):
        part = hidden_in[len(others) * part_rows : (len(others) + 1) * part_rows]
        others.append(swap(after(part, *earlier), seq_hop))

    def quad(flip_seq, flip_core):
        def place(n, at_seq, at):
            one, two = bit_of(seq_hop, at_seq, at), bit_of(core, at_seq, at)
            return 2 * (1 - one if flip_seq else one) + (1 - two if flip_core else two)

        return place

    def both_flipped(at_seq, at):
        return at_seq ^ 1, at ^ 1

    def pairs_of(blocks):
        return blocks.reshape(-1, 2 * blocks.shape[1], blocks.shape[2])

    def hopped(blocks, hop, inner):
        return joined(blocks, swap(blocks, hop), hop, inner)

    (unit,) = merge(
        where,
        [
            (after(unit, other_inner, other_out)[None], quad(False, False)),
            (swap(unit_seq, seq_hop)[None], quad(True, False)),
            (swap(unit_core, core)[None], quad(False, True)),
            (trade(unit_both, both_flipped)[None], quad(True, True)),
        ],
    )
    unit = pairs_of(unit)
    wide, wide_core = cut(where, after(w_inner, unit), w_out, other_inner, other_out, far[0])
    outer_other = swap(after(w_outer, unit), seq_hop)
    next_part(unit)
    wide_item = joined(after(wide, others[0]), swap(wide_core, core), core, 1)
    if done == 2:
        def flipped(one, two):
            def place(n, at_seq, at):
                bits = bit_of(far[0], at_seq, at), bit_of(far[1], at_seq, at)
                return 4 * n + 2 * (1 - bits[0] if one else bits[0]) + (1 - bits[1] if two else bits[1])

            return place

        unit_item = [(unit, flipped(False, False))]
        for one, two in ((True, False), (False, True), (True, True)):
            mask = one * far[0][1] + two * far[1][1]
            unit_item.append((swap(unit, ("fsdp", mask)), flipped(one, two)))
        unit, wide = merge(where, unit_item, wide_item)
    else:
        unit, wide = merge(where, hopped(unit, far[0], 1), wide_item)
        for hop in far[1:]:
            (unit,) = merge(where, hopped(unit, hop, 1))
    outer = jnp.stack([after(w_outer, unit), outer_other])
    outer = lax.all_gather(outer, "fsdp", axis=0, tiled=False)
    if inner_rows % 16 != 0:
        outer = jnp.where(seq == 0, outer, outer[:, ::-1])
        outer = outer.transpose(1, 0, 2, 3).reshape(hidden_units, width)
    wide = pairs_of(wide)
    for hop in far[1:-1]:
        (wide,) = merge(where, hopped(wide, hop, 1))
    next_part(unit)
    wide_item = hopped(after(wide, unit), far[-1], 1)
    in_blocks = 2 * rows % 16 == 0
    unit_other = swap(unit, near)
    if in_blocks:
        near_places = spread(near, 1)
        unit_core, unit_other_core = swap(unit, core), swap(unit_other, core)
        unit_pieces = [
            (unit, near_places[0], 0),
            (unit_other, near_places[1], 0),
            (unit_core, near_places[0], 1),
            (unit_other_core, near_places[1], 1),
        ]
        wide_item[0] = (after(wide, others[1], unit_other), wide_item[0][1])
        (wide,) = merge(where, wide_item)
    else:
        wide_item[0] = (after(wide, others[1]), wide_item[0][1])
        unit, wide = merge(where, joined(unit, unit_other, near, 1), wide_item)
        unit = unit.reshape(width, unit.shape[-1])
        unit_pieces = [(unit, None, 0), (swap(unit, core), None, 1)]
    next_part(unit_pieces[1][0])
    next_part(unit_pieces[1][0])

    def near_or_seq(at_seq, at):
        return across(near if at % 2 == 0 else seq_hop)(at_seq, at)

    def seq_or_near(at_seq, at):
        return across(seq_hop if at % 2 == 0 else near)(at_seq, at)

    wide_other = trade(wide, near_or_seq)
    own_qkv, qkv_weight, small, qkv_bias = project_first(where, hidden_in, unit_pieces)

    seg_rows = segment[:, None]
    seg_cols = segment.reshape(group // window, 1, window)
    own_start = (seq * own_windows).reshape(1)
    other_start = ((1 - seq) * own_windows).reshape(1)

    logits, probs, own_out = attend(
        own_qkv, prev_logits, seg_rows, seg_cols, own_start, 0, own_windows, None
    )
    blocks = wide.shape[0]
    (wide,) = merge(
        where,
        joined_by_core(
            after(wide, own_out, others[-2], others[-1]), wide_other, core, (near, 1), (seq_hop, blocks)
        ),
    )
    wide_other = trade(wide, seq_or_near)
    blocks = wide.shape[0]
    zero_places, one_places = spread(seq_hop, blocks), spread(near, 1)
    wide_places = [by_core(core, zero_places[n], one_places[n]) for n in range(2)]
    other_qkv, other_rows = project_rest(after(tuple(others), wide), qkv_weight, qkv_bias)
    other_out = []
    received = []
    for w in range(own_windows):
        logits, probs, out = attend(
            other_qkv, prev_logits, seg_rows, seg_cols, other_start + w, w, 1, (logits, probs)
        )
        other_out.append(out)
        if w == 0:
            wide_other = after(wide_other, out)
            if in_blocks:
                wide_core, wide_other_core = swap(wide, core), swap(wide_other, core)
                wide_pieces = [
                    (wide, wide_places[0], 0),
                    (wide_other, wide_places[1], 0),
                    (wide_core, wide_places[0], 1),
                    (wide_other_core, wide_places[1], 1),
                ]
            else:
                (wide,) = merge(where, [(wide, wide_places[0]), (wide_other, wide_places[1])])
                wide = wide.reshape(width, wide.shape[-1])
                wide_pieces = [(wide, None, 0), (swap(wide, core), None, 1)]
            other_qkv = after(other_qkv, wide_other)
        received.append(swap(out, seq_hop))
    small = small.astype(F32)
    layer_vectors = jnp.concatenate([small[:, 2:8].T, jnp.zeros((2, width), F32)], axis=0)
    inner_bias = small[:, 8 : 8 + hidden_units // width].reshape(1, hidden_units)

    full = None
    d_others = []
    sums, inner_sums = 0.0, 0.0
    for w in range(own_windows):
        outs = forward_back(
            where,
            own_out,
            received[w],
            hidden_in,
            out_grad,
            wide_pieces,
            outer,
            layer_vectors,
            inner_bias,
            w,
            window,
            full,
        )
        full = outs[:8]
        d_others.append(swap(outs[8], seq_hop))
        sums += outs[9]
        inner_sums += outs[10]
    hidden_out, attended, hidden, inner, d_branch, d_pre, d_proj, d_own = full

    class Reduction:
        def __init__(self, value, hops):
            self.value, self.hops = value, list(hops)
            self.send()

        def send(self):
            if self.hops:
                hop, place = self.hops.pop(0)
                away, self.keep = split(self.value, hop, place)
                self.other = swap(away, hop)

        def add(self, latest):
            self.value = total(after(self.keep, latest), self.other)
            self.send()
            return self.value

    grid = (2,) * (count + 1)
    outer_hops = [(core, done + 2), (near, done + 1)]
    outer_hops += [(far[n], n + 1) for n in reversed(range(done))] + [(seq_hop, 0)]
    inner_hops = [(core, done + 2), (seq_hop, 0), (near, done)]
    inner_hops += [(far[n], n) for n in reversed(range(done))]
    tail_hops = [(core, done + 2), (near, done + 1)]
    tail_hops += [(far[n], n + 1) for n in reversed(range(done))]

    inner, attended = after((inner, attended), d_others[0])
    g_outer = matmul_tn(inner, d_branch).astype(BF16)
    g_out = matmul_tn(attended, d_proj).astype(BF16)
    outer_grad = jnp.concatenate(
        [
            g_outer.reshape(grid + (inner_rows, width)),
            g_out.reshape(grid + (rows, width)),
        ],
        axis=-2,
    )
    outer_sum = Reduction(outer_grad, outer_hops)
    g_inner = matmul_tn(after(hidden, outer_grad), d_pre).astype(BF16)
    inner_sum = Reduction(g_inner.reshape(grid + (rows, hidden_units)), inner_hops)
    latest = outer_sum.add(g_inner)
    latest = inner_sum.add(latest)

    d_scores = None
    input_received = []
    other_qkv = after(other_qkv, latest)
    g_qkv, qkv_sum = 0.0, 0.0
    for w in range(own_windows):
        d_scores, d_qkv, column_sums = attend_back(
            other_qkv, probs, d_others[w], other_out[w], other_start + w, w, 1, d_scores
        )
        input_received.append(swap(matmul_nt(d_qkv, qkv_weight).astype(BF16), seq_hop))
        g_qkv += matmul_tn(other_rows[w * window : (w + 1) * window], d_qkv)
        qkv_sum += column_sums[0]
    latest = outer_sum.add(d_qkv)
    latest = inner_sum.add(latest)
    own_qkv = after(own_qkv, latest)
    d_scores, own_d_qkv, column_sums = attend_back(
        own_qkv, probs, d_own, own_out, own_start, 0, own_windows, d_scores
    )
    own_d_qkv = after(own_d_qkv, outer_sum.other, inner_sum.other)
    g_qkv += matmul_tn(hidden_in, own_d_qkv)
    qkv_sum = (qkv_sum + jnp.sum(column_sums, axis=0)).reshape(-1)

    def both_sides(part):
        blank = jnp.zeros_like(part)
        return jnp.where(
            seq == 0, jnp.concatenate([part, blank]), jnp.concatenate([blank, part])
        )

    small_grads = jnp.concatenate(
        [
            both_sides(qkv_sum[:share])[:, None],
            both_sides(qkv_sum[2 * share :])[:, None],
            sums[:6].T,
            inner_sums.reshape(width, hidden_units // width),
        ],
        axis=1,
    )
    lanes = small_grads.shape[1]
    tail = jnp.concatenate(
        [g_qkv.astype(BF16), jnp.pad(small_grads, ((0, 0), (0, 128 - lanes))).astype(BF16)], axis=1
    ).reshape(grid + (rows, 3 * share + 128))
    direct = done == 2
    tail_sum = Reduction(tail, tail_hops[:2] if direct else tail_hops)
    latest = outer_sum.add(tail)
    latest = tail_sum.add(latest)
    latest = inner_sum.add(latest)
    latest = outer_sum.add(latest)
    latest = tail_sum.add(latest)
    if direct:
        bits = my_bit(far[0]), my_bit(far[1])

        def block(one, two):
            at = (1 - bits[0] if one else bits[0], 1 - bits[1] if two else bits[1])
            blocks = tail_sum.value.reshape((2, 4) + tail_sum.value.shape[-2:])
            return lax.dynamic_index_in_dim(blocks, 2 * at[0] + at[1], 1, keepdims=False)

        arrivals = [
            swap(block(one, two), ("fsdp", one * far[0][1] + two * far[1][1]))
            for one, two in ((True, False), (False, True), (True, True))
        ]
        keep = block(False, False)
    latest = inner_sum.add(latest)
    latest = outer_sum.add(latest)
    if direct:
        terms = [after(keep, latest)] + arrivals
        tail = functools.reduce(jnp.add, [term.astype(F32) for term in terms]).astype(BF16)
        latest = tail
    while not direct and len(tail_sum.value.shape) > 3:
        latest = tail_sum.add(latest)
        tail = latest
    while len(outer_sum.value.shape) > 2:
        latest = outer_sum.add(latest)
    while len(inner_sum.value.shape) > 2:
        latest = inner_sum.add(latest)
    outer_grad, inner_grad = outer_sum.value, inner_sum.value
    send, own_tail = split(tail, seq_hop, 0)
    other_tail = swap(send, seq_hop)
    grads = unpack(own_tail[:, 3 * share :], other_tail[:, 3 * share :], inner_rows)

    def weight_part(slot):
        at = slice(slot * share, (slot + 1) * share)
        return jnp.where(
            seq == 0,
            jnp.concatenate([own_tail[:, at], other_tail[:, at]], axis=1),
            jnp.concatenate([other_tail[:, at], own_tail[:, at]], axis=1),
        ).astype(F32)

    input_grad = (
        d_proj.astype(F32)
        + matmul_nt(own_d_qkv, qkv_weight)
        + jnp.concatenate(input_received, axis=0).astype(F32)
    ).astype(BF16)
    return (
        hidden_out,
        logits,
        input_grad,
        d_scores,
        weight_part(0),
        grads[0],
        weight_part(1),
        weight_part(2),
        grads[1],
        outer_grad[inner_rows:].astype(F32),
        grads[2],
        grads[3],
        grads[4],
        inner_grad.astype(F32),
        grads[8],
        outer_grad[:inner_rows].astype(F32),
        grads[5],
        grads[6],
        grads[7],
    )


def solution(mesh):
    in_specs = (
        P(("fsdp", "seq"), None),
        P("seq", "fsdp", None),
        P("fsdp"),
        P(("seq", "fsdp"), None),
        P(("seq", "fsdp")),
        P(("seq", "fsdp"), None),
        P(("seq", "fsdp"), None),
        P(("seq", "fsdp")),
        P(("seq", "fsdp"), None),
        P(("seq", "fsdp")),
        P(("seq", "fsdp")),
        P(("seq", "fsdp")),
        P(("seq", "fsdp"), None),
        P(("seq", "fsdp")),
        P(("seq", "fsdp"), None),
        P(("seq", "fsdp")),
        P(("seq", "fsdp")),
        P(("seq", "fsdp")),
        P(("fsdp", "seq"), None),
    )
    out_specs = (
        P(("fsdp", "seq"), None),
        P("seq", "fsdp", None),
        P(("fsdp", "seq"), None),
        P("seq", "fsdp", None),
        P(("seq", "fsdp"), None),
        P(("seq", "fsdp")),
        P(("seq", "fsdp"), None),
        P(("seq", "fsdp"), None),
        P(("seq", "fsdp")),
        P(("seq", "fsdp"), None),
        P(("seq", "fsdp")),
        P(("seq", "fsdp")),
        P(("seq", "fsdp")),
        P(("seq", "fsdp"), None),
        P(("seq", "fsdp")),
        P(("seq", "fsdp"), None),
        P(("seq", "fsdp")),
        P(("seq", "fsdp")),
        P(("seq", "fsdp")),
    )
    return jax.shard_map(shards, mesh=mesh, in_specs=in_specs, out_specs=out_specs, check_vma=False)
```
